32 devices in a mesh: req: 16 (over z, y, x), tp: 2 (over core).
Axes of the slice: x: 2, y: 2, z: 4, core: 2. Of those that a mesh axis runs over, the one named last changes fastest.
Arguments:
- tokens: bfloat16 [8192, 3072], P('req', 'tp'), may hold values from -6 to 6
- norm_gain: bfloat16 [3072], P('tp'), may hold values from 0.099609375 to 1.8984375
- qkv_weight: bfloat16 [3, 3072, 3072], P(None, 'req', 'tp'), may hold values from -0.109375 to 0.109375
- out_weight: bfloat16 [3072, 3072], P('tp', 'req'), may hold values from -1.75 to 1.75
- cache: bfloat16 [16, 2, 2048, 3072], P('req', None, None, 'tp'), may hold values from -720 to 720
- cache_lens: int32 [16], P('req'), may hold values from 0 to 2048, as said below
- valid_tokens: int32 [16], P('req'), may hold values from 128 to 512, as said below
Outputs:
- mixed: bfloat16 [8192, 3072], P('req', 'tp')
- new_entries: bfloat16 [16, 2, 512, 3072], P('req', None, None, 'tp')
The draws below stay inside these ranges and needn't reach their ends.
Inputs may be any that keep to these rules, and one draw needn't show every extreme that they name: `cache_lens`: in every draw some request's cache holds all 2048 entries and some request's cache is empty. `valid_tokens`: in every draw some request brings 512 live new tokens.
All inputs are finite; a program needn't handle non-finite values.
Results may differ from the reference program's by a relative error of at most 0.0095.
The reference program's roundings to bfloat16 on the way count: a program that leaves them out, or rounds other values in their place, can miss the bound.
Values may be sent and summed in bfloat16 or wider, within the bound.
A program may use at most 192 MiB of HBM per device.

```python
import math
import jax
import jax.numpy as jnp
from jax import lax

D = 3072
HEADS = 32
HD = 96
SPAN = 512
CACHE = 2048
REQS = 16
TOKENS = 8192
N_TP = 2


def draw_cache_lens(key, part):
    key_one, key_two, key_three, key_four = jax.random.split(jax.random.fold_in(key, 11), 4)
    factor_one = jax.random.randint(key_one, (REQS,), 0, CACHE + 1)
    factor_two = jax.random.randint(key_two, (REQS,), 0, CACHE + 1)
    lengths = factor_one * factor_two // CACHE
    longest = jax.random.randint(key_three, (), 0, REQS)
    offset = jax.random.randint(key_four, (), 1, REQS)
    emptied = (longest + offset) % REQS
    request_ids = jnp.arange(REQS)
    lengths = jnp.where(request_ids == longest, CACHE, lengths)
    lengths = jnp.where(request_ids == emptied, 0, lengths)
    return lengths.astype(jnp.int32)


def draw_valid_tokens(key, part):
    key_one, key_two = jax.random.split(jax.random.fold_in(key, 23), 2)
    counts = jax.random.randint(key_one, (REQS,), SPAN // 4, SPAN + 1)
    fullest = jax.random.randint(key_two, (), 0, REQS)
    counts = jnp.where(jnp.arange(REQS) == fullest, SPAN, counts)
    return counts.astype(jnp.int32)


def draw_cache(key, part):
    key_one = jax.random.fold_in(jax.random.fold_in(key, 37), 0)
    entries = jnp.clip(jax.random.normal(key_one, (REQS, 2, CACHE, HEADS * HD), jnp.float32), -6.0, 6.0)
    return entries.astype(jnp.bfloat16)


def spiked(values, key, source, target, shards_of, factor):
    def block_of(axis_at):
        return (jnp.arange(values.shape[axis_at]) // (values.shape[axis_at] // shards_of)).reshape((-1,) + (1,) * (values.ndim - 1 - axis_at))

    one_side = jax.random.permutation(key, shards_of)[block_of(target)]
    second = (block_of(target) + shards_of // 2) % shards_of
    return jnp.where((block_of(source) == one_side) | (block_of(source) == second), factor * values, values)


def block_scale(stream_key, extent, pieces, smallest, high):
    gain = 1.0
    for dim, blocks in pieces:
        heights = jax.random.uniform(jax.random.fold_in(jax.random.fold_in(stream_key, 6), dim), (blocks,), jnp.float32, smallest / len(pieces), high / len(pieces))
        gain = gain * jnp.repeat(jnp.exp(heights), extent[dim] // blocks).reshape((-1,) + (1,) * (len(extent) - 1 - dim))
    return gain


def gaussian(rng, shape, width, bound, cuts=(), held_as=jnp.bfloat16):
    factor_of = block_scale(rng, shape, cuts, -0.22, 0.18) if cuts else 1.0
    array = jax.random.normal(rng, shape, jnp.float32) * width * factor_of
    return jnp.minimum(jnp.maximum(array, -bound), bound).astype(held_as)


def noise_with(stream_key, extent, deviation, most, pieces, heavy, kind=jnp.bfloat16):
    values = deviation * jax.random.normal(stream_key, extent, jnp.float32)
    if pieces:
        values = values * block_scale(stream_key, extent, pieces, -0.22, 0.18)
    return jnp.clip(spiked(values, jax.random.fold_in(stream_key, 3), *heavy), -most, most).astype(kind)


def setup_inputs(seed: int = 0) -> dict:
    seeds = jax.random.split(jax.random.key(seed), 8)
    return {
        "tokens": gaussian(seeds[0], (TOKENS, D), 1.0, 6.0, ((0, 16), (1, 2))),
        "norm_gain": jnp.clip(1.0 + 0.18 * jax.random.normal(seeds[1], (D,), jnp.float32), 0.099609375, 1.8984375).astype(jnp.bfloat16),
        "qkv_weight": gaussian(seeds[2], (3, D, HEADS * HD), D ** -0.5, 0.109375, ((1, 16), (2, 2))),
        "out_weight": noise_with(seeds[3], (HEADS * HD, D), (HD // 4) ** -0.5, 1.75, ((0, 2), (1, 16)), (0, 1, 16, 2.0)),
        "cache": draw_cache(jax.random.fold_in(seeds[7], 71), 0),
        "cache_lens": draw_cache_lens(jax.random.fold_in(seeds[7], 71), 0),
        "valid_tokens": draw_valid_tokens(jax.random.fold_in(seeds[7], 71), 0),
    }


epsilon = 1e-05
masked_value = -1e+30
theta_base = 10000.0

def rotate(projected, positions):
    tokens_here, columns = projected.shape
    per_head = projected.reshape(tokens_here, columns // HD, HD)
    frequencies = jnp.power(theta_base, -jnp.arange(0, HD, 2, dtype=jnp.float32) / HD)
    angles = positions.astype(jnp.float32)[:, None] * frequencies[None, :]
    cosine = jnp.cos(angles)[:, None, :]
    sine_table = jnp.sin(angles)[:, None, :]
    first_half = per_head[..., :HD // 2]
    second_half = per_head[..., HD // 2:]
    turned = jnp.concatenate([first_half * cosine - second_half * sine_table, second_half * cosine + first_half * sine_table], axis=-1)
    return turned.reshape(tokens_here, columns)

def reference(tokens, norm_gain, qkv_weight, out_weight, cache, cache_lens, valid_tokens):
    head_cols = HEADS * HD
    group_cols = head_cols // N_TP
    score_scale = 1.0 / math.sqrt(HD)
    rows_all = tokens.reshape(REQS, SPAN, D)

    def per_request(inputs_all):
        rows_in, cache_here, length, valid_count = inputs_all
        inputs = rows_in.astype(jnp.float32)
        spread = lax.optimization_barrier(jnp.mean(inputs * inputs, axis=-1, keepdims=True))
        normed = (inputs * lax.rsqrt(spread + epsilon) * norm_gain.astype(jnp.float32)).astype(jnp.bfloat16)
        projected = [jnp.dot(normed, qkv_weight[j], preferred_element_type=jnp.float32) for j in range(3)]
        token_ids = jnp.arange(SPAN, dtype=jnp.int32)
        positions = length + token_ids
        queries = rotate(projected[0], positions).astype(jnp.bfloat16)
        keys_new = rotate(projected[1], positions).astype(jnp.bfloat16)
        values_new = projected[2].astype(jnp.bfloat16)
        kept = (token_ids < valid_count)[:, None]
        entries = jnp.stack([jnp.where(kept, keys_new, jnp.zeros_like(keys_new)), jnp.where(kept, values_new, jnp.zeros_like(values_new))])
        key_rows = jnp.concatenate([cache_here[0], keys_new], axis=0)
        value_rows = jnp.concatenate([cache_here[1], values_new], axis=0)
        cache_ids = jnp.arange(CACHE, dtype=jnp.int32)
        cache_mask = jnp.broadcast_to((cache_ids < length)[None, :], (SPAN, CACHE))
        new_mask = (token_ids[None, :] <= token_ids[:, None]) & (token_ids[None, :] < valid_count)
        live_mask = jnp.concatenate([cache_mask, new_mask], axis=1)
        scores = jnp.einsum('thd,shd->hts', queries.reshape(SPAN, HEADS, HD).astype(jnp.float32), key_rows.reshape(CACHE + SPAN, HEADS, HD).astype(jnp.float32)) * score_scale
        scores = jnp.where(live_mask[None], scores, masked_value)
        maximum = lax.optimization_barrier(jnp.max(scores, axis=-1, keepdims=True))
        expo = jnp.exp(scores - maximum)
        weights = (expo / lax.optimization_barrier(jnp.sum(expo, axis=-1, keepdims=True))).astype(jnp.bfloat16)
        attended = jnp.einsum('hts,shd->thd', weights.astype(jnp.float32), value_rows.reshape(CACHE + SPAN, HEADS, HD).astype(jnp.float32))
        attended = attended.astype(jnp.bfloat16).reshape(SPAN, head_cols)
        partial_value = jnp.einsum('tgc,gcd->gtd', attended.reshape(SPAN, N_TP, group_cols).astype(jnp.float32), out_weight.reshape(N_TP, group_cols, D).astype(jnp.float32))
        partial_value = partial_value.astype(jnp.bfloat16).astype(jnp.float32)
        summed = lax.optimization_barrier(jnp.sum(partial_value, axis=0))
        mixed_rows = jnp.where(kept, summed, jnp.zeros_like(summed)).astype(jnp.bfloat16)
        return (mixed_rows, entries)
    mixed_all, entries_all = lax.map(per_request, (rows_all, cache, cache_lens, valid_tokens))
    return (mixed_all.reshape(TOKENS, D), entries_all)
```

```python
import functools
import math

import jax
import jax.numpy as jnp
import numpy as np
from jax import lax
from jax.experimental import pallas as pl
from jax.experimental.pallas import tpu as pltpu
from jax.sharding import PartitionSpec as P

HD = 96
GROUP = 4 * HD

epsilon = 1e-05
masked_value = -1e30
theta_base = 10000.0


def base_tables(span):
    frequencies = np.power(theta_base, -np.arange(0, HD, 2, dtype=np.float64) / HD)
    row = np.tile(frequencies.astype(np.float32), 2 * GROUP // HD)
    angles = np.arange(span, dtype=np.float64)[:, None] * row[None, :].astype(np.float64)
    sign = np.tile(np.where(np.arange(HD) < HD // 2, -1.0, 1.0), GROUP // HD).astype(np.float32)
    return (
        np.cos(angles).astype(np.float32),
        np.sin(angles).astype(np.float32),
        row,
        sign,
    )


def project_kernel(
    units,
    tok,
    gain,
    shard,
    base_cos,
    base_sin,
    turn,
    out,
    normed,
    weights,
    staged,
    turns,
    squares,
    z_send,
    w_recv,
    own_sem,
    s_send,
    n_send,
    n_recv,
    t_send,
    t_recv,
    q_send,
    q_recv,
    r_send,
    r_recv,
    keep_sem,
):
    me = lax.axis_index("req")
    core = lax.axis_index("tp")
    z, y, x = lax.div(me, 4), lax.rem(lax.div(me, 2), 2), lax.rem(me, 2)
    p = lax.rem(me, 4)
    base = me - p
    px, py, pd = p + 1 - 2 * x, p + 2 - 4 * y, 3 - p
    span, width = tok.shape
    features = 2 * width
    half = span // 2
    mate = (me, 1 - core)

    barrier = pltpu.get_barrier_semaphore()

    def greet(target):
        pl.semaphore_signal(
            barrier, inc=1, device_id=target, device_id_type=pl.DeviceIdType.MESH
        )

    for peer in (px, py, pd):
        greet((base + peer, core))
    greet(mate)

    @pl.when(z < 3)
    def _():
        greet((me + 4, core))

    @pl.when(z > 0)
    def _():
        greet((me - 4, core))

    inner = jnp.where(z > 0, 1, 0) + jnp.where(z < 3, 1, 0)
    pl.semaphore_wait(barrier, 4 + inner)

    def remote(source, target_ref, sent, received, target):
        return pltpu.make_async_remote_copy(
            src_ref=source,
            dst_ref=target_ref,
            send_sem=sent,
            recv_sem=received,
            device_id=target,
            device_id_type=pl.DeviceIdType.MESH,
        )

    def columns(unit, peer):
        part, low, count = units[unit]
        return shard.at[part, :, pl.ds(pl.multiple_of(peer * GROUP + low, 128), count)]

    def block(unit, plane, source):
        part, low, count = units[unit]
        return weights.at[part, plane, source, :, low : low + count]

    def along(unit, plane, source, up, own):
        there = block(unit, plane, source)
        return remote(
            columns(unit, p) if own else there,
            there,
            z_send.at[unit, plane, source, 0 if up else 1],
            w_recv.at[unit, plane, source],
            (me + 4 if up else me - 4, core),
        )

    def scatter(unit, lane, peer):
        return remote(
            columns(unit, peer),
            block(unit, z, p),
            s_send.at[unit, lane],
            w_recv.at[unit, z, p],
            (base + peer, core),
        )

    def keep(unit):
        return pltpu.make_async_copy(columns(unit, p), block(unit, z, p), own_sem.at[unit])

    def own_along(unit, act):
        @pl.when(z < 3)
        def _():
            act(along(unit, z, p, True, True))

        @pl.when(z > 0)
        def _():
            act(along(unit, z, p, False, True))

    def scatters(unit, act):
        for lane, peer in enumerate((pd, px, py)):
            act(scatter(unit, lane, peer))

    def onward(unit, plane, source, up, down, act):
        if up:

            @pl.when(z < 3)
            def _():
                act(along(unit, plane, source, True, False))

        if down:

            @pl.when(z > 0)
            def _():
                act(along(unit, plane, source, False, False))

    def arrivals(unit, steps, act, arrived):
        for step in steps:
            if step == 0:
                for source in (px, py, pd):
                    if arrived:
                        along(unit, z, source, True, False).wait_recv()
                    onward(unit, z, source, True, True, act)
                continue
            for delta in (-step, step):

                def body(plane=z + delta, delta=delta):
                    for source in (p, px, py, pd):
                        if arrived:
                            along(unit, plane, source, True, False).wait_recv()
                        onward(unit, plane, source, delta < 0, delta > 0, act)

                pl.when(z + delta >= 0 if delta < 0 else z + delta <= 3)(body)

    def token(source, side, part, lane, target):
        ref = normed.at[source, pl.ds(2 * side, 2), part * half : (part + 1) * half, :]
        return remote(
            ref,
            ref,
            n_send.at[source, part, lane],
            n_recv.at[source, side, part],
            target,
        )

    to_x, to_y = (base + px, core), (base + py, core)

    def token_moves(source, part, via):
        moves = [(2, mate)]
        if via == "own" or (via == "y" and part == 1):
            moves.insert(0, (0, to_x))
        if via == "own" or (via == "x" and part == 0):
            moves.insert(0, (1, to_y))
        return [token(source, core, part, lane, target) for lane, target in moves]

    def tokens(source, part, via, act, arrived):
        if arrived:
            token(source, core, part, 2, mate).wait_recv()
        for copy in token_moves(source, part, via):
            act(copy)

    def turning(lane, peer):
        return remote(
            turns.at[p], turns.at[p], t_send.at[lane], t_recv.at[p], (base + peer, core)
        )

    def home(unit, peer):
        part, low, count = units[unit]
        return remote(
            staged.at[part, peer, :, low : low + count],
            out.at[part, p, :, low : low + count],
            r_send.at[unit, peer],
            r_recv.at[unit, p],
            (base + peer, core),
        )

    def landed(unit, source):
        part, low, count = units[unit]
        return remote(
            staged.at[part, source, :, low : low + count],
            out.at[part, source, :, low : low + count],
            r_send.at[unit, source],
            r_recv.at[unit, source],
            (base + source, core),
        )

    def stay(unit):
        part, low, count = units[unit]
        return pltpu.make_async_copy(
            staged.at[part, p, :, low : low + count],
            out.at[part, p, :, low : low + count],
            keep_sem.at[unit],
        )

    start = lambda c: c.start()
    sent = lambda c: c.wait_send()

    own_along(0, start)
    scatters(0, start)
    for unit in range(len(units)):
        keep(unit).start()
    turns[p] = turn[...]
    for lane, peer in enumerate((px, py, pd)):
        turning(lane, peer).start()

    rows = 64

    def measure(i, carry):
        at = pl.ds(i * rows, rows)
        v = tok[at, :].astype(jnp.float32)
        total = jnp.sum(v * v, axis=1, keepdims=True)
        squares[core, at, :] = jnp.broadcast_to(total, (rows, 128))
        return carry

    lax.fori_loop(0, span // rows, measure, 0)
    share = remote(squares.at[core], squares.at[core], q_send, q_recv.at[core], mate)
    share.start()
    remote(squares.at[1 - core], squares.at[1 - core], q_send, q_recv.at[1 - core], mate).wait_recv()
    gains = gain[...].astype(jnp.float32)

    def normalize(i, carry):
        at = pl.ds(i * rows, rows)
        spread = (squares[0, at, :] + squares[1, at, :])[:, :1] * (1.0 / features)
        v = tok[at, :].astype(jnp.float32) * lax.rsqrt(spread + epsilon) * gains
        v = v.astype(jnp.bfloat16)
        normed[p, 2 * core, at, :] = v[:, : width // 2]
        normed[p, 2 * core + 1, at, :] = v[:, width // 2 :]
        return carry

    for part in range(2):
        first = part * half // rows
        lax.fori_loop(first, first + half // rows, normalize, 0)
        tokens(p, part, "own", start, False)

    def compute(unit):
        part, low, count = units[unit]
        lane_in_head = lax.broadcasted_iota(jnp.int32, (span, GROUP), 1) % HD

        def body(i, carry):
            peer = jnp.where(i == 0, pd, jnp.where(i == 1, px, jnp.where(i == 2, py, p)))
            value = None
            for plane in range(4):
                chunk = weights[part, plane, :, :, low : low + count]
                term = jnp.dot(
                    normed[peer, plane],
                    chunk.reshape(chunk.shape[0] * chunk.shape[1], count),
                    preferred_element_type=jnp.float32,
                )
                value = term if value is None else value + term
            if part < 2:
                r = turns[peer]
                cosine = r[0:1] * base_cos[...] + r[1:2] * base_sin[...]
                sine = r[2:3] * base_cos[...] + r[3:4] * base_sin[...]
                ahead = pltpu.roll(value, GROUP - HD // 2, 1)
                behind = pltpu.roll(value, HD // 2, 1)
                value = value * cosine + jnp.where(lane_in_head < HD // 2, ahead, behind) * sine
            staged[part, peer, :, low : low + count] = value.astype(jnp.bfloat16)

            @pl.when(i < 3)
            def _():
                home(unit, peer).start()

            return carry

        lax.fori_loop(0, 4, body, 0)
        stay(unit).start()

    arrivals(0, (0, 1), start, True)
    scatters(1, start)
    tokens(px, 0, "x", start, True)
    tokens(py, 0, "y", start, True)
    arrivals(0, (2,), start, True)
    own_along(1, start)
    tokens(px, 1, "x", start, True)
    tokens(py, 1, "y", start, True)
    arrivals(0, (3,), start, True)
    arrivals(1, (0, 1), start, True)
    scatters(2, start)
    tokens(pd, 0, "d", start, True)
    tokens(pd, 1, "d", start, True)
    arrivals(1, (2,), start, True)
    own_along(2, start)
    for source in (p, px, py, pd):
        for part in range(2):
            token(source, 1 - core, part, 2, mate).wait_recv()
    for peer in (px, py, pd):
        remote(turns.at[peer], turns.at[peer], t_send.at[0], t_recv.at[peer], to_x).wait_recv()
    keep(0).wait()
    compute(0)
    arrivals(1, (3,), start, True)
    keep(1).wait()
    compute(1)
    for unit in range(2, len(units)):
        if unit > 2:
            pass
        if unit + 1 < len(units):
            scatters(unit + 1, start)
        arrivals(unit, (0, 1, 2), start, True)
        if unit + 1 < len(units):
            own_along(unit + 1, start)
        arrivals(unit, (3,), start, True)
        keep(unit).wait()
        compute(unit)

    share.wait_send()
    for lane, peer in enumerate((px, py, pd)):
        turning(lane, peer).wait_send()
    for part in range(2):
        for source, via in ((p, "own"), (px, "x"), (py, "y"), (pd, "d")):
            tokens(source, part, via, sent, False)
    for unit in range(len(units)):
        own_along(unit, sent)
        scatters(unit, sent)
        arrivals(unit, (0, 1, 2, 3), sent, False)
        for peer in (pd, px, py):
            home(unit, peer).wait_send()
        stay(unit).wait()
        for peer in (pd, px, py):
            landed(unit, peer).wait_recv()


def project(units, tokens, gain, shard, base_cos, base_sin, turn):
    span, width = tokens.shape
    count, rows, _ = shard.shape
    n = len(units)
    dma = pltpu.SemaphoreType.DMA
    vmem = pl.BlockSpec(memory_space=pltpu.VMEM)
    return pl.pallas_call(
        functools.partial(project_kernel, units),
        out_shape=jax.ShapeDtypeStruct((count, 4, span, GROUP), jnp.bfloat16),
        in_specs=[vmem, vmem, pl.BlockSpec(memory_space=pl.ANY), vmem, vmem, vmem],
        out_specs=pl.BlockSpec(memory_space=pl.ANY),
        scratch_shapes=[
            pltpu.VMEM((4, 4, span, width // 2), jnp.bfloat16),
            pltpu.VMEM((count, 4, 4, rows, GROUP), jnp.bfloat16),
            pltpu.VMEM((count, 4, span, GROUP), jnp.bfloat16),
            pltpu.VMEM((4, 8, GROUP), jnp.float32),
            pltpu.VMEM((2, span, 128), jnp.float32),
            dma((n, 4, 4, 2)),
            dma((n, 4, 4)),
            dma((n,)),
            dma((n, 3)),
            dma((4, 2, 3)),
            dma((4, 2, 2)),
            dma((3,)),
            dma((4,)),
            dma,
            dma((2,)),
            dma((n, 4)),
            dma((n, 4)),
            dma((n,)),
        ],
        compiler_params=pltpu.CompilerParams(
            collective_id=1, has_side_effects=True, vmem_limit_bytes=56 << 20
        ),
        cost_estimate=pl.CostEstimate(
            flops=2 * 4 * span * 2 * width * count * GROUP,
            bytes_accessed=64 << 20,
            transcendentals=0,
        ),
        name="project",
    )(tokens, gain, shard, base_cos, base_sin, turn)


def attend_kernel(span, cached, block, limits, qkv, cache, att, entries):
    length = limits[0]
    valid = limits[1]
    kept = lax.broadcasted_iota(jnp.int32, (span, GROUP), 0) < valid
    zeros = jnp.zeros((span, GROUP), jnp.float32)
    for part in range(2):
        entries[0, part] = jnp.where(kept, qkv[part + 1, 0].astype(jnp.float32), zeros).astype(
            jnp.bfloat16
        )

    scale = math.log2(math.e) / math.sqrt(HD)
    cache_bias = jnp.where(
        lax.broadcasted_iota(jnp.int32, (1, cached), 1) < length, 0.0, masked_value
    )
    dims = (((1,), (1,)), ((), ()))
    for step in range(span // block):
        rows = slice(step * block, (step + 1) * block)
        seen = (step + 1) * block
        row_ids = lax.broadcasted_iota(jnp.int32, (block, seen), 0) + step * block
        col_ids = lax.broadcasted_iota(jnp.int32, (block, seen), 1)
        live = (col_ids <= row_ids) & (col_ids < valid)
        gathered = [None] * (GROUP // 128)
        for head in range(GROUP // HD):
            low = head * HD // 128 * 128
            high = -(-(head + 1) * HD // 128) * 128
            window = slice(low, high)
            lane = lax.broadcasted_iota(jnp.int32, (block, high - low), 1) + low
            mine = (lane >= head * HD) & (lane < (head + 1) * HD)
            query = jnp.where(mine, qkv[0, 0, rows, window].astype(jnp.float32), 0.0).astype(
                jnp.bfloat16
            )
            old = (
                lax.dot_general(
                    query, cache[0, 0, :, window], dims, preferred_element_type=jnp.float32
                )
                * scale
                + cache_bias
            )
            new = (
                lax.dot_general(
                    query, qkv[1, 0, :seen, window], dims, preferred_element_type=jnp.float32
                )
                * scale
            )
            new = jnp.where(live, new, masked_value)
            top = jnp.maximum(
                jnp.max(old, axis=1, keepdims=True), jnp.max(new, axis=1, keepdims=True)
            )
            old = jnp.exp2(old - top)
            new = jnp.exp2(new - top)
            total = jnp.sum(old, axis=1, keepdims=True) + jnp.sum(new, axis=1, keepdims=True)
            inverse = 1.0 / total
            result = jnp.dot(
                (old * inverse).astype(jnp.bfloat16),
                cache[0, 1, :, window],
                preferred_element_type=jnp.float32,
            ) + jnp.dot(
                (new * inverse).astype(jnp.bfloat16),
                qkv[2, 0, :seen, window],
                preferred_element_type=jnp.float32,
            )
            result = jnp.where(mine, result, 0.0)
            for tile in range(low // 128, high // 128):
                piece = result[:, tile * 128 - low : (tile + 1) * 128 - low]
                gathered[tile] = piece if gathered[tile] is None else gathered[tile] + piece
        for tile, piece in enumerate(gathered):
            att[rows, tile * 128 : (tile + 1) * 128] = piece.astype(jnp.bfloat16)


def attend(limits, qkv, cache):
    _, groups, span, _ = qkv.shape
    cols = groups * GROUP
    cached = cache.shape[2]
    block = min(256, span)
    return pl.pallas_call(
        functools.partial(attend_kernel, span, cached, block),
        out_shape=(
            jax.ShapeDtypeStruct((span, cols), jnp.bfloat16),
            jax.ShapeDtypeStruct((1, 2, span, cols), jnp.bfloat16),
        ),
        grid_spec=pltpu.PrefetchScalarGridSpec(
            num_scalar_prefetch=1,
            grid=(groups,),
            in_specs=[
                pl.BlockSpec((3, 1, span, GROUP), lambda i, s: (0, i, 0, 0)),
                pl.BlockSpec((1, 2, cached, GROUP), lambda i, s: (0, 0, 0, i)),
            ],
            out_specs=(
                pl.BlockSpec((span, GROUP), lambda i, s: (0, i)),
                pl.BlockSpec((1, 2, span, GROUP), lambda i, s: (0, 0, 0, i)),
            ),
        ),
        compiler_params=pltpu.CompilerParams(vmem_limit_bytes=48 << 20),
        cost_estimate=pl.CostEstimate(
            flops=span * (cached + span) * cols * 8,
            bytes_accessed=cached * cols * 4 + span * cols * 20,
            transcendentals=span * (cached + span) * cols // HD,
        ),
        name="attend",
    )(limits, qkv, cache)


def project_grouped(tokens, norm_gain, qkv_weight, cache_lens):
    base_cos, base_sin, row, sign = base_tables(tokens.shape[0])
    angle = cache_lens[0].astype(jnp.float32) * row
    cosine, sine = jnp.cos(angle), jnp.sin(angle)
    turn = jnp.stack(
        [cosine, -sine, sine * sign, cosine * sign] + [jnp.zeros_like(cosine)] * 4
    )
    units = ((0, 0, GROUP), (1, 0, GROUP), (2, 0, 256), (2, 256, 128))
    return project(
        units, tokens, norm_gain[None, :], qkv_weight, base_cos, base_sin, turn
    )


def project_alone(tokens, norm_gain, qkv_weight, cache_lens):
    weights = lax.all_gather(qkv_weight, "req", axis=1, tiled=True)
    gathered = lax.all_gather(tokens, "tp", axis=1, tiled=True)
    gain_all = lax.all_gather(norm_gain, "tp", axis=0, tiled=True)
    inputs = gathered.astype(jnp.float32)
    spread = jnp.mean(inputs * inputs, axis=-1, keepdims=True)
    normed = (inputs * lax.rsqrt(spread + epsilon) * gain_all.astype(jnp.float32)).astype(
        jnp.bfloat16
    )
    span = normed.shape[0]
    cols = weights.shape[2]
    projected = jnp.einsum("td,jdc->jtc", normed, weights, preferred_element_type=jnp.float32)
    positions = cache_lens[0] + jnp.arange(span, dtype=jnp.int32)
    frequencies = jnp.power(theta_base, -jnp.arange(0, HD, 2, dtype=jnp.float32) / HD)
    angles = positions.astype(jnp.float32)[:, None] * frequencies[None, :]
    cosine, sine = jnp.cos(angles)[:, None, :], jnp.sin(angles)[:, None, :]
    heads = projected[:2].reshape(2, span, cols // HD, HD)
    a, b = heads[..., : HD // 2], heads[..., HD // 2 :]
    turned = jnp.concatenate([a * cosine - b * sine, b * cosine + a * sine], axis=-1)
    qkv = jnp.concatenate([turned.reshape(2, span, cols), projected[2:]], axis=0)
    return (
        qkv.astype(jnp.bfloat16).reshape(3, span, cols // GROUP, GROUP).transpose(0, 2, 1, 3)
    )


def per_device(mesh, tokens, norm_gain, qkv_weight, out_weight, cache, cache_lens, valid_tokens):
    out_all = lax.all_gather(out_weight.T, "req", axis=0, tiled=True)
    span, width = tokens.shape
    rows, cols = qkv_weight.shape[1:]
    grouped = (
        mesh.shape["req"] == 16
        and mesh.shape["tp"] == 2
        and cols == 4 * GROUP
        and width == 8 * rows
        and rows % 16 == 0
        and width % 256 == 0
        and span % 128 == 0
    )
    make = project_grouped if grouped else project_alone
    qkv = make(tokens, norm_gain, qkv_weight, cache_lens)
    limits = jnp.concatenate([cache_lens, valid_tokens])
    attended, new_entries = attend(limits, qkv, cache)
    partial_value = lax.dot_general(
        attended, out_all, (((1,), (1,)), ((), ())), preferred_element_type=jnp.float32
    )
    summed = lax.psum_scatter(
        partial_value.astype(jnp.bfloat16), "tp", scatter_dimension=1, tiled=True
    ).astype(jnp.float32)
    kept = (jnp.arange(span, dtype=jnp.int32) < valid_tokens[0])[:, None]
    mixed_out = jnp.where(kept, summed, jnp.zeros_like(summed)).astype(jnp.bfloat16)
    return (mixed_out, new_entries)


def solution(mesh):
    placed = (
        P("req", "tp"),
        P("tp"),
        P(None, "req", "tp"),
        P("tp", "req"),
        P("req", None, None, "tp"),
        P("req"),
        P("req"),
    )
    return jax.shard_map(
        functools.partial(per_device, mesh),
        mesh=mesh,
        in_specs=placed,
        out_specs=(P("req", "tp"), P("req", None, None, "tp")),
        check_vma=False,
    )
```

```python
import functools
import math

import jax
import jax.numpy as jnp
import numpy as np
from jax import lax
from jax.experimental import pallas as pl
from jax.experimental.pallas import tpu as pltpu
from jax.sharding import PartitionSpec as P

HD = 96
GROUP = 4 * HD

epsilon = 1e-05
masked_value = -1e30
theta_base = 10000.0


def base_tables(span):
    frequencies = np.power(theta_base, -np.arange(0, HD, 2, dtype=np.float64) / HD)
    row = np.tile(frequencies.astype(np.float32), 2 * GROUP // HD)
    angles = np.arange(span, dtype=np.float64)[:, None] * row[None, :].astype(np.float64)
    sign = np.tile(np.where(np.arange(HD) < HD // 2, -1.0, 1.0), GROUP // HD).astype(np.float32)
    return (
        np.cos(angles).astype(np.float32),
        np.sin(angles).astype(np.float32),
        row,
        sign,
    )


def project_kernel(
    units,
    tok,
    gain,
    shard,
    base_cos,
    base_sin,
    turn,
    out,
    normed,
    weights,
    staged,
    turns,
    squares,
    z_send,
    w_recv,
    own_sem,
    s_send,
    n_send,
    n_recv,
    t_send,
    t_recv,
    q_send,
    q_recv,
    r_send,
    r_recv,
    keep_sem,
):
    me = lax.axis_index("req")
    core = lax.axis_index("tp")
    z, y, x = lax.div(me, 4), lax.rem(lax.div(me, 2), 2), lax.rem(me, 2)
    p = lax.rem(me, 4)
    base = me - p
    px, py, pd = p + 1 - 2 * x, p + 2 - 4 * y, 3 - p
    span, width = tok.shape
    features = 2 * width
    half = span // 2
    mate = (me, 1 - core)

    barrier = pltpu.get_barrier_semaphore()

    def greet(target):
        pl.semaphore_signal(
            barrier, inc=1, device_id=target, device_id_type=pl.DeviceIdType.MESH
        )

    for peer in (px, py, pd):
        greet((base + peer, core))
    greet(mate)

    @pl.when(z < 3)
    def _():
        greet((me + 4, core))

    @pl.when(z > 0)
    def _():
        greet((me - 4, core))

    inner = jnp.where(z > 0, 1, 0) + jnp.where(z < 3, 1, 0)
    pl.semaphore_wait(barrier, 4 + inner)

    def remote(source, target_ref, sent, received, target):
        return pltpu.make_async_remote_copy(
            src_ref=source,
            dst_ref=target_ref,
            send_sem=sent,
            recv_sem=received,
            device_id=target,
            device_id_type=pl.DeviceIdType.MESH,
        )

    def columns(unit, peer):
        part, low, count = units[unit]
        return shard.at[part, :, pl.ds(pl.multiple_of(peer * GROUP + low, 128), count)]

    def block(unit, plane, source):
        part, low, count = units[unit]
        return weights.at[part, plane, source, :, low : low + count]

    def along(unit, plane, source, up, own):
        there = block(unit, plane, source)
        return remote(
            columns(unit, p) if own else there,
            there,
            z_send.at[unit, plane, source, 0 if up else 1],
            w_recv.at[unit, plane, source],
            (me + 4 if up else me - 4, core),
        )

    def scatter(unit, lane, peer):
        return remote(
            columns(unit, peer),
            block(unit, z, p),
            s_send.at[unit, lane],
            w_recv.at[unit, z, p],
            (base + peer, core),
        )

    def keep(unit):
        return pltpu.make_async_copy(columns(unit, p), block(unit, z, p), own_sem.at[unit])

    def own_along(unit, act):
        @pl.when(z < 3)
        def _():
            act(along(unit, z, p, True, True))

        @pl.when(z > 0)
        def _():
            act(along(unit, z, p, False, True))

    def scatters(unit, act):
        for lane, peer in enumerate((pd, px, py)):
            act(scatter(unit, lane, peer))

    def onward(unit, plane, source, up, down, act):
        if up:

            @pl.when(z < 3)
            def _():
                act(along(unit, plane, source, True, False))

        if down:

            @pl.when(z > 0)
            def _():
                act(along(unit, plane, source, False, False))

    def arrivals(unit, steps, act, arrived):
        for step in steps:
            if step == 0:
                for source in (px, py, pd):
                    if arrived:
                        along(unit, z, source, True, False).wait_recv()
                    onward(unit, z, source, True, True, act)
                continue
            for delta in (-step, step):

                def body(plane=z + delta, delta=delta):
                    for source in (p, px, py, pd):
                        if arrived:
                            along(unit, plane, source, True, False).wait_recv()
                        onward(unit, plane, source, delta < 0, delta > 0, act)

                pl.when(z + delta >= 0 if delta < 0 else z + delta <= 3)(body)

    def token(source, side, part, lane, target):
        ref = normed.at[source, pl.ds(2 * side, 2), part * half : (part + 1) * half, :]
        return remote(
            ref,
            ref,
            n_send.at[source, part, lane],
            n_recv.at[source, side, part],
            target,
        )

    to_x, to_y = (base + px, core), (base + py, core)

    def token_moves(source, part, via):
        moves = [(2, mate)]
        if via == "own" or (via == "y" and part == 1):
            moves.insert(0, (0, to_x))
        if via == "own" or (via == "x" and part == 0):
            moves.insert(0, (1, to_y))
        return [token(source, core, part, lane, target) for lane, target in moves]

    def tokens(source, part, via, act, arrived):
        if arrived:
            token(source, core, part, 2, mate).wait_recv()
        for copy in token_moves(source, part, via):
            act(copy)

    def turning(lane, peer):
        return remote(
            turns.at[p], turns.at[p], t_send.at[lane], t_recv.at[p], (base + peer, core)
        )

    def home(unit, peer):
        part, low, count = units[unit]
        return remote(
            staged.at[part, peer, :, low : low + count],
            out.at[part, p, :, low : low + count],
            r_send.at[unit, peer],
            r_recv.at[unit, p],
            (base + peer, core),
        )

    def landed(unit, source):
        part, low, count = units[unit]
        return remote(
            staged.at[part, source, :, low : low + count],
            out.at[part, source, :, low : low + count],
            r_send.at[unit, source],
            r_recv.at[unit, source],
            (base + source, core),
        )

    def stay(unit):
        part, low, count = units[unit]
        return pltpu.make_async_copy(
            staged.at[part, p, :, low : low + count],
            out.at[part, p, :, low : low + count],
            keep_sem.at[unit],
        )

    start = lambda c: c.start()
    sent = lambda c: c.wait_send()

    own_along(0, start)
    scatters(0, start)
    for unit in range(len(units)):
        keep(unit).start()
    turns[p] = turn[...]
    for lane, peer in enumerate((px, py, pd)):
        turning(lane, peer).start()

    rows = 64

    def measure(i, carry):
        at = pl.ds(i * rows, rows)
        v = tok[at, :].astype(jnp.float32)
        total = jnp.sum(v * v, axis=1, keepdims=True)
        squares[core, at, :] = jnp.broadcast_to(total, (rows, 128))
        return carry

    lax.fori_loop(0, span // rows, measure, 0)
    share = remote(squares.at[core], squares.at[core], q_send, q_recv.at[core], mate)
    share.start()
    remote(squares.at[1 - core], squares.at[1 - core], q_send, q_recv.at[1 - core], mate).wait_recv()
    gains = gain[...].astype(jnp.float32)

    def normalize(i, carry):
        at = pl.ds(i * rows, rows)
        spread = (squares[0, at, :] + squares[1, at, :])[:, :1] * (1.0 / features)
        v = tok[at, :].astype(jnp.float32) * lax.rsqrt(spread + epsilon) * gains
        v = v.astype(jnp.bfloat16)
        normed[p, 2 * core, at, :] = v[:, : width // 2]
        normed[p, 2 * core + 1, at, :] = v[:, width // 2 :]
        return carry

    for part in range(2):
        first = part * half // rows
        lax.fori_loop(first, first + half // rows, normalize, 0)
        tokens(p, part, "own", start, False)

    def compute(unit):
        part, low, count = units[unit]
        lane_in_head = lax.broadcasted_iota(jnp.int32, (span, GROUP), 1) % HD

        def body(i, carry):
            peer = jnp.where(i == 0, pd, jnp.where(i == 1, px, jnp.where(i == 2, py, p)))
            value = None
            for plane in range(4):
                chunk = weights[part, plane, :, :, low : low + count]
                term = jnp.dot(
                    normed[peer, plane],
                    chunk.reshape(chunk.shape[0] * chunk.shape[1], count),
                    preferred_element_type=jnp.float32,
                )
                value = term if value is None else value + term
            if part < 2:
                r = turns[peer]
                cosine = r[0:1] * base_cos[...] + r[1:2] * base_sin[...]
                sine = r[2:3] * base_cos[...] + r[3:4] * base_sin[...]
                ahead = pltpu.roll(value, GROUP - HD // 2, 1)
                behind = pltpu.roll(value, HD // 2, 1)
                value = value * cosine + jnp.where(lane_in_head < HD // 2, ahead, behind) * sine
            staged[part, peer, :, low : low + count] = value.astype(jnp.bfloat16)

            @pl.when(i < 3)
            def _():
                home(unit, peer).start()

            return carry

        lax.fori_loop(0, 4, body, 0)
        stay(unit).start()

    arrivals(0, (0, 1), start, True)
    scatters(1, start)
    tokens(px, 0, "x", start, True)
    tokens(py, 0, "y", start, True)
    arrivals(0, (2,), start, True)
    own_along(1, start)
    tokens(px, 1, "x", start, True)
    tokens(py, 1, "y", start, True)
    arrivals(0, (3,), start, True)
    arrivals(1, (0, 1), start, True)
    scatters(2, start)
    tokens(pd, 0, "d", start, True)
    tokens(pd, 1, "d", start, True)
    arrivals(1, (2,), start, True)
    own_along(2, start)
    for source in (p, px, py, pd):
        for part in range(2):
            token(source, 1 - core, part, 2, mate).wait_recv()
    for peer in (px, py, pd):
        remote(turns.at[peer], turns.at[peer], t_send.at[0], t_recv.at[peer], to_x).wait_recv()
    keep(0).wait()
    compute(0)
    arrivals(1, (3,), start, True)
    keep(1).wait()
    compute(1)
    for unit in range(2, len(units)):
        if unit > 2:
            pass
        if unit + 1 < len(units):
            scatters(unit + 1, start)
        arrivals(unit, (0, 1, 2), start, True)
        if unit + 1 < len(units):
            own_along(unit + 1, start)
        arrivals(unit, (3,), start, True)
        keep(unit).wait()
        compute(unit)

    share.wait_send()
    for lane, peer in enumerate((px, py, pd)):
        turning(lane, peer).wait_send()
    for part in range(2):
        for source, via in ((p, "own"), (px, "x"), (py, "y"), (pd, "d")):
            tokens(source, part, via, sent, False)
    for unit in range(len(units)):
        own_along(unit, sent)
        scatters(unit, sent)
        arrivals(unit, (0, 1, 2, 3), sent, False)
        for peer in (pd, px, py):
            home(unit, peer).wait_send()
        stay(unit).wait()
        for peer in (pd, px, py):
            landed(unit, peer).wait_recv()


def project(units, tokens, gain, shard, base_cos, base_sin, turn):
    span, width = tokens.shape
    count, rows, _ = shard.shape
    n = len(units)
    dma = pltpu.SemaphoreType.DMA
    vmem = pl.BlockSpec(memory_space=pltpu.VMEM)
    return pl.pallas_call(
        functools.partial(project_kernel, units),
        out_shape=jax.ShapeDtypeStruct((count, 4, span, GROUP), jnp.bfloat16),
        in_specs=[vmem, vmem, pl.BlockSpec(memory_space=pl.ANY), vmem, vmem, vmem],
        out_specs=pl.BlockSpec(memory_space=pl.ANY),
        scratch_shapes=[
            pltpu.VMEM((4, 4, span, width // 2), jnp.bfloat16),
            pltpu.VMEM((count, 4, 4, rows, GROUP), jnp.bfloat16),
            pltpu.VMEM((count, 4, span, GROUP), jnp.bfloat16),
            pltpu.VMEM((4, 8, GROUP), jnp.float32),
            pltpu.VMEM((2, span, 128), jnp.float32),
            dma((n, 4, 4, 2)),
            dma((n, 4, 4)),
            dma((n,)),
            dma((n, 3)),
            dma((4, 2, 3)),
            dma((4, 2, 2)),
            dma((3,)),
            dma((4,)),
            dma,
            dma((2,)),
            dma((n, 4)),
            dma((n, 4)),
            dma((n,)),
        ],
        compiler_params=pltpu.CompilerParams(
            collective_id=1, has_side_effects=True, vmem_limit_bytes=56 << 20
        ),
        cost_estimate=pl.CostEstimate(
            flops=2 * 4 * span * 2 * width * count * GROUP,
            bytes_accessed=64 << 20,
            transcendentals=0,
        ),
        name="project",
    )(tokens, gain, shard, base_cos, base_sin, turn)


def attend_group(span, cached, block, length, valid, qkv, cache, att, between):
    scale = math.log2(math.e) / math.sqrt(HD)
    cache_bias = jnp.where(
        lax.broadcasted_iota(jnp.int32, (1, cached), 1) < length, 0.0, masked_value
    )
    dims = (((1,), (1,)), ((), ()))
    for step in range(span // block):
        rows = slice(step * block, (step + 1) * block)
        seen = (step + 1) * block
        row_ids = lax.broadcasted_iota(jnp.int32, (block, seen), 0) + step * block
        col_ids = lax.broadcasted_iota(jnp.int32, (block, seen), 1)
        live = (col_ids <= row_ids) & (col_ids < valid)
        gathered = [None] * (GROUP // 128)
        for head in range(GROUP // HD):
            between(step * (GROUP // HD) + head)
            low = head * HD // 128 * 128
            high = -(-(head + 1) * HD // 128) * 128
            window = slice(low, high)
            lane = lax.broadcasted_iota(jnp.int32, (block, high - low), 1) + low
            mine = (lane >= head * HD) & (lane < (head + 1) * HD)
            query = jnp.where(mine, qkv[0, 0, rows, window].astype(jnp.float32), 0.0).astype(
                jnp.bfloat16
            )
            old = (
                lax.dot_general(
                    query, cache[0, 0, :, window], dims, preferred_element_type=jnp.float32
                )
                * scale
                + cache_bias
            )
            new = (
                lax.dot_general(
                    query, qkv[1, 0, :seen, window], dims, preferred_element_type=jnp.float32
                )
                * scale
            )
            new = jnp.where(live, new, masked_value)
            top = jnp.maximum(
                jnp.max(old, axis=1, keepdims=True), jnp.max(new, axis=1, keepdims=True)
            )
            old = jnp.exp2(old - top)
            new = jnp.exp2(new - top)
            total = jnp.sum(old, axis=1, keepdims=True) + jnp.sum(new, axis=1, keepdims=True)
            inverse = 1.0 / total
            result = jnp.dot(
                (old * inverse).astype(jnp.bfloat16),
                cache[0, 1, :, window],
                preferred_element_type=jnp.float32,
            ) + jnp.dot(
                (new * inverse).astype(jnp.bfloat16),
                qkv[2, 0, :seen, window],
                preferred_element_type=jnp.float32,
            )
            result = jnp.where(mine, result, 0.0)
            for tile in range(low // 128, high // 128):
                piece = result[:, tile * 128 - low : (tile + 1) * 128 - low]
                gathered[tile] = piece if gathered[tile] is None else gathered[tile] + piece
        for tile, piece in enumerate(gathered):
            att[rows, tile * 128 : (tile + 1) * 128] = piece.astype(jnp.bfloat16)


def attend_kernel(span, cached, block, limits, qkv, cache, att):
    attend_group(span, cached, block, limits[0], limits[1], qkv, cache, att, lambda slot: None)


def attend(limits, qkv, cache):
    _, groups, span, _ = qkv.shape
    cols = groups * GROUP
    cached = cache.shape[2]
    block = min(256, span)
    return pl.pallas_call(
        functools.partial(attend_kernel, span, cached, block),
        out_shape=jax.ShapeDtypeStruct((span, cols), jnp.bfloat16),
        grid=(groups,),
        in_specs=[
            pl.BlockSpec(memory_space=pltpu.SMEM),
            pl.BlockSpec((3, 1, span, GROUP), lambda i: (0, i, 0, 0)),
            pl.BlockSpec((1, 2, cached, GROUP), lambda i: (0, 0, 0, i)),
        ],
        out_specs=pl.BlockSpec((span, GROUP), lambda i: (0, i)),
        compiler_params=pltpu.CompilerParams(vmem_limit_bytes=48 << 20),
        name="attend",
    )(limits, qkv, cache)


def gather_events():
    events = []
    for stream, order in enumerate(("xyz", "zyx", "zxy")):
        for dz in range(-3, 4):
            for dy in range(2):
                for dx in range(2):
                    offset = {"z": dz, "y": dy, "x": dx}
                    moved = [axis for axis in order if offset[axis]]
                    if moved:
                        hops = abs(dz) + dy + dx
                        events.append((hops, order.index(moved[-1]), stream, moved[-1], dz, dy, dx))
    events.sort()
    return [(stream, via, dz, dy, dx) for _, _, stream, via, dz, dy, dx in events]


def attend_gather_kernel(
    cuts,
    span,
    cached,
    block,
    limits,
    qkv,
    cache,
    shard,
    att,
    full,
    send_sem,
    recv_sem,
    own_sem,
):
    step_id = pl.program_id(0)
    steps = 4
    me = lax.axis_index("req")
    core = lax.axis_index("tp")
    z, y, x = lax.div(me, 4), lax.rem(lax.div(me, 2), 2), lax.rem(me, 2)
    beside = {"x": me + 1 - 2 * x, "y": me + 2 - 4 * y}
    orders = ("xyz", "zyx", "zxy")

    def piece(ref, stream, source):
        return ref.at[source, cuts[stream] : cuts[stream + 1], :]

    def copy(stream, source, lane, target, own):
        there = piece(full, stream, source)
        here = shard.at[cuts[stream] : cuts[stream + 1], :] if own else there
        return pltpu.make_async_remote_copy(
            src_ref=here,
            dst_ref=there,
            send_sem=send_sem.at[stream, source, lane],
            recv_sem=recv_sem.at[stream, source],
            device_id=(target, core),
            device_id_type=pl.DeviceIdType.MESH,
        )

    def forward(stream, source, via, dz, own, act):
        order = orders[stream]
        for axis in order[order.index(via) if via else 0 :]:
            if axis == "z":
                if not via or dz < 0 or via != "z":

                    @pl.when(z < 3)
                    def _():
                        act(copy(stream, source, 0, me + 4, own))

                if not via or dz > 0 or via != "z":

                    @pl.when(z > 0)
                    def _():
                        act(copy(stream, source, 1, me - 4, own))

            elif axis != via:
                lane = 2 if axis == "y" else 3
                act(copy(stream, source, lane, beside[axis], own))

    @pl.when(step_id == 0)
    def _():
        barrier = pltpu.get_barrier_semaphore()

        def greet(target):
            pl.semaphore_signal(
                barrier, inc=1, device_id=(target, core), device_id_type=pl.DeviceIdType.MESH
            )

        greet(beside["x"])
        greet(beside["y"])

        @pl.when(z < 3)
        def _():
            greet(me + 4)

        @pl.when(z > 0)
        def _():
            greet(me - 4)

        inner = jnp.where(z > 0, 1, 0) + jnp.where(z < 3, 1, 0)
        pl.semaphore_wait(barrier, 2 + inner)

        for stream in (1, 2, 0):
            forward(stream, me, None, 0, True, lambda c: c.start())
        pltpu.make_async_copy(shard, full.at[me], own_sem).start()

    def visit(event, act, arrived):
        stream, via, dz, dy, dx = event
        source = me + 4 * dz + dy * (2 - 4 * y) + dx * (1 - 2 * x)

        def body():
            if arrived:
                copy(stream, source, 0, beside["x"], False).wait_recv()
            forward(stream, source, via, dz, False, act)

        if dz > 0:
            pl.when(z + dz <= 3)(body)
        elif dz < 0:
            pl.when(z + dz >= 0)(body)
        else:
            body()

    events = gather_events()
    slots = span // block * (GROUP // HD)
    spread = steps * slots

    def between(slot):
        for step in range(steps):
            at = step * slots + slot
            first = len(events) * at // spread
            last = len(events) * (at + 1) // spread
            if first < last:

                @pl.when(step_id == step)
                def _():
                    for event in events[first:last]:
                        visit(event, lambda c: c.start(), True)

    attend_group(span, cached, block, limits[0], limits[1], qkv, cache, att, between)

    @pl.when(step_id == steps - 1)
    def _():
        for stream in (1, 2, 0):
            forward(stream, me, None, 0, True, lambda c: c.wait_send())
        for event in events:
            visit(event, lambda c: c.wait_send(), False)
        pltpu.make_async_copy(shard, full.at[me], own_sem).wait()


def attend_gather(limits, qkv, cache, shard):
    _, groups, span, _ = qkv.shape
    cols = groups * GROUP
    cached = cache.shape[2]
    block = min(256, span)
    rows = shard.shape[0]
    unit = rows // 12
    cuts = (0, 2 * unit, 7 * unit, rows)
    att, full = pl.pallas_call(
        functools.partial(attend_gather_kernel, cuts, span, cached, block),
        out_shape=(
            jax.ShapeDtypeStruct((span, cols), jnp.bfloat16),
            jax.ShapeDtypeStruct((16,) + shard.shape, shard.dtype),
        ),
        grid=(groups,),
        in_specs=[
            pl.BlockSpec(memory_space=pltpu.SMEM),
            pl.BlockSpec((3, 1, span, GROUP), lambda i: (0, i, 0, 0)),
            pl.BlockSpec((1, 2, cached, GROUP), lambda i: (0, 0, 0, i)),
            pl.BlockSpec(memory_space=pl.ANY),
        ],
        out_specs=(
            pl.BlockSpec((span, GROUP), lambda i: (0, i)),
            pl.BlockSpec(memory_space=pl.ANY),
        ),
        scratch_shapes=[
            pltpu.SemaphoreType.DMA((3, 16, 4)),
            pltpu.SemaphoreType.DMA((3, 16)),
            pltpu.SemaphoreType.DMA,
        ],
        compiler_params=pltpu.CompilerParams(
            collective_id=2, has_side_effects=True, vmem_limit_bytes=48 << 20
        ),
        cost_estimate=pl.CostEstimate(
            flops=span * (cached + span) * cols * 8,
            bytes_accessed=cached * cols * 4 + span * cols * 20,
            transcendentals=span * (cached + span) * cols // HD,
        ),
        name="attend_gather",
    )(limits, qkv, cache, shard)
    return att, full.reshape(16 * rows, cols)


def project_grouped(tokens, norm_gain, qkv_weight, cache_lens):
    base_cos, base_sin, row, sign = base_tables(tokens.shape[0])
    angle = cache_lens[0].astype(jnp.float32) * row
    cosine, sine = jnp.cos(angle), jnp.sin(angle)
    turn = jnp.stack(
        [cosine, -sine, sine * sign, cosine * sign] + [jnp.zeros_like(cosine)] * 4
    )
    units = ((0, 0, GROUP), (1, 0, GROUP), (2, 0, 256), (2, 256, 128))
    return project(
        units, tokens, norm_gain[None, :], qkv_weight, base_cos, base_sin, turn
    )


def project_alone(tokens, norm_gain, qkv_weight, cache_lens):
    weights = lax.all_gather(qkv_weight, "req", axis=1, tiled=True)
    gathered = lax.all_gather(tokens, "tp", axis=1, tiled=True)
    gain_all = lax.all_gather(norm_gain, "tp", axis=0, tiled=True)
    inputs = gathered.astype(jnp.float32)
    spread = jnp.mean(inputs * inputs, axis=-1, keepdims=True)
    normed = (inputs * lax.rsqrt(spread + epsilon) * gain_all.astype(jnp.float32)).astype(
        jnp.bfloat16
    )
    span = normed.shape[0]
    cols = weights.shape[2]
    projected = jnp.einsum("td,jdc->jtc", normed, weights, preferred_element_type=jnp.float32)
    positions = cache_lens[0] + jnp.arange(span, dtype=jnp.int32)
    frequencies = jnp.power(theta_base, -jnp.arange(0, HD, 2, dtype=jnp.float32) / HD)
    angles = positions.astype(jnp.float32)[:, None] * frequencies[None, :]
    cosine, sine = jnp.cos(angles)[:, None, :], jnp.sin(angles)[:, None, :]
    heads = projected[:2].reshape(2, span, cols // HD, HD)
    a, b = heads[..., : HD // 2], heads[..., HD // 2 :]
    turned = jnp.concatenate([a * cosine - b * sine, b * cosine + a * sine], axis=-1)
    qkv = jnp.concatenate([turned.reshape(2, span, cols), projected[2:]], axis=0)
    return (
        qkv.astype(jnp.bfloat16).reshape(3, span, cols // GROUP, GROUP).transpose(0, 2, 1, 3)
    )


def per_device(mesh, tokens, norm_gain, qkv_weight, out_weight, cache, cache_lens, valid_tokens):
    span, width = tokens.shape
    rows, cols = qkv_weight.shape[1:]
    grouped = (
        mesh.shape["req"] == 16
        and mesh.shape["tp"] == 2
        and cols == 4 * GROUP
        and width == 8 * rows
        and rows % 16 == 0
        and width % 256 == 0
        and span % 128 == 0
        and rows % 192 == 0
        and out_weight.shape == (cols, rows)
    )
    limits = jnp.concatenate([cache_lens, valid_tokens])
    if grouped:
        qkv = project_grouped(tokens, norm_gain, qkv_weight, cache_lens)
        attended, out_all = attend_gather(limits, qkv, cache, out_weight.T)
    else:
        qkv = project_alone(tokens, norm_gain, qkv_weight, cache_lens)
        out_all = lax.all_gather(out_weight.T, "req", axis=0, tiled=True)
        attended = attend(limits, qkv, cache)
    kept = (jnp.arange(span, dtype=jnp.int32) < valid_tokens[0])[:, None]
    entries = qkv[1:].transpose(0, 2, 1, 3).reshape(2, span, cols)
    new_entries = jnp.where(kept, entries, jnp.zeros_like(entries))[None]
    partial_value = lax.dot_general(
        attended, out_all, (((1,), (1,)), ((), ())), preferred_element_type=jnp.float32
    )
    summed = lax.psum_scatter(
        partial_value.astype(jnp.bfloat16), "tp", scatter_dimension=1, tiled=True
    ).astype(jnp.float32)
    mixed_out = jnp.where(kept, summed, jnp.zeros_like(summed)).astype(jnp.bfloat16)
    return (mixed_out, new_entries)


def solution(mesh):
    placed = (
        P("req", "tp"),
        P("tp"),
        P(None, "req", "tp"),
        P("tp", "req"),
        P("req", None, None, "tp"),
        P("req"),
        P("req"),
    )
    return jax.shard_map(
        functools.partial(per_device, mesh),
        mesh=mesh,
        in_specs=placed,
        out_specs=(P("req", "tp"), P("req", None, None, "tp")),
        check_vma=False,
    )
```

```python
import functools
import math

import jax
import jax.numpy as jnp
import numpy as np
from jax import lax
from jax.experimental import pallas as pl
from jax.experimental.pallas import tpu as pltpu
from jax.sharding import PartitionSpec as P

HD = 96
GROUP = 4 * HD

epsilon = 1e-05
masked_value = -1e30
theta_base = 10000.0


def base_tables(span):
    frequencies = np.power(theta_base, -np.arange(0, HD, 2, dtype=np.float64) / HD)
    row = np.tile(frequencies.astype(np.float32), 2 * GROUP // HD)
    angles = np.arange(span, dtype=np.float64)[:, None] * row[None, :].astype(np.float64)
    sign = np.tile(np.where(np.arange(HD) < HD // 2, -1.0, 1.0), GROUP // HD).astype(np.float32)
    return (
        np.cos(angles).astype(np.float32),
        np.sin(angles).astype(np.float32),
        row,
        sign,
    )


def project_kernel(
    units,
    tok,
    gain,
    shard,
    base_cos,
    base_sin,
    turn,
    later,
    out,
    full,
    normed,
    weights,
    staged,
    turns,
    squares,
    z_send,
    w_recv,
    own_sem,
    s_send,
    n_send,
    n_recv,
    t_send,
    t_recv,
    q_send,
    q_recv,
    r_send,
    r_recv,
    keep_sem,
    f_send,
    f_recv,
    f_own,
):
    me = lax.axis_index("req")
    core = lax.axis_index("tp")
    z, y, x = lax.div(me, 4), lax.rem(lax.div(me, 2), 2), lax.rem(me, 2)
    p = lax.rem(me, 4)
    base = me - p
    px, py, pd = p + 1 - 2 * x, p + 2 - 4 * y, 3 - p
    span, width = tok.shape
    features = 2 * width
    half = span // 2
    mate = (me, 1 - core)

    barrier = pltpu.get_barrier_semaphore()

    def greet(target):
        pl.semaphore_signal(
            barrier, inc=1, device_id=target, device_id_type=pl.DeviceIdType.MESH
        )

    for peer in (px, py, pd):
        greet((base + peer, core))
    greet(mate)

    @pl.when(z < 3)
    def _():
        greet((me + 4, core))

    @pl.when(z > 0)
    def _():
        greet((me - 4, core))

    inner = jnp.where(z > 0, 1, 0) + jnp.where(z < 3, 1, 0)
    pl.semaphore_wait(barrier, 4 + inner)

    def remote(source, target_ref, sent, received, target):
        return pltpu.make_async_remote_copy(
            src_ref=source,
            dst_ref=target_ref,
            send_sem=sent,
            recv_sem=received,
            device_id=target,
            device_id_type=pl.DeviceIdType.MESH,
        )

    def columns(unit, peer):
        part, low, count = units[unit]
        return shard.at[part, :, pl.ds(pl.multiple_of(peer * GROUP + low, 128), count)]

    def block(unit, plane, source):
        part, low, count = units[unit]
        return weights.at[part, plane, source, :, low : low + count]

    def along(unit, plane, source, up, own):
        there = block(unit, plane, source)
        return remote(
            columns(unit, p) if own else there,
            there,
            z_send.at[unit, plane, source, 0 if up else 1],
            w_recv.at[unit, plane, source],
            (me + 4 if up else me - 4, core),
        )

    def scatter(unit, lane, peer):
        return remote(
            columns(unit, peer),
            block(unit, z, p),
            s_send.at[unit, lane],
            w_recv.at[unit, z, p],
            (base + peer, core),
        )

    def keep(unit):
        return pltpu.make_async_copy(columns(unit, p), block(unit, z, p), own_sem.at[unit])

    def own_along(unit, act):
        @pl.when(z < 3)
        def _():
            act(along(unit, z, p, True, True))

        @pl.when(z > 0)
        def _():
            act(along(unit, z, p, False, True))

    def scatters(unit, act):
        for lane, peer in enumerate((pd, px, py)):
            act(scatter(unit, lane, peer))

    def onward(unit, plane, source, up, down, act):
        if up:

            @pl.when(z < 3)
            def _():
                act(along(unit, plane, source, True, False))

        if down:

            @pl.when(z > 0)
            def _():
                act(along(unit, plane, source, False, False))

    def arrivals(unit, steps, act, arrived):
        for step in steps:
            if step == 0:
                for source in (px, py, pd):
                    if arrived:
                        along(unit, z, source, True, False).wait_recv()
                    onward(unit, z, source, True, True, act)
                continue
            for delta in (-step, step):

                def body(plane=z + delta, delta=delta):
                    for source in (p, px, py, pd):
                        if arrived:
                            along(unit, plane, source, True, False).wait_recv()
                        onward(unit, plane, source, delta < 0, delta > 0, act)

                pl.when(z + delta >= 0 if delta < 0 else z + delta <= 3)(body)

    def token(source, side, part, lane, target):
        ref = normed.at[source, pl.ds(2 * side, 2), part * half : (part + 1) * half, :]
        return remote(
            ref,
            ref,
            n_send.at[source, part, lane],
            n_recv.at[source, side, part],
            target,
        )

    to_x, to_y = (base + px, core), (base + py, core)

    def token_moves(source, part, via):
        moves = [(2, mate)]
        if via == "own" or (via == "y" and part == 1):
            moves.insert(0, (0, to_x))
        if via == "own" or (via == "x" and part == 0):
            moves.insert(0, (1, to_y))
        return [token(source, core, part, lane, target) for lane, target in moves]

    def tokens(source, part, via, act, arrived):
        if arrived:
            token(source, core, part, 2, mate).wait_recv()
        for copy in token_moves(source, part, via):
            act(copy)

    def turning(lane, peer):
        return remote(
            turns.at[p], turns.at[p], t_send.at[lane], t_recv.at[p], (base + peer, core)
        )

    def home(unit, peer):
        part, low, count = units[unit]
        return remote(
            staged.at[part, peer, :, low : low + count],
            out.at[part, :, pl.ds(pl.multiple_of(p * GROUP + low, 128), count)],
            r_send.at[unit, peer],
            r_recv.at[unit, p],
            (base + peer, core),
        )

    def landed(unit, source):
        part, low, count = units[unit]
        return remote(
            staged.at[part, source, :, low : low + count],
            out.at[part, :, pl.ds(pl.multiple_of(source * GROUP + low, 128), count)],
            r_send.at[unit, source],
            r_recv.at[unit, source],
            (base + source, core),
        )

    def stay(unit):
        part, low, count = units[unit]
        return pltpu.make_async_copy(
            staged.at[part, p, :, low : low + count],
            out.at[part, :, pl.ds(pl.multiple_of(p * GROUP + low, 128), count)],
            keep_sem.at[unit],
        )

    start = lambda c: c.start()
    sent = lambda c: c.wait_send()

    own_along(0, start)
    scatters(0, start)
    for unit in range(len(units)):
        keep(unit).start()
    turns[p] = turn[...]
    for lane, peer in enumerate((px, py, pd)):
        turning(lane, peer).start()

    rows = 64

    def measure(i, carry):
        at = pl.ds(i * rows, rows)
        v = tok[at, :].astype(jnp.float32)
        total = jnp.sum(v * v, axis=1, keepdims=True)
        squares[core, at, :] = jnp.broadcast_to(total, (rows, 128))
        return carry

    lax.fori_loop(0, span // rows, measure, 0)
    share = remote(squares.at[core], squares.at[core], q_send, q_recv.at[core], mate)
    share.start()
    remote(squares.at[1 - core], squares.at[1 - core], q_send, q_recv.at[1 - core], mate).wait_recv()
    gains = gain[...].astype(jnp.float32)

    def normalize(i, carry):
        at = pl.ds(i * rows, rows)
        spread = (squares[0, at, :] + squares[1, at, :])[:, :1] * (1.0 / features)
        v = tok[at, :].astype(jnp.float32) * lax.rsqrt(spread + epsilon) * gains
        v = v.astype(jnp.bfloat16)
        normed[p, 2 * core, at, :] = v[:, : width // 2]
        normed[p, 2 * core + 1, at, :] = v[:, width // 2 :]
        return carry

    for part in range(2):
        first = part * half // rows
        lax.fori_loop(first, first + half // rows, normalize, 0)
        tokens(p, part, "own", start, False)

    def compute(unit):
        part, low, count = units[unit]
        lane_in_head = lax.broadcasted_iota(jnp.int32, (span, GROUP), 1) % HD

        def body(i, carry):
            peer = jnp.where(i == 0, pd, jnp.where(i == 1, px, jnp.where(i == 2, py, p)))
            value = None
            for plane in range(4):
                chunk = weights[part, plane, :, :, low : low + count]
                term = jnp.dot(
                    normed[peer, plane],
                    chunk.reshape(chunk.shape[0] * chunk.shape[1], count),
                    preferred_element_type=jnp.float32,
                )
                value = term if value is None else value + term
            if part < 2:
                r = turns[peer]
                cosine = r[0:1] * base_cos[...] + r[1:2] * base_sin[...]
                sine = r[2:3] * base_cos[...] + r[3:4] * base_sin[...]
                ahead = pltpu.roll(value, GROUP - HD // 2, 1)
                behind = pltpu.roll(value, HD // 2, 1)
                value = value * cosine + jnp.where(lane_in_head < HD // 2, ahead, behind) * sine
            staged[part, peer, :, low : low + count] = value.astype(jnp.bfloat16)

            @pl.when(i < 3)
            def _():
                home(unit, peer).start()

            return carry

        lax.fori_loop(0, 4, body, 0)
        stay(unit).start()

    spread = Spread(later.at[:, : full.shape[2]], full, f_send, f_recv, f_own)
    slot = [0]

    def more():
        spread.step(slot[0], 5 + 4 * (len(units) - 1))
        slot[0] += 1

    arrivals(0, (0, 1), start, True)
    scatters(1, start)
    tokens(px, 0, "x", start, True)
    tokens(py, 0, "y", start, True)
    arrivals(0, (2,), start, True)
    own_along(1, start)
    tokens(px, 1, "x", start, True)
    tokens(py, 1, "y", start, True)
    spread.begin()
    arrivals(0, (3,), start, True)
    more()
    arrivals(1, (0, 1), start, True)
    scatters(2, start)
    more()
    tokens(pd, 0, "d", start, True)
    tokens(pd, 1, "d", start, True)
    more()
    arrivals(1, (2,), start, True)
    own_along(2, start)
    more()
    for source in (p, px, py, pd):
        for part in range(2):
            token(source, 1 - core, part, 2, mate).wait_recv()
    for peer in (px, py, pd):
        remote(turns.at[peer], turns.at[peer], t_send.at[0], t_recv.at[peer], to_x).wait_recv()
    keep(0).wait()
    compute(0)
    more()
    arrivals(1, (3,), start, True)
    more()
    keep(1).wait()
    compute(1)
    for unit in range(2, len(units)):
        more()
        if unit + 1 < len(units):
            scatters(unit + 1, start)
        arrivals(unit, (0, 1), start, True)
        more()
        arrivals(unit, (2,), start, True)
        if unit + 1 < len(units):
            own_along(unit + 1, start)
        more()
        arrivals(unit, (3,), start, True)
        more()
        keep(unit).wait()
        compute(unit)
    while slot[0] < 5 + 4 * (len(units) - 1):
        more()

    share.wait_send()
    for lane, peer in enumerate((px, py, pd)):
        turning(lane, peer).wait_send()
    for part in range(2):
        for source, via in ((p, "own"), (px, "x"), (py, "y"), (pd, "d")):
            tokens(source, part, via, sent, False)
    for unit in range(len(units)):
        own_along(unit, sent)
        scatters(unit, sent)
        arrivals(unit, (0, 1, 2, 3), sent, False)
        for peer in (pd, px, py):
            home(unit, peer).wait_send()
        stay(unit).wait()
        for peer in (pd, px, py):
            landed(unit, peer).wait_recv()
    spread.kept().wait()
    spread.end()


def project(units, cut, tokens, gain, shard, base_cos, base_sin, turn, later):
    span, width = tokens.shape
    count, rows, _ = shard.shape
    n = len(units)
    dma = pltpu.SemaphoreType.DMA
    vmem = pl.BlockSpec(memory_space=pltpu.VMEM)
    hbm = pl.BlockSpec(memory_space=pl.ANY)
    return pl.pallas_call(
        functools.partial(project_kernel, units),
        out_shape=(
            jax.ShapeDtypeStruct((count, span, 4 * GROUP), jnp.bfloat16),
            jax.ShapeDtypeStruct((16, later.shape[0], cut), later.dtype),
        ),
        in_specs=[vmem, vmem, hbm, vmem, vmem, vmem, hbm],
        out_specs=(hbm, hbm),
        scratch_shapes=[
            pltpu.VMEM((4, 4, span, width // 2), jnp.bfloat16),
            pltpu.VMEM((count, 4, 4, rows, GROUP), jnp.bfloat16),
            pltpu.VMEM((count, 4, span, GROUP), jnp.bfloat16),
            pltpu.VMEM((4, 8, GROUP), jnp.float32),
            pltpu.VMEM((2, span, 128), jnp.float32),
            dma((n, 4, 4, 2)),
            dma((n, 4, 4)),
            dma((n,)),
            dma((n, 3)),
            dma((4, 2, 3)),
            dma((4, 2, 2)),
            dma((3,)),
            dma((4,)),
            dma,
            dma((2,)),
            dma((n, 4)),
            dma((n, 4)),
            dma((n,)),
        ]
        + spread_semaphores(),
        compiler_params=pltpu.CompilerParams(
            collective_id=1, has_side_effects=True, vmem_limit_bytes=56 << 20
        ),
        cost_estimate=pl.CostEstimate(
            flops=2 * 4 * span * 2 * width * count * GROUP,
            bytes_accessed=64 << 20,
            transcendentals=0,
        ),
        name="project",
    )(tokens, gain, shard, base_cos, base_sin, turn, later)


def attend_group(span, cached, block, length, valid, qkv, cache, store, between):
    scale = math.log2(math.e) / math.sqrt(HD)
    cache_bias = jnp.where(
        lax.broadcasted_iota(jnp.int32, (1, cached), 1) < length, 0.0, masked_value
    )
    dims = (((1,), (1,)), ((), ()))
    for step in range(span // block):
        rows = slice(step * block, (step + 1) * block)
        seen = (step + 1) * block
        row_ids = lax.broadcasted_iota(jnp.int32, (block, seen), 0) + step * block
        col_ids = lax.broadcasted_iota(jnp.int32, (block, seen), 1)
        live = (col_ids <= row_ids) & (col_ids < valid)
        gathered = [None] * (GROUP // 128)
        for head in range(GROUP // HD):
            between(step * (GROUP // HD) + head)
            low = head * HD // 128 * 128
            high = -(-(head + 1) * HD // 128) * 128
            window = slice(low, high)
            lane = lax.broadcasted_iota(jnp.int32, (block, high - low), 1) + low
            mine = (lane >= head * HD) & (lane < (head + 1) * HD)
            query = jnp.where(mine, qkv[0, rows, window].astype(jnp.float32), 0.0).astype(
                jnp.bfloat16
            )
            old = (
                lax.dot_general(
                    query, cache[0, 0, :, window], dims, preferred_element_type=jnp.float32
                )
                * scale
                + cache_bias
            )
            new = (
                lax.dot_general(
                    query, qkv[1, :seen, window], dims, preferred_element_type=jnp.float32
                )
                * scale
            )
            new = jnp.where(live, new, masked_value)
            top = jnp.maximum(
                jnp.max(old, axis=1, keepdims=True), jnp.max(new, axis=1, keepdims=True)
            )
            old = jnp.exp2(old - top)
            new = jnp.exp2(new - top)
            total = jnp.sum(old, axis=1, keepdims=True) + jnp.sum(new, axis=1, keepdims=True)
            inverse = 1.0 / total
            result = jnp.dot(
                (old * inverse).astype(jnp.bfloat16),
                cache[0, 1, :, window],
                preferred_element_type=jnp.float32,
            ) + jnp.dot(
                (new * inverse).astype(jnp.bfloat16),
                qkv[2, :seen, window],
                preferred_element_type=jnp.float32,
            )
            result = jnp.where(mine, result, 0.0)
            for tile in range(low // 128, high // 128):
                piece = result[:, tile * 128 - low : (tile + 1) * 128 - low]
                gathered[tile] = piece if gathered[tile] is None else gathered[tile] + piece
        for tile, piece in enumerate(gathered):
            store(rows, slice(tile * 128, (tile + 1) * 128), piece.astype(jnp.bfloat16))


def attend_kernel(span, cached, block, limits, qkv, cache, att):
    def store(rows, columns, value):
        att[rows, columns] = value

    attend_group(
        span, cached, block, limits[0], limits[1], qkv, cache, store, lambda slot: None
    )


def attend(limits, qkv, cache):
    _, span, cols = qkv.shape
    groups = cols // GROUP
    cached = cache.shape[2]
    block = min(256, span)
    return pl.pallas_call(
        functools.partial(attend_kernel, span, cached, block),
        out_shape=jax.ShapeDtypeStruct((span, cols), jnp.bfloat16),
        grid=(groups,),
        in_specs=[
            pl.BlockSpec(memory_space=pltpu.SMEM),
            pl.BlockSpec((3, span, GROUP), lambda i: (0, 0, i)),
            pl.BlockSpec((1, 2, cached, GROUP), lambda i: (0, 0, 0, i)),
        ],
        out_specs=pl.BlockSpec((span, GROUP), lambda i: (0, i)),
        compiler_params=pltpu.CompilerParams(vmem_limit_bytes=48 << 20),
        name="attend",
    )(limits, qkv, cache)


def gather_events():
    events = []
    for stream, order in enumerate(("xyz", "zyx", "zxy")):
        for dz in range(-3, 4):
            for dy in range(2):
                for dx in range(2):
                    offset = {"z": dz, "y": dy, "x": dx}
                    moved = [axis for axis in order if offset[axis]]
                    if moved:
                        hops = abs(dz) + dy + dx
                        events.append((hops, order.index(moved[-1]), stream, moved[-1], dz, dy, dx))
    events.sort()
    return [(stream, via, dz, dy, dx) for _, _, stream, via, dz, dy, dx in events]


class Spread:
    def __init__(self, shard, full, send_sem, recv_sem, own_sem):
        me = lax.axis_index("req")
        core = lax.axis_index("tp")
        z, y, x = lax.div(me, 4), lax.rem(lax.div(me, 2), 2), lax.rem(me, 2)
        beside = {"x": me + 1 - 2 * x, "y": me + 2 - 4 * y}
        orders = ("xyz", "zyx", "zxy")
        unit = shard.shape[0] // 12
        cuts = (0, 2 * unit, 7 * unit, 12 * unit)

        def copy(stream, source, lane, target, own):
            there = full.at[source, cuts[stream] : cuts[stream + 1], :]
            here = shard.at[cuts[stream] : cuts[stream + 1], :] if own else there
            return pltpu.make_async_remote_copy(
                src_ref=here,
                dst_ref=there,
                send_sem=send_sem.at[stream, source, lane],
                recv_sem=recv_sem.at[stream, source],
                device_id=(target, core),
                device_id_type=pl.DeviceIdType.MESH,
            )

        def forward(stream, source, via, dz, own, act):
            order = orders[stream]
            for axis in order[order.index(via) if via else 0 :]:
                if axis == "z":
                    if not via or dz < 0 or via != "z":

                        @pl.when(z < 3)
                        def _():
                            act(copy(stream, source, 0, me + 4, own))

                    if not via or dz > 0 or via != "z":

                        @pl.when(z > 0)
                        def _():
                            act(copy(stream, source, 1, me - 4, own))

                elif axis != via:
                    lane = 2 if axis == "y" else 3
                    act(copy(stream, source, lane, beside[axis], own))

        def visit(event, act, arrived):
            stream, via, dz, dy, dx = event
            source = me + 4 * dz + dy * (2 - 4 * y) + dx * (1 - 2 * x)

            def body():
                if arrived:
                    copy(stream, source, 0, beside["x"], False).wait_recv()
                forward(stream, source, via, dz, False, act)

            if dz > 0:
                pl.when(z + dz <= 3)(body)
            elif dz < 0:
                pl.when(z + dz >= 0)(body)
            else:
                body()

        self.events = gather_events()
        self.own = lambda act: [forward(i, me, None, 0, True, act) for i in (1, 2, 0)]
        self.kept = lambda: pltpu.make_async_copy(shard, full.at[me], own_sem)
        self.visit = visit

    def begin(self):
        self.own(lambda c: c.start())
        self.kept().start()

    def step(self, slot, slots):
        n = len(self.events)
        for event in self.events[n * slot // slots : n * (slot + 1) // slots]:
            self.visit(event, lambda c: c.start(), True)

    def end(self):
        self.own(lambda c: c.wait_send())
        for event in self.events:
            self.visit(event, lambda c: c.wait_send(), False)


def spread_semaphores():
    return [
        pltpu.SemaphoreType.DMA((3, 16, 4)),
        pltpu.SemaphoreType.DMA((3, 16)),
        pltpu.SemaphoreType.DMA,
    ]


def finish_kernel(
    span,
    cached,
    block,
    limits,
    qkv,
    cache,
    early,
    shard,
    mixed,
    att,
    first,
    rest,
    away,
    back,
    send_sem,
    recv_sem,
    own_sem,
    first_sem,
    away_sem,
    back_sem,
):
    step_id = pl.program_id(0)
    steps = att.shape[0]
    me = lax.axis_index("req")
    core = lax.axis_index("tp")
    z, y, x = lax.div(me, 4), lax.rem(lax.div(me, 2), 2), lax.rem(me, 2)
    mate = (me, 1 - core)
    cut = first.shape[2]
    spread = Spread(shard.at[:, cut:], rest, send_sem, recv_sem, own_sem)
    load = pltpu.make_async_copy(early, first, first_sem)

    @pl.when(step_id == 0)
    def _():
        barrier = pltpu.get_barrier_semaphore()

        def greet(target):
            pl.semaphore_signal(
                barrier, inc=1, device_id=target, device_id_type=pl.DeviceIdType.MESH
            )

        greet((me + 1 - 2 * x, core))
        greet((me + 2 - 4 * y, core))
        greet(mate)

        @pl.when(z < 3)
        def _():
            greet((me + 4, core))

        @pl.when(z > 0)
        def _():
            greet((me - 4, core))

        inner = jnp.where(z > 0, 1, 0) + jnp.where(z < 3, 1, 0)
        pl.semaphore_wait(barrier, 3 + inner)
        spread.begin()
        load.start()

    slots = span // block * (GROUP // HD)

    def between(slot):
        for step in range(steps):

            @pl.when(step_id == step)
            def _():
                spread.step(step * slots + slot, steps * slots)

    def store(rows, columns, value):
        att[step_id, rows, columns] = value

    attend_group(
        span, cached, block, limits[0], limits[1], qkv, cache, store, between
    )

    @pl.when(step_id == steps - 1)
    def _():
        valid = limits[1]
        load.wait()
        spread.kept().wait()

        def product(pair):
            at = pl.ds(2 * pair, 2)
            value = None
            for step in range(steps):
                low = step * GROUP
                if low < cut:
                    side = first[at, :, low : low + GROUP]
                else:
                    side = rest[at, :, low - cut : low - cut + GROUP]
                term = lax.dot_general(
                    att[step],
                    side.reshape(2 * side.shape[1], GROUP),
                    (((1,), (1,)), ((), ())),
                    preferred_element_type=jnp.float32,
                )
                value = term if value is None else value + term
            return value.astype(jnp.bfloat16)

        def over(k):
            return pltpu.make_async_remote_copy(
                src_ref=away.at[k],
                dst_ref=back.at[k],
                send_sem=away_sem.at[k],
                recv_sem=back_sem.at[k],
                device_id=mate,
                device_id_type=pl.DeviceIdType.MESH,
            )

        def give(k, carry):
            away[k] = product(4 * (1 - core) + k)
            over(k).start()
            return carry

        def take(k, carry):
            value = product(4 * core + k).astype(jnp.float32)
            over(k).wait_recv()
            total = value + back[k].astype(jnp.float32)
            kept = lax.broadcasted_iota(jnp.int32, total.shape, 0) < valid
            width = total.shape[1]
            at = pl.ds(pl.multiple_of(k * width, 128), width)
            mixed[:, at] = jnp.where(kept, total, 0.0).astype(jnp.bfloat16)
            return carry

        lax.fori_loop(0, 4, give, 0)
        lax.fori_loop(0, 4, take, 0)
        for k in range(4):
            over(k).wait_send()
        spread.end()


def finish(limits, qkv, cache, early, shard):
    _, span, cols = qkv.shape
    groups = cols // GROUP
    cached = cache.shape[2]
    block = min(256, span)
    rows = shard.shape[0]
    cut = early.shape[2]
    pair = 2 * rows
    return pl.pallas_call(
        functools.partial(finish_kernel, span, cached, block),
        out_shape=jax.ShapeDtypeStruct((span, 4 * pair), jnp.bfloat16),
        grid=(groups,),
        in_specs=[
            pl.BlockSpec(memory_space=pltpu.SMEM),
            pl.BlockSpec((3, span, GROUP), lambda i: (0, 0, i)),
            pl.BlockSpec((1, 2, cached, GROUP), lambda i: (0, 0, 0, i)),
            pl.BlockSpec(memory_space=pl.ANY),
            pl.BlockSpec(memory_space=pl.ANY),
        ],
        out_specs=pl.BlockSpec((span, 4 * pair), lambda i: (0, 0)),
        scratch_shapes=[
            pltpu.VMEM((groups, span, GROUP), jnp.bfloat16),
            pltpu.VMEM((16, rows, cut), shard.dtype),
            pltpu.VMEM((16, rows, cols - cut), shard.dtype),
            pltpu.VMEM((4, span, pair), jnp.bfloat16),
            pltpu.VMEM((4, span, pair), jnp.bfloat16),
        ]
        + spread_semaphores()
        + [
            pltpu.SemaphoreType.DMA,
            pltpu.SemaphoreType.DMA((4,)),
            pltpu.SemaphoreType.DMA((4,)),
        ],
        compiler_params=pltpu.CompilerParams(
            collective_id=2, has_side_effects=True, vmem_limit_bytes=58 << 20
        ),
        name="finish",
    )(limits, qkv, cache, early, shard)


def project_grouped(tokens, norm_gain, qkv_weight, cache_lens, later):
    base_cos, base_sin, row, sign = base_tables(tokens.shape[0])
    angle = cache_lens[0].astype(jnp.float32) * row
    cosine, sine = jnp.cos(angle), jnp.sin(angle)
    turn = jnp.stack(
        [cosine, -sine, sine * sign, cosine * sign] + [jnp.zeros_like(cosine)] * 4
    )
    units = ((0, 0, GROUP), (1, 0, GROUP), (2, 0, 256), (2, 256, 128))
    return project(
        units,
        2 * GROUP,
        tokens,
        norm_gain[None, :],
        qkv_weight,
        base_cos,
        base_sin,
        turn,
        later,
    )


def project_alone(tokens, norm_gain, qkv_weight, cache_lens):
    weights = lax.all_gather(qkv_weight, "req", axis=1, tiled=True)
    gathered = lax.all_gather(tokens, "tp", axis=1, tiled=True)
    gain_all = lax.all_gather(norm_gain, "tp", axis=0, tiled=True)
    inputs = gathered.astype(jnp.float32)
    spread = jnp.mean(inputs * inputs, axis=-1, keepdims=True)
    normed = (inputs * lax.rsqrt(spread + epsilon) * gain_all.astype(jnp.float32)).astype(
        jnp.bfloat16
    )
    span = normed.shape[0]
    cols = weights.shape[2]
    projected = jnp.einsum("td,jdc->jtc", normed, weights, preferred_element_type=jnp.float32)
    positions = cache_lens[0] + jnp.arange(span, dtype=jnp.int32)
    frequencies = jnp.power(theta_base, -jnp.arange(0, HD, 2, dtype=jnp.float32) / HD)
    angles = positions.astype(jnp.float32)[:, None] * frequencies[None, :]
    cosine, sine = jnp.cos(angles)[:, None, :], jnp.sin(angles)[:, None, :]
    heads = projected[:2].reshape(2, span, cols // HD, HD)
    a, b = heads[..., : HD // 2], heads[..., HD // 2 :]
    turned = jnp.concatenate([a * cosine - b * sine, b * cosine + a * sine], axis=-1)
    qkv = jnp.concatenate([turned.reshape(2, span, cols), projected[2:]], axis=0)
    return qkv.astype(jnp.bfloat16)


def per_device(mesh, tokens, norm_gain, qkv_weight, out_weight, cache, cache_lens, valid_tokens):
    span, width = tokens.shape
    rows, cols = qkv_weight.shape[1:]
    grouped = (
        mesh.shape["req"] == 16
        and mesh.shape["tp"] == 2
        and cols == 4 * GROUP
        and width == 8 * rows
        and rows % 16 == 0
        and width % 256 == 0
        and span % 128 == 0
        and rows % 192 == 0
        and out_weight.shape == (cols, rows)
    )
    limits = jnp.concatenate([cache_lens, valid_tokens])
    kept = (jnp.arange(span, dtype=jnp.int32) < valid_tokens[0])[:, None]
    if grouped:
        later = out_weight.T
        qkv, early = project_grouped(tokens, norm_gain, qkv_weight, cache_lens, later)
        mixed_out = finish(limits, qkv, cache, early, later)
    else:
        qkv = project_alone(tokens, norm_gain, qkv_weight, cache_lens)
        out_all = lax.all_gather(out_weight.T, "req", axis=0, tiled=True)
        partial_value = lax.dot_general(
            attend(limits, qkv, cache),
            out_all,
            (((1,), (1,)), ((), ())),
            preferred_element_type=jnp.float32,
        )
        summed = lax.psum_scatter(
            partial_value.astype(jnp.bfloat16), "tp", scatter_dimension=1, tiled=True
        ).astype(jnp.float32)
        mixed_out = jnp.where(kept, summed, jnp.zeros_like(summed)).astype(jnp.bfloat16)
    new_entries = jnp.where(kept, qkv[1:], jnp.zeros_like(qkv[1:]))[None]
    return (mixed_out, new_entries)


def solution(mesh):
    placed = (
        P("req", "tp"),
        P("tp"),
        P(None, "req", "tp"),
        P("tp", "req"),
        P("req", None, None, "tp"),
        P("req"),
        P("req"),
    )
    return jax.shard_map(
        functools.partial(per_device, mesh),
        mesh=mesh,
        in_specs=placed,
        out_specs=(P("req", "tp"), P("req", None, None, "tp")),
        check_vma=False,
    )
```

```python
import functools
import math

import jax
import jax.numpy as jnp
import numpy as np
from jax import lax
from jax.experimental import pallas as pl
from jax.experimental.pallas import tpu as pltpu
from jax.sharding import PartitionSpec as P

HD = 96
GROUP = 4 * HD

epsilon = 1e-05
masked_value = -1e30
theta_base = 10000.0


def base_tables(span):
    frequencies = np.power(theta_base, -np.arange(0, HD, 2, dtype=np.float64) / HD)
    row = np.tile(frequencies.astype(np.float32), 2 * GROUP // HD)
    angles = np.arange(span, dtype=np.float64)[:, None] * row[None, :].astype(np.float64)
    sign = np.tile(np.where(np.arange(HD) < HD // 2, -1.0, 1.0), GROUP // HD).astype(np.float32)
    return (
        np.cos(angles).astype(np.float32),
        np.sin(angles).astype(np.float32),
        row,
        sign,
    )


def project_kernel(
    units,
    tok,
    gain,
    shard,
    base_cos,
    base_sin,
    turn,
    out,
    normed,
    weights,
    staged,
    turns,
    squares,
    z_send,
    w_recv,
    own_sem,
    s_send,
    n_send,
    n_recv,
    t_send,
    t_recv,
    q_send,
    q_recv,
    r_send,
    r_recv,
    keep_sem,
):
    me = lax.axis_index("req")
    core = lax.axis_index("tp")
    z, y, x = lax.div(me, 4), lax.rem(lax.div(me, 2), 2), lax.rem(me, 2)
    p = lax.rem(me, 4)
    base = me - p
    px, py, pd = p + 1 - 2 * x, p + 2 - 4 * y, 3 - p
    span, width = tok.shape
    features = 2 * width
    half = span // 2
    mate = (me, 1 - core)

    barrier = pltpu.get_barrier_semaphore()

    def greet(target):
        pl.semaphore_signal(
            barrier, inc=1, device_id=target, device_id_type=pl.DeviceIdType.MESH
        )

    for peer in (px, py, pd):
        greet((base + peer, core))
    greet(mate)

    @pl.when(z < 3)
    def _():
        greet((me + 4, core))

    @pl.when(z > 0)
    def _():
        greet((me - 4, core))

    inner = jnp.where(z > 0, 1, 0) + jnp.where(z < 3, 1, 0)
    pl.semaphore_wait(barrier, 4 + inner)

    def remote(source, target_ref, sent, received, target):
        return pltpu.make_async_remote_copy(
            src_ref=source,
            dst_ref=target_ref,
            send_sem=sent,
            recv_sem=received,
            device_id=target,
            device_id_type=pl.DeviceIdType.MESH,
        )

    def columns(unit, peer):
        part, low, count = units[unit]
        return shard.at[part, :, pl.ds(pl.multiple_of(peer * GROUP + low, 128), count)]

    def block(unit, plane, source):
        part, low, count = units[unit]
        return weights.at[part, plane, source, :, low : low + count]

    def along(unit, plane, source, up, own):
        there = block(unit, plane, source)
        return remote(
            columns(unit, p) if own else there,
            there,
            z_send.at[unit, plane, source, 0 if up else 1],
            w_recv.at[unit, plane, source],
            (me + 4 if up else me - 4, core),
        )

    def scatter(unit, lane, peer):
        return remote(
            columns(unit, peer),
            block(unit, z, p),
            s_send.at[unit, lane],
            w_recv.at[unit, z, p],
            (base + peer, core),
        )

    def keep(unit):
        return pltpu.make_async_copy(columns(unit, p), block(unit, z, p), own_sem.at[unit])

    def own_along(unit, act):
        @pl.when(z < 3)
        def _():
            act(along(unit, z, p, True, True))

        @pl.when(z > 0)
        def _():
            act(along(unit, z, p, False, True))

    def scatters(unit, act):
        for lane, peer in enumerate((pd, px, py)):
            act(scatter(unit, lane, peer))

    def onward(unit, plane, source, up, down, act):
        if up:

            @pl.when(z < 3)
            def _():
                act(along(unit, plane, source, True, False))

        if down:

            @pl.when(z > 0)
            def _():
                act(along(unit, plane, source, False, False))

    def arrivals(unit, steps, act, arrived):
        for step in steps:
            if step == 0:
                for source in (px, py, pd):
                    if arrived:
                        along(unit, z, source, True, False).wait_recv()
                    onward(unit, z, source, True, True, act)
                continue
            for delta in (-step, step):

                def body(plane=z + delta, delta=delta):
                    for source in (p, px, py, pd):
                        if arrived:
                            along(unit, plane, source, True, False).wait_recv()
                        onward(unit, plane, source, delta < 0, delta > 0, act)

                pl.when(z + delta >= 0 if delta < 0 else z + delta <= 3)(body)

    def token(source, side, part, lane, target):
        ref = normed.at[source, pl.ds(2 * side, 2), part * half : (part + 1) * half, :]
        return remote(
            ref,
            ref,
            n_send.at[source, part, lane],
            n_recv.at[source, side, part],
            target,
        )

    to_x, to_y = (base + px, core), (base + py, core)

    def token_moves(source, part, via):
        moves = [(2, mate)]
        if via == "own" or (via == "y" and part == 1):
            moves.insert(0, (0, to_x))
        if via == "own" or (via == "x" and part == 0):
            moves.insert(0, (1, to_y))
        return [token(source, core, part, lane, target) for lane, target in moves]

    def tokens(source, part, via, act, arrived):
        if arrived:
            token(source, core, part, 2, mate).wait_recv()
        for copy in token_moves(source, part, via):
            act(copy)

    def turning(lane, peer):
        return remote(
            turns.at[p], turns.at[p], t_send.at[lane], t_recv.at[p], (base + peer, core)
        )

    def home(unit, peer):
        part, low, count = units[unit]
        return remote(
            staged.at[part, peer, :, low : low + count],
            out.at[part, :, pl.ds(pl.multiple_of(p * GROUP + low, 128), count)],
            r_send.at[unit, peer],
            r_recv.at[unit, p],
            (base + peer, core),
        )

    def landed(unit, source):
        part, low, count = units[unit]
        return remote(
            staged.at[part, source, :, low : low + count],
            out.at[part, :, pl.ds(pl.multiple_of(source * GROUP + low, 128), count)],
            r_send.at[unit, source],
            r_recv.at[unit, source],
            (base + source, core),
        )

    def stay(unit):
        part, low, count = units[unit]
        return pltpu.make_async_copy(
            staged.at[part, p, :, low : low + count],
            out.at[part, :, pl.ds(pl.multiple_of(p * GROUP + low, 128), count)],
            keep_sem.at[unit],
        )

    start = lambda c: c.start()
    sent = lambda c: c.wait_send()

    own_along(0, start)
    scatters(0, start)
    for unit in range(len(units)):
        keep(unit).start()
    turns[p] = turn[...]
    for lane, peer in enumerate((px, py, pd)):
        turning(lane, peer).start()

    rows = 64

    def measure(i, carry):
        at = pl.ds(i * rows, rows)
        v = tok[at, :].astype(jnp.float32)
        total = jnp.sum(v * v, axis=1, keepdims=True)
        squares[core, at, :] = jnp.broadcast_to(total, (rows, 128))
        return carry

    lax.fori_loop(0, span // rows, measure, 0)
    share = remote(squares.at[core], squares.at[core], q_send, q_recv.at[core], mate)
    share.start()
    remote(squares.at[1 - core], squares.at[1 - core], q_send, q_recv.at[1 - core], mate).wait_recv()
    gains = gain[...].astype(jnp.float32)

    def normalize(i, carry):
        at = pl.ds(i * rows, rows)
        spread = (squares[0, at, :] + squares[1, at, :])[:, :1] * (1.0 / features)
        v = tok[at, :].astype(jnp.float32) * lax.rsqrt(spread + epsilon) * gains
        v = v.astype(jnp.bfloat16)
        normed[p, 2 * core, at, :] = v[:, : width // 2]
        normed[p, 2 * core + 1, at, :] = v[:, width // 2 :]
        return carry

    for part in range(2):
        first = part * half // rows
        lax.fori_loop(first, first + half // rows, normalize, 0)
        tokens(p, part, "own", start, False)

    def compute(unit):
        part, low, count = units[unit]
        lane_in_head = lax.broadcasted_iota(jnp.int32, (span, GROUP), 1) % HD

        def body(i, carry):
            peer = jnp.where(i == 0, pd, jnp.where(i == 1, px, jnp.where(i == 2, py, p)))
            value = None
            for plane in range(4):
                chunk = weights[part, plane, :, :, low : low + count]
                term = jnp.dot(
                    normed[peer, plane],
                    chunk.reshape(chunk.shape[0] * chunk.shape[1], count),
                    preferred_element_type=jnp.float32,
                )
                value = term if value is None else value + term
            if part < 2:
                r = turns[peer]
                cosine = r[0:1] * base_cos[...] + r[1:2] * base_sin[...]
                sine = r[2:3] * base_cos[...] + r[3:4] * base_sin[...]
                ahead = pltpu.roll(value, GROUP - HD // 2, 1)
                behind = pltpu.roll(value, HD // 2, 1)
                value = value * cosine + jnp.where(lane_in_head < HD // 2, ahead, behind) * sine
            staged[part, peer, :, low : low + count] = value.astype(jnp.bfloat16)

            @pl.when(i < 3)
            def _():
                home(unit, peer).start()

            return carry

        lax.fori_loop(0, 4, body, 0)
        stay(unit).start()

    arrivals(0, (0, 1), start, True)
    scatters(1, start)
    tokens(px, 0, "x", start, True)
    tokens(py, 0, "y", start, True)
    arrivals(0, (2,), start, True)
    own_along(1, start)
    tokens(px, 1, "x", start, True)
    tokens(py, 1, "y", start, True)
    arrivals(0, (3,), start, True)
    arrivals(1, (0, 1), start, True)
    scatters(2, start)
    tokens(pd, 0, "d", start, True)
    tokens(pd, 1, "d", start, True)
    arrivals(1, (2,), start, True)
    own_along(2, start)
    for source in (p, px, py, pd):
        for part in range(2):
            token(source, 1 - core, part, 2, mate).wait_recv()
    for peer in (px, py, pd):
        remote(turns.at[peer], turns.at[peer], t_send.at[0], t_recv.at[peer], to_x).wait_recv()
    keep(0).wait()
    compute(0)
    arrivals(1, (3,), start, True)
    keep(1).wait()
    compute(1)
    for unit in range(2, len(units)):
        if unit + 1 < len(units):
            scatters(unit + 1, start)
        arrivals(unit, (0, 1), start, True)
        arrivals(unit, (2,), start, True)
        if unit + 1 < len(units):
            own_along(unit + 1, start)
        arrivals(unit, (3,), start, True)
        keep(unit).wait()
        compute(unit)

    share.wait_send()
    for lane, peer in enumerate((px, py, pd)):
        turning(lane, peer).wait_send()
    for part in range(2):
        for source, via in ((p, "own"), (px, "x"), (py, "y"), (pd, "d")):
            tokens(source, part, via, sent, False)
    for unit in range(len(units)):
        own_along(unit, sent)
        scatters(unit, sent)
        arrivals(unit, (0, 1, 2, 3), sent, False)
        for peer in (pd, px, py):
            home(unit, peer).wait_send()
        stay(unit).wait()
        for peer in (pd, px, py):
            landed(unit, peer).wait_recv()


def project(units, tokens, gain, shard, base_cos, base_sin, turn):
    span, width = tokens.shape
    count, rows, _ = shard.shape
    n = len(units)
    dma = pltpu.SemaphoreType.DMA
    vmem = pl.BlockSpec(memory_space=pltpu.VMEM)
    hbm = pl.BlockSpec(memory_space=pl.ANY)
    return pl.pallas_call(
        functools.partial(project_kernel, units),
        out_shape=jax.ShapeDtypeStruct((count, span, 4 * GROUP), jnp.bfloat16),
        in_specs=[vmem, vmem, hbm, vmem, vmem, vmem],
        out_specs=hbm,
        scratch_shapes=[
            pltpu.VMEM((4, 4, span, width // 2), jnp.bfloat16),
            pltpu.VMEM((count, 4, 4, rows, GROUP), jnp.bfloat16),
            pltpu.VMEM((count, 4, span, GROUP), jnp.bfloat16),
            pltpu.VMEM((4, 8, GROUP), jnp.float32),
            pltpu.VMEM((2, span, 128), jnp.float32),
            dma((n, 4, 4, 2)),
            dma((n, 4, 4)),
            dma((n,)),
            dma((n, 3)),
            dma((4, 2, 3)),
            dma((4, 2, 2)),
            dma((3,)),
            dma((4,)),
            dma,
            dma((2,)),
            dma((n, 4)),
            dma((n, 4)),
            dma((n,)),
        ],
        compiler_params=pltpu.CompilerParams(
            collective_id=1, has_side_effects=True, vmem_limit_bytes=56 << 20
        ),
        cost_estimate=pl.CostEstimate(
            flops=2 * 4 * span * 2 * width * count * GROUP,
            bytes_accessed=64 << 20,
            transcendentals=0,
        ),
        name="project",
    )(tokens, gain, shard, base_cos, base_sin, turn)


def attend_group(span, cached, block, length, valid, qkv, cache, store, between):
    scale = math.log2(math.e) / math.sqrt(HD)
    cache_bias = jnp.where(
        lax.broadcasted_iota(jnp.int32, (1, cached), 1) < length, 0.0, masked_value
    )
    dims = (((1,), (1,)), ((), ()))
    for step in range(span // block):
        rows = slice(step * block, (step + 1) * block)
        seen = (step + 1) * block
        row_ids = lax.broadcasted_iota(jnp.int32, (block, seen), 0) + step * block
        col_ids = lax.broadcasted_iota(jnp.int32, (block, seen), 1)
        live = (col_ids <= row_ids) & (col_ids < valid)
        gathered = [None] * (GROUP // 128)
        for head in range(GROUP // HD):
            between(step * (GROUP // HD) + head)
            low = head * HD // 128 * 128
            high = -(-(head + 1) * HD // 128) * 128
            window = slice(low, high)
            lane = lax.broadcasted_iota(jnp.int32, (block, high - low), 1) + low
            mine = (lane >= head * HD) & (lane < (head + 1) * HD)
            query = jnp.where(mine, qkv[0, rows, window].astype(jnp.float32), 0.0).astype(
                jnp.bfloat16
            )
            old = (
                lax.dot_general(
                    query, cache[0, 0, :, window], dims, preferred_element_type=jnp.float32
                )
                * scale
                + cache_bias
            )
            new = (
                lax.dot_general(
                    query, qkv[1, :seen, window], dims, preferred_element_type=jnp.float32
                )
                * scale
            )
            new = jnp.where(live, new, masked_value)
            top = jnp.maximum(
                jnp.max(old, axis=1, keepdims=True), jnp.max(new, axis=1, keepdims=True)
            )
            old = jnp.exp2(old - top)
            new = jnp.exp2(new - top)
            total = jnp.sum(old, axis=1, keepdims=True) + jnp.sum(new, axis=1, keepdims=True)
            inverse = 1.0 / total
            result = jnp.dot(
                (old * inverse).astype(jnp.bfloat16),
                cache[0, 1, :, window],
                preferred_element_type=jnp.float32,
            ) + jnp.dot(
                (new * inverse).astype(jnp.bfloat16),
                qkv[2, :seen, window],
                preferred_element_type=jnp.float32,
            )
            result = jnp.where(mine, result, 0.0)
            for tile in range(low // 128, high // 128):
                piece = result[:, tile * 128 - low : (tile + 1) * 128 - low]
                gathered[tile] = piece if gathered[tile] is None else gathered[tile] + piece
        for tile, piece in enumerate(gathered):
            store(rows, slice(tile * 128, (tile + 1) * 128), piece.astype(jnp.bfloat16))


def attend_kernel(span, cached, block, limits, qkv, cache, att):
    def store(rows, columns, value):
        att[rows, columns] = value

    attend_group(
        span, cached, block, limits[0], limits[1], qkv, cache, store, lambda slot: None
    )


def attend(limits, qkv, cache):
    _, span, cols = qkv.shape
    groups = cols // GROUP
    cached = cache.shape[2]
    block = min(256, span)
    return pl.pallas_call(
        functools.partial(attend_kernel, span, cached, block),
        out_shape=jax.ShapeDtypeStruct((span, cols), jnp.bfloat16),
        grid=(groups,),
        in_specs=[
            pl.BlockSpec(memory_space=pltpu.SMEM),
            pl.BlockSpec((3, span, GROUP), lambda i: (0, 0, i)),
            pl.BlockSpec((1, 2, cached, GROUP), lambda i: (0, 0, 0, i)),
        ],
        out_specs=pl.BlockSpec((span, GROUP), lambda i: (0, i)),
        compiler_params=pltpu.CompilerParams(vmem_limit_bytes=48 << 20),
        name="attend",
    )(limits, qkv, cache)


def finish_kernel(
    span,
    cached,
    block,
    limits,
    qkv,
    cache,
    shard,
    mixed,
    att,
    wide,
    away,
    back,
    done,
    home,
    a_send,
    a_recv,
    w_send,
    w_recv,
    w_own,
    m_send,
    m_recv,
    h_send,
    h_recv,
):
    step_id = pl.program_id(0)
    steps = att.shape[1]
    me = lax.axis_index("req")
    core = lax.axis_index("tp")
    z, y, x = lax.div(me, 4), lax.rem(lax.div(me, 2), 2), lax.rem(me, 2)
    p = lax.rem(me, 4)
    base = me - p
    px, py, pd = p + 1 - 2 * x, p + 2 - 4 * y, 3 - p
    mate = (me, 1 - core)
    half = span // 2
    slots = span // block * (GROUP // HD)

    def remote(source, target_ref, sent, received, target):
        return pltpu.make_async_remote_copy(
            src_ref=source,
            dst_ref=target_ref,
            send_sem=sent,
            recv_sem=received,
            device_id=target,
            device_id_type=pl.DeviceIdType.MESH,
        )

    def ship(source, group, part, lane):
        ref = att.at[source, group, part * half : (part + 1) * half, :]
        return remote(
            ref,
            ref,
            a_send.at[source, group, part, lane],
            a_recv.at[source, group, part],
            (base + (px if lane == 0 else py), core),
        )

    def both(group, part, act):
        for lane in range(2):
            act(ship(p, group, part, lane))

    def from_x(group):
        ship(px, group, 0, 0).wait_recv()
        ship(px, group, 0, 1).start()

    def from_y(group):
        ship(py, group, 1, 0).wait_recv()
        ship(py, group, 1, 0).start()

    def along(plane, up, own):
        there = wide.at[plane]
        return remote(
            shard if own else there,
            there,
            w_send.at[plane, 0 if up else 1],
            w_recv.at[plane],
            (me + 4 if up else me - 4, core),
        )

    def own_along(act):
        @pl.when(z < 3)
        def _():
            act(along(z, True, True))

        @pl.when(z > 0)
        def _():
            act(along(z, False, True))

    def arrivals(distance, act, arrived):
        for delta in (-distance, distance):

            def body(plane=z + delta, delta=delta):
                if arrived:
                    along(plane, True, False).wait_recv()
                if delta < 0:

                    @pl.when(z < 3)
                    def _():
                        act(along(plane, True, False))

                else:

                    @pl.when(z > 0)
                    def _():
                        act(along(plane, False, False))

            pl.when(z + delta >= 0 if delta < 0 else z + delta <= 3)(body)

    keep = pltpu.make_async_copy(shard, wide.at[z], w_own)
    start = lambda c: c.start()
    sent = lambda c: c.wait_send()

    @pl.when(step_id == 0)
    def _():
        barrier = pltpu.get_barrier_semaphore()

        def greet(target):
            pl.semaphore_signal(
                barrier, inc=1, device_id=target, device_id_type=pl.DeviceIdType.MESH
            )

        for peer in (px, py, pd):
            greet((base + peer, core))
        greet(mate)

        @pl.when(z < 3)
        def _():
            greet((me + 4, core))

        @pl.when(z > 0)
        def _():
            greet((me - 4, core))

        inner = jnp.where(z > 0, 1, 0) + jnp.where(z < 3, 1, 0)
        pl.semaphore_wait(barrier, 4 + inner)
        own_along(start)
        keep.start()

    def between(slot):
        if slot == slots // 2:
            both(step_id, 0, start)
            pl.when(step_id == 1)(lambda: arrivals(1, start, True))
        if slot == slots - 1:
            pl.when(step_id == 2)(lambda: arrivals(2, start, True))
        if slot in (0, slots // 4, 3 * slots // 4):

            @pl.when(step_id > 0)
            def _():
                if slot == 0:
                    both(step_id - 1, 1, start)
                elif slot == slots // 4:
                    from_x(step_id - 1)
                else:
                    from_y(step_id - 1)

    def store(rows, columns, value):
        att[p, step_id, rows, columns] = value

    attend_group(
        span, cached, block, limits[0], limits[1], qkv, cache, store, between
    )

    @pl.when(step_id == steps - 1)
    def _():
        last = steps - 1
        both(last, 1, start)
        from_x(last)
        keep.wait()
        arrivals(3, start, True)

        def product(source, side):
            value = None
            for group in range(steps):
                part = wide[pl.ds(2 * side, 2), :, group * GROUP : (group + 1) * GROUP]
                term = lax.dot_general(
                    att[source, group],
                    part.reshape(2 * part.shape[1], GROUP),
                    (((1,), (1,)), ((), ())),
                    preferred_element_type=jnp.float32,
                )
                value = term if value is None else value + term
            return value.astype(jnp.bfloat16)

        def over(source):
            return remote(
                away.at[source], back.at[source], m_send.at[source], m_recv.at[source], mate
            )

        def deliver(source, lane):
            return remote(
                done.at[lane],
                home.at[p],
                h_send.at[lane],
                h_recv.at[p],
                (base + source, core),
            )

        def work(source, lane):
            away[source] = product(source, 1 - core)
            over(source).start()
            value = product(source, core).astype(jnp.float32)
            over(source).wait_recv()
            value = (value + back[source].astype(jnp.float32)).astype(jnp.bfloat16)
            if lane is None:
                home[p] = value
            else:
                done[lane] = value
                deliver(source, lane).start()

        work(p, None)
        from_y(last)
        for group in range(steps):
            ship(px, group, 1, 0).wait_recv()
        work(px, 0)
        for group in range(steps):
            ship(py, group, 0, 0).wait_recv()
        work(py, 1)
        for group in range(steps):
            for part in range(2):
                ship(pd, group, part, 0).wait_recv()
        work(pd, 2)
        kept = lax.broadcasted_iota(jnp.int32, (span, GROUP), 0) < limits[1]
        low_lanes = lax.broadcasted_iota(jnp.int32, (span, GROUP), 1) < GROUP // 2
        for peer in (px, py, pd):
            remote(
                done.at[0], home.at[peer], h_send.at[0], h_recv.at[peer], mate
            ).wait_recv()
        for pair in range(2):
            even = home[2 * pair].astype(jnp.float32)
            odd = home[2 * pair + 1].astype(jnp.float32)
            for side in range(2):
                if side == 0:
                    value = jnp.where(low_lanes, even, pltpu.roll(odd, GROUP // 2, 1))
                else:
                    value = jnp.where(low_lanes, pltpu.roll(even, GROUP // 2, 1), odd)
                at = (2 * side + pair) * GROUP
                mixed[:, at : at + GROUP] = jnp.where(kept, value, 0.0).astype(jnp.bfloat16)
        for group in range(steps):
            for part in range(2):
                both(group, part, sent)
            ship(px, group, 0, 1).wait_send()
            ship(py, group, 1, 0).wait_send()
        own_along(sent)
        for distance in (1, 2, 3):
            arrivals(distance, sent, False)
        for source in range(4):
            over(source).wait_send()
        for lane, source in enumerate((px, py, pd)):
            deliver(source, lane).wait_send()


def finish(limits, qkv, cache, shard):
    _, span, cols = qkv.shape
    groups = cols // GROUP
    cached = cache.shape[2]
    block = min(256, span)
    dma = pltpu.SemaphoreType.DMA
    plane = pltpu.VMEM((4, span, GROUP), jnp.bfloat16)
    return pl.pallas_call(
        functools.partial(finish_kernel, span, cached, block),
        out_shape=jax.ShapeDtypeStruct((span, cols), jnp.bfloat16),
        grid=(groups,),
        in_specs=[
            pl.BlockSpec(memory_space=pltpu.SMEM),
            pl.BlockSpec((3, span, GROUP), lambda i: (0, 0, i)),
            pl.BlockSpec((1, 2, cached, GROUP), lambda i: (0, 0, 0, i)),
            pl.BlockSpec(memory_space=pl.ANY),
        ],
        out_specs=pl.BlockSpec((span, cols), lambda i: (0, 0)),
        scratch_shapes=[
            pltpu.VMEM((4, groups, span, GROUP), jnp.bfloat16),
            pltpu.VMEM((4,) + shard.shape, shard.dtype),
            plane,
            plane,
            pltpu.VMEM((3, span, GROUP), jnp.bfloat16),
            plane,
            dma((4, groups, 2, 2)),
            dma((4, groups, 2)),
            dma((4, 2)),
            dma((4,)),
            dma,
            dma((4,)),
            dma((4,)),
            dma((3,)),
            dma((4,)),
        ],
        compiler_params=pltpu.CompilerParams(
            collective_id=2, has_side_effects=True, vmem_limit_bytes=58 << 20
        ),
        name="finish",
    )(limits, qkv, cache, shard)


def project_grouped(tokens, norm_gain, qkv_weight, cache_lens):
    base_cos, base_sin, row, sign = base_tables(tokens.shape[0])
    angle = cache_lens[0].astype(jnp.float32) * row
    cosine, sine = jnp.cos(angle), jnp.sin(angle)
    turn = jnp.stack(
        [cosine, -sine, sine * sign, cosine * sign] + [jnp.zeros_like(cosine)] * 4
    )
    units = ((0, 0, GROUP), (1, 0, GROUP), (2, 0, 256), (2, 256, 128))
    return project(
        units,
        tokens,
        norm_gain[None, :],
        qkv_weight,
        base_cos,
        base_sin,
        turn,
    )


def project_alone(tokens, norm_gain, qkv_weight, cache_lens):
    weights = lax.all_gather(qkv_weight, "req", axis=1, tiled=True)
    gathered = lax.all_gather(tokens, "tp", axis=1, tiled=True)
    gain_all = lax.all_gather(norm_gain, "tp", axis=0, tiled=True)
    inputs = gathered.astype(jnp.float32)
    spread = jnp.mean(inputs * inputs, axis=-1, keepdims=True)
    normed = (inputs * lax.rsqrt(spread + epsilon) * gain_all.astype(jnp.float32)).astype(
        jnp.bfloat16
    )
    span = normed.shape[0]
    cols = weights.shape[2]
    projected = jnp.einsum("td,jdc->jtc", normed, weights, preferred_element_type=jnp.float32)
    positions = cache_lens[0] + jnp.arange(span, dtype=jnp.int32)
    frequencies = jnp.power(theta_base, -jnp.arange(0, HD, 2, dtype=jnp.float32) / HD)
    angles = positions.astype(jnp.float32)[:, None] * frequencies[None, :]
    cosine, sine = jnp.cos(angles)[:, None, :], jnp.sin(angles)[:, None, :]
    heads = projected[:2].reshape(2, span, cols // HD, HD)
    a, b = heads[..., : HD // 2], heads[..., HD // 2 :]
    turned = jnp.concatenate([a * cosine - b * sine, b * cosine + a * sine], axis=-1)
    qkv = jnp.concatenate([turned.reshape(2, span, cols), projected[2:]], axis=0)
    return qkv.astype(jnp.bfloat16)


def per_device(mesh, tokens, norm_gain, qkv_weight, out_weight, cache, cache_lens, valid_tokens):
    span, width = tokens.shape
    rows, cols = qkv_weight.shape[1:]
    grouped = (
        mesh.shape["req"] == 16
        and mesh.shape["tp"] == 2
        and cols == 4 * GROUP
        and width == 8 * rows
        and rows % 16 == 0
        and width % 256 == 0
        and span % 128 == 0
        and 2 * rows == GROUP
        and out_weight.shape == (cols, rows)
    )
    limits = jnp.concatenate([cache_lens, valid_tokens])
    kept = (jnp.arange(span, dtype=jnp.int32) < valid_tokens[0])[:, None]
    if grouped:
        qkv = project_grouped(tokens, norm_gain, qkv_weight, cache_lens)
        mixed_out = finish(limits, qkv, cache, out_weight.T)
    else:
        qkv = project_alone(tokens, norm_gain, qkv_weight, cache_lens)
        out_all = lax.all_gather(out_weight.T, "req", axis=0, tiled=True)
        partial_value = lax.dot_general(
            attend(limits, qkv, cache),
            out_all,
            (((1,), (1,)), ((), ())),
            preferred_element_type=jnp.float32,
        )
        summed = lax.psum_scatter(
            partial_value.astype(jnp.bfloat16), "tp", scatter_dimension=1, tiled=True
        ).astype(jnp.float32)
        mixed_out = jnp.where(kept, summed, jnp.zeros_like(summed)).astype(jnp.bfloat16)
    new_entries = jnp.where(kept, qkv[1:], jnp.zeros_like(qkv[1:]))[None]
    return (mixed_out, new_entries)


def solution(mesh):
    placed = (
        P("req", "tp"),
        P("tp"),
        P(None, "req", "tp"),
        P("tp", "req"),
        P("req", None, None, "tp"),
        P("req"),
        P("req"),
    )
    return jax.shard_map(
        functools.partial(per_device, mesh),
        mesh=mesh,
        in_specs=placed,
        out_specs=(P("req", "tp"), P("req", None, None, "tp")),
        check_vma=False,
    )
```

```python
import functools
import math

import jax
import jax.numpy as jnp
import numpy as np
from jax import lax
from jax.experimental import pallas as pl
from jax.experimental.pallas import tpu as pltpu
from jax.sharding import PartitionSpec as P

HD = 96
GROUP = 4 * HD

epsilon = 1e-05
masked_value = -1e30
theta_base = 10000.0


def base_tables(span):
    frequencies = np.power(theta_base, -np.arange(0, HD, 2, dtype=np.float64) / HD)
    row = np.tile(frequencies.astype(np.float32), 2 * GROUP // HD)
    angles = np.arange(span, dtype=np.float64)[:, None] * row[None, :].astype(np.float64)
    sign = np.tile(np.where(np.arange(HD) < HD // 2, -1.0, 1.0), GROUP // HD).astype(np.float32)
    return (
        np.cos(angles).astype(np.float32),
        np.sin(angles).astype(np.float32),
        row,
        sign,
    )


def project_kernel(
    units,
    tok,
    gain,
    shard,
    base_cos,
    base_sin,
    turn,
    out,
    normed,
    weights,
    staged,
    turns,
    squares,
    z_send,
    w_recv,
    own_sem,
    s_send,
    n_send,
    n_recv,
    t_send,
    t_recv,
    q_send,
    q_recv,
    r_send,
    r_recv,
    keep_sem,
):
    me = lax.axis_index("req")
    core = lax.axis_index("tp")
    z, y, x = lax.div(me, 4), lax.rem(lax.div(me, 2), 2), lax.rem(me, 2)
    p = lax.rem(me, 4)
    base = me - p
    px, py, pd = p + 1 - 2 * x, p + 2 - 4 * y, 3 - p
    span, width = tok.shape
    features = 2 * width
    half = span // 2
    mate = (me, 1 - core)

    barrier = pltpu.get_barrier_semaphore()

    def greet(target):
        pl.semaphore_signal(
            barrier, inc=1, device_id=target, device_id_type=pl.DeviceIdType.MESH
        )

    for peer in (px, py, pd):
        greet((base + peer, core))
    greet(mate)

    @pl.when(z < 3)
    def _():
        greet((me + 4, core))

    @pl.when(z > 0)
    def _():
        greet((me - 4, core))

    inner = jnp.where(z > 0, 1, 0) + jnp.where(z < 3, 1, 0)
    pl.semaphore_wait(barrier, 4 + inner)

    def remote(source, target_ref, sent, received, target):
        return pltpu.make_async_remote_copy(
            src_ref=source,
            dst_ref=target_ref,
            send_sem=sent,
            recv_sem=received,
            device_id=target,
            device_id_type=pl.DeviceIdType.MESH,
        )

    def columns(unit, peer):
        part, low, count = units[unit]
        return shard.at[part, :, pl.ds(pl.multiple_of(peer * GROUP + low, 128), count)]

    def block(unit, plane, source):
        part, low, count = units[unit]
        return weights.at[part, plane, source, :, low : low + count]

    def along(unit, plane, source, up, own):
        there = block(unit, plane, source)
        return remote(
            columns(unit, p) if own else there,
            there,
            z_send.at[unit, plane, source, 0 if up else 1],
            w_recv.at[unit, plane, source],
            (me + 4 if up else me - 4, core),
        )

    def scatter(unit, lane, peer):
        return remote(
            columns(unit, peer),
            block(unit, z, p),
            s_send.at[unit, lane],
            w_recv.at[unit, z, p],
            (base + peer, core),
        )

    def keep(unit):
        return pltpu.make_async_copy(columns(unit, p), block(unit, z, p), own_sem.at[unit])

    def own_along(unit, act):
        @pl.when(z < 3)
        def _():
            act(along(unit, z, p, True, True))

        @pl.when(z > 0)
        def _():
            act(along(unit, z, p, False, True))

    def scatters(unit, act):
        for lane, peer in enumerate((pd, px, py)):
            act(scatter(unit, lane, peer))

    def onward(unit, plane, source, up, down, act):
        if up:

            @pl.when(z < 3)
            def _():
                act(along(unit, plane, source, True, False))

        if down:

            @pl.when(z > 0)
            def _():
                act(along(unit, plane, source, False, False))

    def arrivals(unit, steps, act, arrived):
        for step in steps:
            if step == 0:
                for source in (px, py, pd):
                    if arrived:
                        along(unit, z, source, True, False).wait_recv()
                    onward(unit, z, source, True, True, act)
                continue
            for delta in (-step, step):

                def body(plane=z + delta, delta=delta):
                    for source in (p, px, py, pd):
                        if arrived:
                            along(unit, plane, source, True, False).wait_recv()
                        onward(unit, plane, source, delta < 0, delta > 0, act)

                pl.when(z + delta >= 0 if delta < 0 else z + delta <= 3)(body)

    def token(source, side, part, lane, target):
        ref = normed.at[source, pl.ds(2 * side, 2), part * half : (part + 1) * half, :]
        return remote(
            ref,
            ref,
            n_send.at[source, part, lane],
            n_recv.at[source, side, part],
            target,
        )

    to_x, to_y = (base + px, core), (base + py, core)

    def token_moves(source, part, via):
        moves = [(2, mate)]
        if via == "own" or (via == "y" and part == 1):
            moves.insert(0, (0, to_x))
        if via == "own" or (via == "x" and part == 0):
            moves.insert(0, (1, to_y))
        return [token(source, core, part, lane, target) for lane, target in moves]

    def tokens(source, part, via, act, arrived):
        if arrived:
            token(source, core, part, 2, mate).wait_recv()
        for copy in token_moves(source, part, via):
            act(copy)

    def turning(lane, peer):
        return remote(
            turns.at[p], turns.at[p], t_send.at[lane], t_recv.at[p], (base + peer, core)
        )

    def home(unit, peer):
        part, low, count = units[unit]
        return remote(
            staged.at[part, peer, :, low : low + count],
            out.at[part, :, pl.ds(pl.multiple_of(p * GROUP + low, 128), count)],
            r_send.at[unit, peer],
            r_recv.at[unit, p],
            (base + peer, core),
        )

    def landed(unit, source):
        part, low, count = units[unit]
        return remote(
            staged.at[part, source, :, low : low + count],
            out.at[part, :, pl.ds(pl.multiple_of(source * GROUP + low, 128), count)],
            r_send.at[unit, source],
            r_recv.at[unit, source],
            (base + source, core),
        )

    def stay(unit):
        part, low, count = units[unit]
        return pltpu.make_async_copy(
            staged.at[part, p, :, low : low + count],
            out.at[part, :, pl.ds(pl.multiple_of(p * GROUP + low, 128), count)],
            keep_sem.at[unit],
        )

    start = lambda c: c.start()
    sent = lambda c: c.wait_send()

    own_along(0, start)
    scatters(0, start)
    for unit in range(len(units)):
        keep(unit).start()
    turns[p] = turn[...]
    for lane, peer in enumerate((px, py, pd)):
        turning(lane, peer).start()

    rows = 64

    def measure(i, carry):
        at = pl.ds(i * rows, rows)
        v = tok[at, :].astype(jnp.float32)
        total = jnp.sum(v * v, axis=1, keepdims=True)
        squares[core, at, :] = jnp.broadcast_to(total, (rows, 128))
        return carry

    lax.fori_loop(0, span // rows, measure, 0)
    share = remote(squares.at[core], squares.at[core], q_send, q_recv.at[core], mate)
    share.start()
    remote(squares.at[1 - core], squares.at[1 - core], q_send, q_recv.at[1 - core], mate).wait_recv()
    gains = gain[...].astype(jnp.float32)

    def normalize(i, carry):
        at = pl.ds(i * rows, rows)
        spread = (squares[0, at, :] + squares[1, at, :])[:, :1] * (1.0 / features)
        v = tok[at, :].astype(jnp.float32) * lax.rsqrt(spread + epsilon) * gains
        v = v.astype(jnp.bfloat16)
        normed[p, 2 * core, at, :] = v[:, : width // 2]
        normed[p, 2 * core + 1, at, :] = v[:, width // 2 :]
        return carry

    for part in range(2):
        first = part * half // rows
        lax.fori_loop(first, first + half // rows, normalize, 0)
        tokens(p, part, "own", start, False)

    def compute(unit):
        part, low, count = units[unit]
        lane_in_head = lax.broadcasted_iota(jnp.int32, (span, GROUP), 1) % HD

        def body(i, carry):
            peer = jnp.where(i == 0, pd, jnp.where(i == 1, px, jnp.where(i == 2, py, p)))
            value = None
            for plane in range(4):
                chunk = weights[part, plane, :, :, low : low + count]
                term = jnp.dot(
                    normed[peer, plane],
                    chunk.reshape(chunk.shape[0] * chunk.shape[1], count),
                    preferred_element_type=jnp.float32,
                )
                value = term if value is None else value + term
            if part < 2:
                r = turns[peer]
                cosine = r[0:1] * base_cos[...] + r[1:2] * base_sin[...]
                sine = r[2:3] * base_cos[...] + r[3:4] * base_sin[...]
                ahead = pltpu.roll(value, GROUP - HD // 2, 1)
                behind = pltpu.roll(value, HD // 2, 1)
                value = value * cosine + jnp.where(lane_in_head < HD // 2, ahead, behind) * sine
            staged[part, peer, :, low : low + count] = value.astype(jnp.bfloat16)

            @pl.when(i < 3)
            def _():
                home(unit, peer).start()

            return carry

        lax.fori_loop(0, 4, body, 0)
        stay(unit).start()

    arrivals(0, (0, 1), start, True)
    scatters(1, start)
    tokens(px, 0, "x", start, True)
    tokens(py, 0, "y", start, True)
    arrivals(0, (2,), start, True)
    own_along(1, start)
    tokens(px, 1, "x", start, True)
    tokens(py, 1, "y", start, True)
    arrivals(0, (3,), start, True)
    arrivals(1, (0, 1), start, True)
    scatters(2, start)
    tokens(pd, 0, "d", start, True)
    tokens(pd, 1, "d", start, True)
    arrivals(1, (2,), start, True)
    own_along(2, start)
    for source in (p, px, py, pd):
        for part in range(2):
            token(source, 1 - core, part, 2, mate).wait_recv()
    for peer in (px, py, pd):
        remote(turns.at[peer], turns.at[peer], t_send.at[0], t_recv.at[peer], to_x).wait_recv()
    keep(0).wait()
    compute(0)
    arrivals(1, (3,), start, True)
    keep(1).wait()
    compute(1)
    for unit in range(2, len(units)):
        if unit + 1 < len(units):
            scatters(unit + 1, start)
        arrivals(unit, (0, 1), start, True)
        arrivals(unit, (2,), start, True)
        if unit + 1 < len(units):
            own_along(unit + 1, start)
        arrivals(unit, (3,), start, True)
        keep(unit).wait()
        compute(unit)

    share.wait_send()
    for lane, peer in enumerate((px, py, pd)):
        turning(lane, peer).wait_send()
    for part in range(2):
        for source, via in ((p, "own"), (px, "x"), (py, "y"), (pd, "d")):
            tokens(source, part, via, sent, False)
    for unit in range(len(units)):
        own_along(unit, sent)
        scatters(unit, sent)
        arrivals(unit, (0, 1, 2, 3), sent, False)
        for peer in (pd, px, py):
            home(unit, peer).wait_send()
        stay(unit).wait()
        for peer in (pd, px, py):
            landed(unit, peer).wait_recv()


def project(units, tokens, gain, shard, base_cos, base_sin, turn):
    span, width = tokens.shape
    count, rows, _ = shard.shape
    n = len(units)
    dma = pltpu.SemaphoreType.DMA
    vmem = pl.BlockSpec(memory_space=pltpu.VMEM)
    hbm = pl.BlockSpec(memory_space=pl.ANY)
    return pl.pallas_call(
        functools.partial(project_kernel, units),
        out_shape=jax.ShapeDtypeStruct((count, span, 4 * GROUP), jnp.bfloat16),
        in_specs=[vmem, vmem, hbm, vmem, vmem, vmem],
        out_specs=hbm,
        scratch_shapes=[
            pltpu.VMEM((4, 4, span, width // 2), jnp.bfloat16),
            pltpu.VMEM((count, 4, 4, rows, GROUP), jnp.bfloat16),
            pltpu.VMEM((count, 4, span, GROUP), jnp.bfloat16),
            pltpu.VMEM((4, 8, GROUP), jnp.float32),
            pltpu.VMEM((2, span, 128), jnp.float32),
            dma((n, 4, 4, 2)),
            dma((n, 4, 4)),
            dma((n,)),
            dma((n, 3)),
            dma((4, 2, 3)),
            dma((4, 2, 2)),
            dma((3,)),
            dma((4,)),
            dma,
            dma((2,)),
            dma((n, 4)),
            dma((n, 4)),
            dma((n,)),
        ],
        compiler_params=pltpu.CompilerParams(
            collective_id=1, has_side_effects=True, vmem_limit_bytes=56 << 20
        ),
        cost_estimate=pl.CostEstimate(
            flops=2 * 4 * span * 2 * width * count * GROUP,
            bytes_accessed=64 << 20,
            transcendentals=0,
        ),
        name="project",
    )(tokens, gain, shard, base_cos, base_sin, turn)


def attend_group(span, cached, block, length, valid, qkv, cache, store, between):
    scale = math.log2(math.e) / math.sqrt(HD)
    cache_bias = jnp.where(
        lax.broadcasted_iota(jnp.int32, (1, cached), 1) < length, 0.0, masked_value
    )
    dims = (((1,), (1,)), ((), ()))
    for step in range(span // block):
        rows = slice(step * block, (step + 1) * block)
        seen = (step + 1) * block
        row_ids = lax.broadcasted_iota(jnp.int32, (block, seen), 0) + step * block
        col_ids = lax.broadcasted_iota(jnp.int32, (block, seen), 1)
        live = (col_ids <= row_ids) & (col_ids < valid)
        gathered = [None] * (GROUP // 128)
        for head in range(GROUP // HD):
            between(step * (GROUP // HD) + head)
            low = head * HD // 128 * 128
            high = -(-(head + 1) * HD // 128) * 128
            window = slice(low, high)
            lane = lax.broadcasted_iota(jnp.int32, (block, high - low), 1) + low
            mine = (lane >= head * HD) & (lane < (head + 1) * HD)
            query = jnp.where(mine, qkv[0, rows, window].astype(jnp.float32), 0.0).astype(
                jnp.bfloat16
            )
            old = (
                lax.dot_general(
                    query, cache[0, 0, :, window], dims, preferred_element_type=jnp.float32
                )
                * scale
                + cache_bias
            )
            new = (
                lax.dot_general(
                    query, qkv[1, :seen, window], dims, preferred_element_type=jnp.float32
                )
                * scale
            )
            new = jnp.where(live, new, masked_value)
            top = jnp.maximum(
                jnp.max(old, axis=1, keepdims=True), jnp.max(new, axis=1, keepdims=True)
            )
            old = jnp.exp2(old - top)
            new = jnp.exp2(new - top)
            total = jnp.sum(old, axis=1, keepdims=True) + jnp.sum(new, axis=1, keepdims=True)
            inverse = 1.0 / total
            result = jnp.dot(
                (old * inverse).astype(jnp.bfloat16),
                cache[0, 1, :, window],
                preferred_element_type=jnp.float32,
            ) + jnp.dot(
                (new * inverse).astype(jnp.bfloat16),
                qkv[2, :seen, window],
                preferred_element_type=jnp.float32,
            )
            result = jnp.where(mine, result, 0.0)
            for tile in range(low // 128, high // 128):
                piece = result[:, tile * 128 - low : (tile + 1) * 128 - low]
                gathered[tile] = piece if gathered[tile] is None else gathered[tile] + piece
        for tile, piece in enumerate(gathered):
            store(rows, slice(tile * 128, (tile + 1) * 128), piece.astype(jnp.bfloat16))


def attend_kernel(span, cached, block, limits, qkv, cache, att):
    def store(rows, columns, value):
        att[rows, columns] = value

    attend_group(
        span, cached, block, limits[0], limits[1], qkv, cache, store, lambda slot: None
    )


def attend(limits, qkv, cache):
    _, span, cols = qkv.shape
    groups = cols // GROUP
    cached = cache.shape[2]
    block = min(256, span)
    return pl.pallas_call(
        functools.partial(attend_kernel, span, cached, block),
        out_shape=jax.ShapeDtypeStruct((span, cols), jnp.bfloat16),
        grid=(groups,),
        in_specs=[
            pl.BlockSpec(memory_space=pltpu.SMEM),
            pl.BlockSpec((3, span, GROUP), lambda i: (0, 0, i)),
            pl.BlockSpec((1, 2, cached, GROUP), lambda i: (0, 0, 0, i)),
        ],
        out_specs=pl.BlockSpec((span, GROUP), lambda i: (0, i)),
        compiler_params=pltpu.CompilerParams(vmem_limit_bytes=48 << 20),
        name="attend",
    )(limits, qkv, cache)


def finish_kernel(
    span,
    cached,
    block,
    limits,
    qkv,
    cache,
    shard,
    mixed,
    att,
    wide,
    term,
    back,
    done,
    home,
    a_send,
    a_recv,
    z_send,
    z_recv,
    y_send,
    y_recv,
    w_own,
    m_send,
    m_recv,
    h_send,
    h_recv,
):
    step_id = pl.program_id(0)
    steps = att.shape[1]
    me = lax.axis_index("req")
    core = lax.axis_index("tp")
    z, y, x = lax.div(me, 4), lax.rem(lax.div(me, 2), 2), lax.rem(me, 2)
    to_x, to_y, mate = (me + 1 - 2 * x, core), (me + 2 - 4 * y, core), (me, 1 - core)
    half = span // 2
    slots = span // block * (GROUP // HD)

    def remote(source, target_ref, sent, received, target):
        return pltpu.make_async_remote_copy(
            src_ref=source,
            dst_ref=target_ref,
            send_sem=sent,
            recv_sem=received,
            device_id=target,
            device_id_type=pl.DeviceIdType.MESH,
        )

    def ship(side, group, part):
        ref = att.at[side, group, part * half : (part + 1) * half, :]
        return remote(ref, ref, a_send.at[group, part], a_recv.at[group, part], to_x)

    def along(plane, up, own):
        there = wide.at[plane, y]
        return remote(
            shard if own else there,
            there,
            z_send.at[plane, 0 if up else 1],
            z_recv.at[plane],
            (me + 4 if up else me - 4, core),
        )

    def across(plane, own):
        there = wide.at[plane, y]
        return remote(
            shard if own else there, there, y_send.at[plane], y_recv.at[plane], to_y
        )

    def crossed(plane):
        there = wide.at[plane, 1 - y]
        return remote(there, there, y_send.at[plane], y_recv.at[plane], to_y)

    def own_along(act):
        @pl.when(z < 3)
        def _():
            act(along(z, True, True))

        @pl.when(z > 0)
        def _():
            act(along(z, False, True))

        act(across(z, True))

    def arrivals(distance, act, arrived):
        for delta in (-distance, distance):

            def body(plane=z + delta, delta=delta):
                if arrived:
                    along(plane, True, False).wait_recv()
                if delta < 0:

                    @pl.when(z < 3)
                    def _():
                        act(along(plane, True, False))

                else:

                    @pl.when(z > 0)
                    def _():
                        act(along(plane, False, False))

                act(across(plane, False))

            pl.when(z + delta >= 0 if delta < 0 else z + delta <= 3)(body)

    keep = pltpu.make_async_copy(shard, wide.at[z, y], w_own)
    start = lambda c: c.start()
    sent = lambda c: c.wait_send()

    @pl.when(step_id == 0)
    def _():
        barrier = pltpu.get_barrier_semaphore()

        def greet(target):
            pl.semaphore_signal(
                barrier, inc=1, device_id=target, device_id_type=pl.DeviceIdType.MESH
            )

        greet(to_x)
        greet(to_y)
        greet(mate)

        @pl.when(z < 3)
        def _():
            greet((me + 4, core))

        @pl.when(z > 0)
        def _():
            greet((me - 4, core))

        inner = jnp.where(z > 0, 1, 0) + jnp.where(z < 3, 1, 0)
        pl.semaphore_wait(barrier, 3 + inner)
        own_along(start)
        keep.start()

    schedule = {(1, 3 * slots // 8): 1, (2, 5 * slots // 8): 2, (3, 6 * slots // 8): 3}

    def between(slot):
        if slot == slots // 2:
            ship(x, step_id, 0).start()
        if slot == 0:

            @pl.when(step_id > 0)
            def _():
                ship(x, step_id - 1, 1).start()

        for (step, at), distance in schedule.items():
            if at == slot:
                pl.when(step_id == step)(lambda d=distance: arrivals(d, start, True))

    def store(rows, columns, value):
        att[x, step_id, rows, columns] = value

    attend_group(
        span, cached, block, limits[0], limits[1], qkv, cache, store, between
    )

    @pl.when(step_id == steps - 1)
    def _():
        ship(x, steps - 1, 1).start()
        keep.wait()

        def product(side, plane):
            value = None
            for group in range(steps):
                part = wide[plane, :, :, group * GROUP : (group + 1) * GROUP]
                one = lax.dot_general(
                    att[side, group],
                    part.reshape(2 * part.shape[1], GROUP),
                    (((1,), (1,)), ((), ())),
                    preferred_element_type=jnp.float32,
                )
                value = one if value is None else value + one
            return value.astype(jnp.bfloat16)

        def over(side, plane):
            return remote(
                term.at[side, plane],
                back.at[side, lax.rem(plane, 2)],
                m_send.at[side, lax.rem(plane, 2)],
                m_recv.at[side, lax.rem(plane, 2)],
                mate,
            )

        def deliver(rel):
            return remote(
                done.at[rel], home.at[x, rel], h_send.at[rel], h_recv.at[rel], to_x
            )

        def total(side, plane, rel):
            over(side, plane).wait_recv()
            return (
                term[side, plane].astype(jnp.float32) + back[side, rel].astype(jnp.float32)
            ).astype(jnp.bfloat16)

        def body(k, carry):
            near = jnp.where(z < 2, 1 - z, 5 - z)
            third = jnp.where(z < 2, 2, 1)
            fourth = jnp.where(z < 2, 3, 0)
            plane = jnp.where(
                k == 0, z, jnp.where(k == 1, near, jnp.where(k == 2, third, fourth))
            )
            rel = lax.rem(plane, 2)
            mine = lax.div(plane, 2) == core
            crossed(plane).wait_recv()
            for side in (1 - x, x):
                term[side, plane] = product(side, plane)

                @pl.when(jnp.logical_not(mine))
                def _():
                    over(side, plane).start()

            @pl.when(mine)
            def _():
                done[rel] = total(1 - x, plane, rel)
                deliver(rel).start()
                home[x, rel] = total(x, plane, rel)

            return carry

        for group in range(steps):
            for part in range(2):
                ship(1 - x, group, part).wait_recv()
        lax.fori_loop(0, 4, body, 0)
        kept = lax.broadcasted_iota(jnp.int32, (span, GROUP), 0) < limits[1]
        low_lanes = lax.broadcasted_iota(jnp.int32, (span, GROUP), 1) < GROUP // 2
        for rel in range(2):
            remote(
                done.at[rel], home.at[1 - x, rel], h_send.at[rel], h_recv.at[rel], to_x
            ).wait_recv()
        for rel in range(2):
            even = home[0, rel].astype(jnp.float32)
            odd = home[1, rel].astype(jnp.float32)
            for side in range(2):
                if side == 0:
                    value = jnp.where(low_lanes, even, pltpu.roll(odd, GROUP // 2, 1))
                else:
                    value = jnp.where(low_lanes, pltpu.roll(even, GROUP // 2, 1), odd)
                at = (2 * rel + side) * GROUP
                mixed[:, at : at + GROUP] = jnp.where(kept, value, 0.0).astype(jnp.bfloat16)
        for group in range(steps):
            for part in range(2):
                ship(x, group, part).wait_send()
        own_along(sent)
        for distance in (1, 2, 3):
            arrivals(distance, sent, False)
        for rel in range(2):
            for side in range(2):
                over(side, 2 * (1 - core) + rel).wait_send()
            deliver(rel).wait_send()


def finish(limits, qkv, cache, shard):
    _, span, cols = qkv.shape
    groups = cols // GROUP
    cached = cache.shape[2]
    block = min(256, span)
    dma = pltpu.SemaphoreType.DMA
    return pl.pallas_call(
        functools.partial(finish_kernel, span, cached, block),
        out_shape=jax.ShapeDtypeStruct((span, cols), jnp.bfloat16),
        grid=(groups,),
        in_specs=[
            pl.BlockSpec(memory_space=pltpu.SMEM),
            pl.BlockSpec((3, span, GROUP), lambda i: (0, 0, i)),
            pl.BlockSpec((1, 2, cached, GROUP), lambda i: (0, 0, 0, i)),
            pl.BlockSpec(memory_space=pl.ANY),
        ],
        out_specs=pl.BlockSpec((span, cols), lambda i: (0, 0)),
        scratch_shapes=[
            pltpu.VMEM((2, groups, span, GROUP), jnp.bfloat16),
            pltpu.VMEM((4, 2) + shard.shape, shard.dtype),
            pltpu.VMEM((2, 4, span, GROUP), jnp.bfloat16),
            pltpu.VMEM((2, 2, span, GROUP), jnp.bfloat16),
            pltpu.VMEM((2, span, GROUP), jnp.bfloat16),
            pltpu.VMEM((2, 2, span, GROUP), jnp.bfloat16),
            dma((groups, 2)),
            dma((groups, 2)),
            dma((4, 2)),
            dma((4,)),
            dma((4,)),
            dma((4,)),
            dma,
            dma((2, 2)),
            dma((2, 2)),
            dma((2,)),
            dma((2,)),
        ],
        compiler_params=pltpu.CompilerParams(
            collective_id=2, has_side_effects=True, vmem_limit_bytes=58 << 20
        ),
        name="finish",
    )(limits, qkv, cache, shard)


def project_grouped(tokens, norm_gain, qkv_weight, cache_lens):
    base_cos, base_sin, row, sign = base_tables(tokens.shape[0])
    angle = cache_lens[0].astype(jnp.float32) * row
    cosine, sine = jnp.cos(angle), jnp.sin(angle)
    turn = jnp.stack(
        [cosine, -sine, sine * sign, cosine * sign] + [jnp.zeros_like(cosine)] * 4
    )
    units = ((0, 0, GROUP), (1, 0, GROUP), (2, 0, 256), (2, 256, 128))
    return project(
        units,
        tokens,
        norm_gain[None, :],
        qkv_weight,
        base_cos,
        base_sin,
        turn,
    )


def project_alone(tokens, norm_gain, qkv_weight, cache_lens):
    weights = lax.all_gather(qkv_weight, "req", axis=1, tiled=True)
    gathered = lax.all_gather(tokens, "tp", axis=1, tiled=True)
    gain_all = lax.all_gather(norm_gain, "tp", axis=0, tiled=True)
    inputs = gathered.astype(jnp.float32)
    spread = jnp.mean(inputs * inputs, axis=-1, keepdims=True)
    normed = (inputs * lax.rsqrt(spread + epsilon) * gain_all.astype(jnp.float32)).astype(
        jnp.bfloat16
    )
    span = normed.shape[0]
    cols = weights.shape[2]
    projected = jnp.einsum("td,jdc->jtc", normed, weights, preferred_element_type=jnp.float32)
    positions = cache_lens[0] + jnp.arange(span, dtype=jnp.int32)
    frequencies = jnp.power(theta_base, -jnp.arange(0, HD, 2, dtype=jnp.float32) / HD)
    angles = positions.astype(jnp.float32)[:, None] * frequencies[None, :]
    cosine, sine = jnp.cos(angles)[:, None, :], jnp.sin(angles)[:, None, :]
    heads = projected[:2].reshape(2, span, cols // HD, HD)
    a, b = heads[..., : HD // 2], heads[..., HD // 2 :]
    turned = jnp.concatenate([a * cosine - b * sine, b * cosine + a * sine], axis=-1)
    qkv = jnp.concatenate([turned.reshape(2, span, cols), projected[2:]], axis=0)
    return qkv.astype(jnp.bfloat16)


def per_device(mesh, tokens, norm_gain, qkv_weight, out_weight, cache, cache_lens, valid_tokens):
    span, width = tokens.shape
    rows, cols = qkv_weight.shape[1:]
    grouped = (
        mesh.shape["req"] == 16
        and mesh.shape["tp"] == 2
        and cols == 4 * GROUP
        and width == 8 * rows
        and rows % 16 == 0
        and width % 256 == 0
        and span % 128 == 0
        and 2 * rows == GROUP
        and out_weight.shape == (cols, rows)
    )
    limits = jnp.concatenate([cache_lens, valid_tokens])
    kept = (jnp.arange(span, dtype=jnp.int32) < valid_tokens[0])[:, None]
    if grouped:
        qkv = project_grouped(tokens, norm_gain, qkv_weight, cache_lens)
        mixed_out = finish(limits, qkv, cache, out_weight.T)
    else:
        qkv = project_alone(tokens, norm_gain, qkv_weight, cache_lens)
        out_all = lax.all_gather(out_weight.T, "req", axis=0, tiled=True)
        partial_value = lax.dot_general(
            attend(limits, qkv, cache),
            out_all,
            (((1,), (1,)), ((), ())),
            preferred_element_type=jnp.float32,
        )
        summed = lax.psum_scatter(
            partial_value.astype(jnp.bfloat16), "tp", scatter_dimension=1, tiled=True
        ).astype(jnp.float32)
        mixed_out = jnp.where(kept, summed, jnp.zeros_like(summed)).astype(jnp.bfloat16)
    new_entries = jnp.where(kept, qkv[1:], jnp.zeros_like(qkv[1:]))[None]
    return (mixed_out, new_entries)


def solution(mesh):
    placed = (
        P("req", "tp"),
        P("tp"),
        P(None, "req", "tp"),
        P("tp", "req"),
        P("req", None, None, "tp"),
        P("req"),
        P("req"),
    )
    return jax.shard_map(
        functools.partial(per_device, mesh),
        mesh=mesh,
        in_specs=placed,
        out_specs=(P("req", "tp"), P("req", None, None, "tp")),
        check_vma=False,
    )
```

```python
import functools
import math

import jax
import jax.numpy as jnp
import numpy as np
from jax import lax
from jax.experimental import pallas as pl
from jax.experimental.pallas import tpu as pltpu
from jax.sharding import PartitionSpec as P

HD = 96
GROUP = 4 * HD

epsilon = 1e-05
masked_value = -1e30
theta_base = 10000.0


def base_tables(span):
    frequencies = np.power(theta_base, -np.arange(0, HD, 2, dtype=np.float64) / HD)
    row = np.tile(frequencies.astype(np.float32), 2 * GROUP // HD)
    angles = np.arange(span, dtype=np.float64)[:, None] * row[None, :].astype(np.float64)
    sign = np.tile(np.where(np.arange(HD) < HD // 2, -1.0, 1.0), GROUP // HD).astype(np.float32)
    return (
        np.cos(angles).astype(np.float32),
        np.sin(angles).astype(np.float32),
        row,
        sign,
    )


def project_kernel(
    units,
    tok,
    gain,
    shard,
    base_cos,
    base_sin,
    row,
    lens,
    out,
    normed,
    weights,
    staged,
    turns,
    squares,
    z_send,
    w_recv,
    own_sem,
    s_send,
    n_send,
    n_recv,
    t_send,
    t_recv,
    q_send,
    q_recv,
    r_send,
    r_recv,
    keep_sem,
):
    me = lax.axis_index("req")
    core = lax.axis_index("tp")
    z, y, x = lax.div(me, 4), lax.rem(lax.div(me, 2), 2), lax.rem(me, 2)
    p = lax.rem(me, 4)
    base = me - p
    px, py, pd = p + 1 - 2 * x, p + 2 - 4 * y, 3 - p
    span, width = tok.shape
    features = 2 * width
    half = span // 2
    mate = (me, 1 - core)

    barrier = pltpu.get_barrier_semaphore()

    def greet(target):
        pl.semaphore_signal(
            barrier, inc=1, device_id=target, device_id_type=pl.DeviceIdType.MESH
        )

    for peer in (px, py, pd):
        greet((base + peer, core))
    greet(mate)

    @pl.when(z < 3)
    def _():
        greet((me + 4, core))

    @pl.when(z > 0)
    def _():
        greet((me - 4, core))

    inner = jnp.where(z > 0, 1, 0) + jnp.where(z < 3, 1, 0)
    pl.semaphore_wait(barrier, 4 + inner)

    def remote(source, target_ref, sent, received, target):
        return pltpu.make_async_remote_copy(
            src_ref=source,
            dst_ref=target_ref,
            send_sem=sent,
            recv_sem=received,
            device_id=target,
            device_id_type=pl.DeviceIdType.MESH,
        )

    def columns(unit, peer):
        part, low, count = units[unit]
        return shard.at[part, :, pl.ds(pl.multiple_of(peer * GROUP + low, 128), count)]

    def block(unit, plane, source):
        part, low, count = units[unit]
        return weights.at[part, plane, source, :, low : low + count]

    def along(unit, plane, source, up, own):
        there = block(unit, plane, source)
        return remote(
            columns(unit, p) if own else there,
            there,
            z_send.at[unit, plane, source, 0 if up else 1],
            w_recv.at[unit, plane, source],
            (me + 4 if up else me - 4, core),
        )

    def scatter(unit, lane, peer):
        return remote(
            columns(unit, peer),
            block(unit, z, p),
            s_send.at[unit, lane],
            w_recv.at[unit, z, p],
            (base + peer, core),
        )

    def keep(unit):
        return pltpu.make_async_copy(columns(unit, p), block(unit, z, p), own_sem.at[unit])

    def own_along(unit, act):
        @pl.when(z < 3)
        def _():
            act(along(unit, z, p, True, True))

        @pl.when(z > 0)
        def _():
            act(along(unit, z, p, False, True))

    def scatters(unit, act):
        for lane, peer in enumerate((pd, px, py)):
            act(scatter(unit, lane, peer))

    def onward(unit, plane, source, up, down, act):
        if up:

            @pl.when(z < 3)
            def _():
                act(along(unit, plane, source, True, False))

        if down:

            @pl.when(z > 0)
            def _():
                act(along(unit, plane, source, False, False))

    def arrivals(unit, steps, act, arrived):
        for step in steps:
            if step == 0:
                for source in (px, py, pd):
                    if arrived:
                        along(unit, z, source, True, False).wait_recv()
                    onward(unit, z, source, True, True, act)
                continue
            for delta in (-step, step):

                def body(plane=z + delta, delta=delta):
                    for source in (p, px, py, pd):
                        if arrived:
                            along(unit, plane, source, True, False).wait_recv()
                        onward(unit, plane, source, delta < 0, delta > 0, act)

                pl.when(z + delta >= 0 if delta < 0 else z + delta <= 3)(body)

    def token(source, side, part, lane, target):
        ref = normed.at[source, pl.ds(2 * side, 2), part * half : (part + 1) * half, :]
        return remote(
            ref,
            ref,
            n_send.at[source, part, lane],
            n_recv.at[source, side, part],
            target,
        )

    to_x, to_y = (base + px, core), (base + py, core)

    def token_moves(source, part, via):
        moves = [(2, mate)]
        if via == "own" or (via == "y" and part == 1):
            moves.insert(0, (0, to_x))
        if via == "own" or (via == "x" and part == 0):
            moves.insert(0, (1, to_y))
        return [token(source, core, part, lane, target) for lane, target in moves]

    def tokens(source, part, via, act, arrived):
        if arrived:
            token(source, core, part, 2, mate).wait_recv()
        for copy in token_moves(source, part, via):
            act(copy)

    def turning(lane, peer):
        return remote(
            turns.at[p], turns.at[p], t_send.at[lane], t_recv.at[p], (base + peer, core)
        )

    def home(unit, peer):
        part, low, count = units[unit]
        return remote(
            staged.at[part, peer, :, low : low + count],
            out.at[part, :, pl.ds(pl.multiple_of(p * GROUP + low, 128), count)],
            r_send.at[unit, peer],
            r_recv.at[unit, p],
            (base + peer, core),
        )

    def landed(unit, source):
        part, low, count = units[unit]
        return remote(
            staged.at[part, source, :, low : low + count],
            out.at[part, :, pl.ds(pl.multiple_of(source * GROUP + low, 128), count)],
            r_send.at[unit, source],
            r_recv.at[unit, source],
            (base + source, core),
        )

    def stay(unit):
        part, low, count = units[unit]
        return pltpu.make_async_copy(
            staged.at[part, p, :, low : low + count],
            out.at[part, :, pl.ds(pl.multiple_of(p * GROUP + low, 128), count)],
            keep_sem.at[unit],
        )

    start = lambda c: c.start()
    sent = lambda c: c.wait_send()

    own_along(0, start)
    scatters(0, start)
    for unit in range(len(units)):
        keep(unit).start()
    angle = lens[0].astype(jnp.float32) * row[...]
    turned = (jnp.cos(angle[0:1]), jnp.sin(angle[0:1]))
    sign = row[1:2]
    turns[p] = jnp.concatenate(
        [
            turned[0],
            -turned[1],
            turned[1] * sign,
            turned[0] * sign,
            jnp.zeros((4, GROUP), jnp.float32),
        ]
    )
    for lane, peer in enumerate((px, py, pd)):
        turning(lane, peer).start()

    rows = 64

    def measure(i, carry):
        at = pl.ds(i * rows, rows)
        v = tok[at, :].astype(jnp.float32)
        total = jnp.sum(v * v, axis=1, keepdims=True)
        squares[core, at, :] = jnp.broadcast_to(total, (rows, 128))
        return carry

    lax.fori_loop(0, span // rows, measure, 0)
    share = remote(squares.at[core], squares.at[core], q_send, q_recv.at[core], mate)
    share.start()
    remote(squares.at[1 - core], squares.at[1 - core], q_send, q_recv.at[1 - core], mate).wait_recv()
    gains = gain[...].astype(jnp.float32).reshape(1, width)

    def normalize(i, carry):
        at = pl.ds(i * rows, rows)
        spread = (squares[0, at, :] + squares[1, at, :])[:, :1] * (1.0 / features)
        v = tok[at, :].astype(jnp.float32) * lax.rsqrt(spread + epsilon) * gains
        v = v.astype(jnp.bfloat16)
        normed[p, 2 * core, at, :] = v[:, : width // 2]
        normed[p, 2 * core + 1, at, :] = v[:, width // 2 :]
        return carry

    for part in range(2):
        first = part * half // rows
        lax.fori_loop(first, first + half // rows, normalize, 0)
        tokens(p, part, "own", start, False)

    def compute(unit, begin, end):
        part, low, count = units[unit]
        lane_in_head = lax.broadcasted_iota(jnp.int32, (span, GROUP), 1) % HD

        def body(i, carry):
            peer = jnp.where(i == 0, pd, jnp.where(i == 1, px, jnp.where(i == 2, py, p)))
            value = None
            for plane in range(4):
                chunk = weights[part, plane, :, :, low : low + count]
                term = jnp.dot(
                    normed[peer, plane],
                    chunk.reshape(chunk.shape[0] * chunk.shape[1], count),
                    preferred_element_type=jnp.float32,
                )
                value = term if value is None else value + term
            if part < 2:
                r = turns[peer]
                cosine = r[0:1] * base_cos[...] + r[1:2] * base_sin[...]
                sine = r[2:3] * base_cos[...] + r[3:4] * base_sin[...]
                ahead = pltpu.roll(value, GROUP - HD // 2, 1)
                behind = pltpu.roll(value, HD // 2, 1)
                value = value * cosine + jnp.where(lane_in_head < HD // 2, ahead, behind) * sine
            staged[part, peer, :, low : low + count] = value.astype(jnp.bfloat16)

            @pl.when(i < 3)
            def _():
                home(unit, peer).start()

            return carry

        lax.fori_loop(begin, end, body, 0)
        if end == 4:
            stay(unit).start()

    def mates(sources):
        for source in sources:
            for part in range(2):
                token(source, 1 - core, part, 2, mate).wait_recv()

    arrivals(0, (0, 1), start, True)
    scatters(1, start)
    arrivals(0, (2,), start, True)
    own_along(1, start)
    arrivals(0, (3,), start, True)
    tokens(px, 0, "x", start, True)
    tokens(py, 0, "y", start, True)
    tokens(px, 1, "x", start, True)
    tokens(py, 1, "y", start, True)
    arrivals(1, (0, 1), start, True)
    scatters(2, start)
    arrivals(1, (2,), start, True)
    own_along(2, start)
    tokens(pd, 0, "d", start, True)
    tokens(pd, 1, "d", start, True)
    for peer in (px, py, pd):
        remote(turns.at[peer], turns.at[peer], t_send.at[0], t_recv.at[peer], to_x).wait_recv()
    mates((p, px, py, pd))
    keep(0).wait()
    compute(0, 0, 2)
    arrivals(1, (3,), start, True)
    compute(0, 2, 4)
    arrivals(2, (0, 1), start, True)
    scatters(3, start)
    keep(1).wait()
    compute(1, 0, 2)
    arrivals(2, (2,), start, True)
    own_along(3, start)
    compute(1, 2, 4)
    arrivals(2, (3,), start, True)
    arrivals(3, (0, 1), start, True)
    keep(2).wait()
    compute(2, 0, 2)
    arrivals(3, (2,), start, True)
    compute(2, 2, 4)
    arrivals(3, (3,), start, True)
    keep(3).wait()
    compute(3, 0, 4)

    share.wait_send()
    for lane, peer in enumerate((px, py, pd)):
        turning(lane, peer).wait_send()
    for part in range(2):
        for source, via in ((p, "own"), (px, "x"), (py, "y"), (pd, "d")):
            tokens(source, part, via, sent, False)
    for unit in range(len(units)):
        own_along(unit, sent)
        scatters(unit, sent)
        arrivals(unit, (0, 1, 2, 3), sent, False)
        for peer in (pd, px, py):
            home(unit, peer).wait_send()
        stay(unit).wait()
        for peer in (pd, px, py):
            landed(unit, peer).wait_recv()


def project(units, tokens, gain, shard, base_cos, base_sin, row, lens):
    span, width = tokens.shape
    count, rows, _ = shard.shape
    n = len(units)
    dma = pltpu.SemaphoreType.DMA
    vmem = pl.BlockSpec(memory_space=pltpu.VMEM)
    hbm = pl.BlockSpec(memory_space=pl.ANY)
    smem = pl.BlockSpec(memory_space=pltpu.SMEM)
    return pl.pallas_call(
        functools.partial(project_kernel, units),
        out_shape=jax.ShapeDtypeStruct((count, span, 4 * GROUP), jnp.bfloat16),
        in_specs=[vmem, vmem, hbm, vmem, vmem, vmem, smem],
        out_specs=hbm,
        scratch_shapes=[
            pltpu.VMEM((4, 4, span, width // 2), jnp.bfloat16),
            pltpu.VMEM((count, 4, 4, rows, GROUP), jnp.bfloat16),
            pltpu.VMEM((count, 4, span, GROUP), jnp.bfloat16),
            pltpu.VMEM((4, 8, GROUP), jnp.float32),
            pltpu.VMEM((2, span, 128), jnp.float32),
            dma((n, 4, 4, 2)),
            dma((n, 4, 4)),
            dma((n,)),
            dma((n, 3)),
            dma((4, 2, 3)),
            dma((4, 2, 2)),
            dma((3,)),
            dma((4,)),
            dma,
            dma((2,)),
            dma((n, 4)),
            dma((n, 4)),
            dma((n,)),
        ],
        compiler_params=pltpu.CompilerParams(
            collective_id=1, has_side_effects=True, vmem_limit_bytes=56 << 20
        ),
        cost_estimate=pl.CostEstimate(
            flops=2 * 4 * span * 2 * width * count * GROUP,
            bytes_accessed=64 << 20,
            transcendentals=0,
        ),
        name="project",
    )(tokens, gain, shard, base_cos, base_sin, row, lens)


def attend_group(span, cached, block, length, valid, qkv, cache, store, between):
    scale = math.log2(math.e) / math.sqrt(HD)
    cache_bias = jnp.where(
        lax.broadcasted_iota(jnp.int32, (1, cached), 1) < length, 0.0, masked_value
    )
    dims = (((1,), (1,)), ((), ()))
    for step in range(span // block):
        rows = slice(step * block, (step + 1) * block)
        seen = (step + 1) * block
        row_ids = lax.broadcasted_iota(jnp.int32, (block, seen), 0) + step * block
        col_ids = lax.broadcasted_iota(jnp.int32, (block, seen), 1)
        live = (col_ids <= row_ids) & (col_ids < valid)
        gathered = [None] * (GROUP // 128)
        for head in range(GROUP // HD):
            between(step * (GROUP // HD) + head)
            low = head * HD // 128 * 128
            high = -(-(head + 1) * HD // 128) * 128
            window = slice(low, high)
            lane = lax.broadcasted_iota(jnp.int32, (block, high - low), 1) + low
            mine = (lane >= head * HD) & (lane < (head + 1) * HD)
            query = jnp.where(mine, qkv[0, rows, window].astype(jnp.float32), 0.0).astype(
                jnp.bfloat16
            )
            old = (
                lax.dot_general(
                    query, cache[0, 0, :, window], dims, preferred_element_type=jnp.float32
                )
                * scale
                + cache_bias
            )
            new = (
                lax.dot_general(
                    query, qkv[1, :seen, window], dims, preferred_element_type=jnp.float32
                )
                * scale
            )
            new = jnp.where(live, new, masked_value)
            top = jnp.maximum(
                jnp.max(old, axis=1, keepdims=True), jnp.max(new, axis=1, keepdims=True)
            )
            old = jnp.exp2(old - top)
            new = jnp.exp2(new - top)
            total = jnp.sum(old, axis=1, keepdims=True) + jnp.sum(new, axis=1, keepdims=True)
            inverse = 1.0 / total
            result = jnp.dot(
                (old * inverse).astype(jnp.bfloat16),
                cache[0, 1, :, window],
                preferred_element_type=jnp.float32,
            ) + jnp.dot(
                (new * inverse).astype(jnp.bfloat16),
                qkv[2, :seen, window],
                preferred_element_type=jnp.float32,
            )
            result = jnp.where(mine, result, 0.0)
            for tile in range(low // 128, high // 128):
                piece = result[:, tile * 128 - low : (tile + 1) * 128 - low]
                gathered[tile] = piece if gathered[tile] is None else gathered[tile] + piece
        for tile, piece in enumerate(gathered):
            store(rows, slice(tile * 128, (tile + 1) * 128), piece.astype(jnp.bfloat16))


def attend_kernel(span, cached, block, limits, qkv, cache, att):
    def store(rows, columns, value):
        att[rows, columns] = value

    attend_group(
        span, cached, block, limits[0], limits[1], qkv, cache, store, lambda slot: None
    )


def attend(limits, qkv, cache):
    _, span, cols = qkv.shape
    groups = cols // GROUP
    cached = cache.shape[2]
    block = min(256, span)
    return pl.pallas_call(
        functools.partial(attend_kernel, span, cached, block),
        out_shape=jax.ShapeDtypeStruct((span, cols), jnp.bfloat16),
        grid=(groups,),
        in_specs=[
            pl.BlockSpec(memory_space=pltpu.SMEM),
            pl.BlockSpec((3, span, GROUP), lambda i: (0, 0, i)),
            pl.BlockSpec((1, 2, cached, GROUP), lambda i: (0, 0, 0, i)),
        ],
        out_specs=pl.BlockSpec((span, GROUP), lambda i: (0, i)),
        compiler_params=pltpu.CompilerParams(vmem_limit_bytes=48 << 20),
        name="attend",
    )(limits, qkv, cache)


def finish_kernel(
    span,
    cached,
    block,
    limits,
    qkv,
    cache,
    shard,
    mixed,
    att,
    wide,
    term,
    back,
    done,
    home,
    a_send,
    a_recv,
    z_send,
    z_recv,
    y_send,
    y_recv,
    w_own,
    m_send,
    m_recv,
    h_send,
    h_recv,
):
    step_id = pl.program_id(0)
    steps = att.shape[1]
    me = lax.axis_index("req")
    core = lax.axis_index("tp")
    z, y, x = lax.div(me, 4), lax.rem(lax.div(me, 2), 2), lax.rem(me, 2)
    to_x, to_y, mate = (me + 1 - 2 * x, core), (me + 2 - 4 * y, core), (me, 1 - core)
    half = span // 2
    slots = span // block * (GROUP // HD)

    def remote(source, target_ref, sent, received, target):
        return pltpu.make_async_remote_copy(
            src_ref=source,
            dst_ref=target_ref,
            send_sem=sent,
            recv_sem=received,
            device_id=target,
            device_id_type=pl.DeviceIdType.MESH,
        )

    def ship(side, group, part):
        ref = att.at[side, group, part * half : (part + 1) * half, :]
        return remote(ref, ref, a_send.at[group, part], a_recv.at[group, part], to_x)

    def along(plane, up, own):
        there = wide.at[plane, y]
        return remote(
            shard if own else there,
            there,
            z_send.at[plane, 0 if up else 1],
            z_recv.at[plane],
            (me + 4 if up else me - 4, core),
        )

    def across(plane, own):
        there = wide.at[plane, y]
        return remote(
            shard if own else there, there, y_send.at[plane], y_recv.at[plane], to_y
        )

    def crossed(plane):
        there = wide.at[plane, 1 - y]
        return remote(there, there, y_send.at[plane], y_recv.at[plane], to_y)

    def own_along(act):
        @pl.when(z < 3)
        def _():
            act(along(z, True, True))

        @pl.when(z > 0)
        def _():
            act(along(z, False, True))

        act(across(z, True))

    def arrivals(distance, act, arrived):
        for delta in (-distance, distance):

            def body(plane=z + delta, delta=delta):
                if arrived:
                    along(plane, True, False).wait_recv()
                if delta < 0:

                    @pl.when(z < 3)
                    def _():
                        act(along(plane, True, False))

                else:

                    @pl.when(z > 0)
                    def _():
                        act(along(plane, False, False))

                act(across(plane, False))

            pl.when(z + delta >= 0 if delta < 0 else z + delta <= 3)(body)

    keep = pltpu.make_async_copy(shard, wide.at[z, y], w_own)
    start = lambda c: c.start()
    sent = lambda c: c.wait_send()

    @pl.when(step_id == 0)
    def _():
        barrier = pltpu.get_barrier_semaphore()

        def greet(target):
            pl.semaphore_signal(
                barrier, inc=1, device_id=target, device_id_type=pl.DeviceIdType.MESH
            )

        greet(to_x)
        greet(to_y)
        greet(mate)

        @pl.when(z < 3)
        def _():
            greet((me + 4, core))

        @pl.when(z > 0)
        def _():
            greet((me - 4, core))

        inner = jnp.where(z > 0, 1, 0) + jnp.where(z < 3, 1, 0)
        pl.semaphore_wait(barrier, 3 + inner)
        own_along(start)
        keep.start()

    schedule = {(1, 3 * slots // 8): 1, (2, 5 * slots // 8): 2, (3, 6 * slots // 8): 3}

    def between(slot):
        if slot == slots // 2:
            ship(x, step_id, 0).start()
        if slot == 0:

            @pl.when(step_id > 0)
            def _():
                ship(x, step_id - 1, 1).start()

        for (step, at), distance in schedule.items():
            if at == slot:
                pl.when(step_id == step)(lambda d=distance: arrivals(d, start, True))

    def store(rows, columns, value):
        att[x, step_id, rows, columns] = value

    attend_group(
        span, cached, block, limits[0], limits[1], qkv, cache, store, between
    )

    @pl.when(step_id == steps - 1)
    def _():
        ship(x, steps - 1, 1).start()
        keep.wait()

        def product(side, plane):
            value = None
            for group in range(steps):
                part = wide[plane, :, :, group * GROUP : (group + 1) * GROUP]
                one = lax.dot_general(
                    att[side, group],
                    part.reshape(2 * part.shape[1], GROUP),
                    (((1,), (1,)), ((), ())),
                    preferred_element_type=jnp.float32,
                )
                value = one if value is None else value + one
            return value.astype(jnp.bfloat16)

        def over(side, plane):
            return remote(
                term.at[side, plane],
                back.at[side, lax.rem(plane, 2)],
                m_send.at[side, lax.rem(plane, 2)],
                m_recv.at[side, lax.rem(plane, 2)],
                mate,
            )

        def deliver(rel):
            return remote(
                done.at[rel], home.at[x, rel], h_send.at[rel], h_recv.at[rel], to_x
            )

        def total(side, plane, rel):
            over(side, plane).wait_recv()
            return (
                term[side, plane].astype(jnp.float32) + back[side, rel].astype(jnp.float32)
            ).astype(jnp.bfloat16)

        def nearest(k):
            near = jnp.where(z < 2, 1 - z, 5 - z)
            third = jnp.where(z < 2, 2, 1)
            fourth = jnp.where(z < 2, 3, 0)
            plane = jnp.where(
                k == 0, z, jnp.where(k == 1, near, jnp.where(k == 2, third, fourth))
            )
            return plane, lax.rem(plane, 2), lax.div(plane, 2) == core

        def make(side, plane, mine):
            term[side, plane] = product(side, plane)

            @pl.when(jnp.logical_not(mine))
            def _():
                over(side, plane).start()

        def send_home(plane, rel, mine):
            @pl.when(mine)
            def _():
                done[rel] = total(1 - x, plane, rel)
                deliver(rel).start()

        def own_rows(k, carry):
            plane, _, mine = nearest(k)
            crossed(plane).wait_recv()
            make(x, plane, mine)
            return carry

        def other_rows(k, carry):
            plane, rel, mine = nearest(k)
            make(1 - x, plane, mine)
            send_home(plane, rel, mine)
            return carry

        lax.fori_loop(0, 3, own_rows, 0)
        for group in range(steps):
            for part in range(2):
                ship(1 - x, group, part).wait_recv()
        lax.fori_loop(0, 3, other_rows, 0)
        plane, rel, mine = nearest(3)
        crossed(plane).wait_recv()
        make(1 - x, plane, mine)
        make(x, plane, mine)
        send_home(plane, rel, mine)
        for rel in range(2):
            home[x, rel] = total(x, 2 * core + rel, rel)
        kept = lax.broadcasted_iota(jnp.int32, (span, GROUP), 0) < limits[1]
        low_lanes = lax.broadcasted_iota(jnp.int32, (span, GROUP), 1) < GROUP // 2
        for rel in range(2):
            remote(
                done.at[rel], home.at[1 - x, rel], h_send.at[rel], h_recv.at[rel], to_x
            ).wait_recv()
        for rel in range(2):
            even = home[0, rel].astype(jnp.float32)
            odd = home[1, rel].astype(jnp.float32)
            for side in range(2):
                if side == 0:
                    value = jnp.where(low_lanes, even, pltpu.roll(odd, GROUP // 2, 1))
                else:
                    value = jnp.where(low_lanes, pltpu.roll(even, GROUP // 2, 1), odd)
                at = (2 * rel + side) * GROUP
                mixed[:, at : at + GROUP] = jnp.where(kept, value, 0.0).astype(jnp.bfloat16)
        for group in range(steps):
            for part in range(2):
                ship(x, group, part).wait_send()
        own_along(sent)
        for distance in (1, 2, 3):
            arrivals(distance, sent, False)
        for rel in range(2):
            for side in range(2):
                over(side, 2 * (1 - core) + rel).wait_send()
            deliver(rel).wait_send()


def finish(limits, qkv, cache, shard):
    _, span, cols = qkv.shape
    groups = cols // GROUP
    cached = cache.shape[2]
    block = min(256, span)
    dma = pltpu.SemaphoreType.DMA
    return pl.pallas_call(
        functools.partial(finish_kernel, span, cached, block),
        out_shape=jax.ShapeDtypeStruct((span, cols), jnp.bfloat16),
        grid=(groups,),
        in_specs=[
            pl.BlockSpec(memory_space=pltpu.SMEM),
            pl.BlockSpec((3, span, GROUP), lambda i: (0, 0, i)),
            pl.BlockSpec((1, 2, cached, GROUP), lambda i: (0, 0, 0, i)),
            pl.BlockSpec(memory_space=pl.ANY),
        ],
        out_specs=pl.BlockSpec((span, cols), lambda i: (0, 0)),
        scratch_shapes=[
            pltpu.VMEM((2, groups, span, GROUP), jnp.bfloat16),
            pltpu.VMEM((4, 2) + shard.shape, shard.dtype),
            pltpu.VMEM((2, 4, span, GROUP), jnp.bfloat16),
            pltpu.VMEM((2, 2, span, GROUP), jnp.bfloat16),
            pltpu.VMEM((2, span, GROUP), jnp.bfloat16),
            pltpu.VMEM((2, 2, span, GROUP), jnp.bfloat16),
            dma((groups, 2)),
            dma((groups, 2)),
            dma((4, 2)),
            dma((4,)),
            dma((4,)),
            dma((4,)),
            dma,
            dma((2, 2)),
            dma((2, 2)),
            dma((2,)),
            dma((2,)),
        ],
        compiler_params=pltpu.CompilerParams(
            collective_id=2, has_side_effects=True, vmem_limit_bytes=58 << 20
        ),
        name="finish",
    )(limits, qkv, cache, shard)


def project_grouped(tokens, norm_gain, qkv_weight, cache_lens):
    base_cos, base_sin, row, sign = base_tables(tokens.shape[0])
    rows = np.concatenate([row[None], sign[None], np.zeros((6, GROUP), np.float32)])
    units = ((0, 0, GROUP), (1, 0, GROUP), (2, 0, 256), (2, 256, 128))
    return project(units, tokens, norm_gain, qkv_weight, base_cos, base_sin, rows, cache_lens)


def project_alone(tokens, norm_gain, qkv_weight, cache_lens):
    weights = lax.all_gather(qkv_weight, "req", axis=1, tiled=True)
    gathered = lax.all_gather(tokens, "tp", axis=1, tiled=True)
    gain_all = lax.all_gather(norm_gain, "tp", axis=0, tiled=True)
    inputs = gathered.astype(jnp.float32)
    spread = jnp.mean(inputs * inputs, axis=-1, keepdims=True)
    normed = (inputs * lax.rsqrt(spread + epsilon) * gain_all.astype(jnp.float32)).astype(
        jnp.bfloat16
    )
    span = normed.shape[0]
    cols = weights.shape[2]
    projected = jnp.einsum("td,jdc->jtc", normed, weights, preferred_element_type=jnp.float32)
    positions = cache_lens[0] + jnp.arange(span, dtype=jnp.int32)
    frequencies = jnp.power(theta_base, -jnp.arange(0, HD, 2, dtype=jnp.float32) / HD)
    angles = positions.astype(jnp.float32)[:, None] * frequencies[None, :]
    cosine, sine = jnp.cos(angles)[:, None, :], jnp.sin(angles)[:, None, :]
    heads = projected[:2].reshape(2, span, cols // HD, HD)
    a, b = heads[..., : HD // 2], heads[..., HD // 2 :]
    turned = jnp.concatenate([a * cosine - b * sine, b * cosine + a * sine], axis=-1)
    qkv = jnp.concatenate([turned.reshape(2, span, cols), projected[2:]], axis=0)
    return qkv.astype(jnp.bfloat16)


def per_device(mesh, tokens, norm_gain, qkv_weight, out_weight, cache, cache_lens, valid_tokens):
    span, width = tokens.shape
    rows, cols = qkv_weight.shape[1:]
    grouped = (
        mesh.shape["req"] == 16
        and mesh.shape["tp"] == 2
        and cols == 4 * GROUP
        and width == 8 * rows
        and rows % 16 == 0
        and width % 256 == 0
        and span % 128 == 0
        and 2 * rows == GROUP
        and out_weight.shape == (cols, rows)
    )
    limits = jnp.concatenate([cache_lens, valid_tokens])
    kept = (jnp.arange(span, dtype=jnp.int32) < valid_tokens[0])[:, None]
    if grouped:
        qkv = project_grouped(tokens, norm_gain, qkv_weight, cache_lens)
        mixed_out = finish(limits, qkv, cache, out_weight.T)
    else:
        qkv = project_alone(tokens, norm_gain, qkv_weight, cache_lens)
        out_all = lax.all_gather(out_weight.T, "req", axis=0, tiled=True)
        partial_value = lax.dot_general(
            attend(limits, qkv, cache),
            out_all,
            (((1,), (1,)), ((), ())),
            preferred_element_type=jnp.float32,
        )
        summed = lax.psum_scatter(
            partial_value.astype(jnp.bfloat16), "tp", scatter_dimension=1, tiled=True
        ).astype(jnp.float32)
        mixed_out = jnp.where(kept, summed, jnp.zeros_like(summed)).astype(jnp.bfloat16)
    new_entries = jnp.where(kept, qkv[1:], jnp.zeros_like(qkv[1:]))[None]
    return (mixed_out, new_entries)


def solution(mesh):
    placed = (
        P("req", "tp"),
        P("tp"),
        P(None, "req", "tp"),
        P("tp", "req"),
        P("req", None, None, "tp"),
        P("req"),
        P("req"),
    )
    return jax.shard_map(
        functools.partial(per_device, mesh),
        mesh=mesh,
        in_specs=placed,
        out_specs=(P("req", "tp"), P("req", None, None, "tp")),
        check_vma=False,
    )
```

```python
import functools
import math

import jax
import jax.numpy as jnp
import numpy as np
from jax import lax
from jax.experimental import pallas as pl
from jax.experimental.pallas import tpu as pltpu
from jax.sharding import PartitionSpec as P

HD = 96
GROUP = 4 * HD

epsilon = 1e-05
masked_value = -1e30
theta_base = 10000.0


def base_tables(span):
    frequencies = np.power(theta_base, -np.arange(0, HD, 2, dtype=np.float64) / HD)
    row = np.tile(frequencies.astype(np.float32), 2 * GROUP // HD)
    angles = np.arange(span, dtype=np.float64)[:, None] * row[None, :].astype(np.float64)
    sign = np.tile(np.where(np.arange(HD) < HD // 2, -1.0, 1.0), GROUP // HD).astype(np.float32)
    return (
        np.cos(angles).astype(np.float32),
        np.sin(angles).astype(np.float32),
        row,
        sign,
    )


def project_kernel(
    units,
    tok_in,
    gain,
    shard,
    base_in,
    row,
    lens,
    out,
    tok,
    base,
    near_terms,
    normed,
    weights,
    staged,
    turns,
    squares,
    z_send,
    w_recv,
    own_sem,
    s_send,
    n_send,
    n_recv,
    t_send,
    t_recv,
    q_send,
    q_recv,
    r_send,
    r_recv,
    keep_sem,
    load_sem,
):
    me = lax.axis_index("req")
    core = lax.axis_index("tp")
    z, y, x = lax.div(me, 4), lax.rem(lax.div(me, 2), 2), lax.rem(me, 2)
    p = lax.rem(me, 4)
    first_id = me - p
    px, py, pd = p + 1 - 2 * x, p + 2 - 4 * y, 3 - p
    span, width = tok.shape
    features = 2 * width
    half = span // 2
    mate = (me, 1 - core)

    barrier = pltpu.get_barrier_semaphore()

    def greet(target):
        pl.semaphore_signal(
            barrier, inc=1, device_id=target, device_id_type=pl.DeviceIdType.MESH
        )

    for peer in (px, py, pd):
        greet((first_id + peer, core))
    greet(mate)

    @pl.when(z < 3)
    def _():
        greet((me + 4, core))

    @pl.when(z > 0)
    def _():
        greet((me - 4, core))

    inner = jnp.where(z > 0, 1, 0) + jnp.where(z < 3, 1, 0)
    pl.semaphore_wait(barrier, 4 + inner)

    def remote(source, target_ref, sent, received, target):
        return pltpu.make_async_remote_copy(
            src_ref=source,
            dst_ref=target_ref,
            send_sem=sent,
            recv_sem=received,
            device_id=target,
            device_id_type=pl.DeviceIdType.MESH,
        )

    def columns(unit, peer):
        part, low, count = units[unit]
        return shard.at[part, :, pl.ds(pl.multiple_of(peer * GROUP + low, 128), count)]

    def block(unit, plane, source):
        part, low, count = units[unit]
        return weights.at[part, plane, source, :, low : low + count]

    def along(unit, plane, source, up, own):
        there = block(unit, plane, source)
        return remote(
            columns(unit, p) if own else there,
            there,
            z_send.at[unit, plane, source, 0 if up else 1],
            w_recv.at[unit, plane, source],
            (me + 4 if up else me - 4, core),
        )

    def scatter(unit, lane, peer):
        return remote(
            columns(unit, peer),
            block(unit, z, p),
            s_send.at[unit, lane],
            w_recv.at[unit, z, p],
            (first_id + peer, core),
        )

    def keep(unit):
        return pltpu.make_async_copy(columns(unit, p), block(unit, z, p), own_sem.at[unit])

    def own_along(unit, act):
        @pl.when(z < 3)
        def _():
            act(along(unit, z, p, True, True))

        @pl.when(z > 0)
        def _():
            act(along(unit, z, p, False, True))

    def scatters(unit, act):
        for lane, peer in enumerate((pd, px, py)):
            act(scatter(unit, lane, peer))

    def onward(unit, plane, source, up, down, act):
        if up:

            @pl.when(z < 3)
            def _():
                act(along(unit, plane, source, True, False))

        if down:

            @pl.when(z > 0)
            def _():
                act(along(unit, plane, source, False, False))

    def arrivals(unit, steps, act, arrived):
        for step in steps:
            if step == 0:
                for source in (px, py, pd):
                    if arrived:
                        along(unit, z, source, True, False).wait_recv()
                    onward(unit, z, source, True, True, act)
                continue
            for delta in (-step, step):

                def body(plane=z + delta, delta=delta):
                    for source in (p, px, py, pd):
                        if arrived:
                            along(unit, plane, source, True, False).wait_recv()
                        onward(unit, plane, source, delta < 0, delta > 0, act)

                pl.when(z + delta >= 0 if delta < 0 else z + delta <= 3)(body)

    def token(source, side, part, lane, target):
        ref = normed.at[source, pl.ds(2 * side, 2), part * half : (part + 1) * half, :]
        return remote(
            ref,
            ref,
            n_send.at[source, part, lane],
            n_recv.at[source, side, part],
            target,
        )

    to_x, to_y = (first_id + px, core), (first_id + py, core)

    def token_moves(source, part, via):
        moves = [(2, mate)]
        if via == "own" or (via == "y" and part == 1):
            moves.insert(0, (0, to_x))
        if via == "own" or (via == "x" and part == 0):
            moves.insert(0, (1, to_y))
        return [token(source, core, part, lane, target) for lane, target in moves]

    def tokens(source, part, via, act, arrived):
        if arrived:
            token(source, core, part, 2, mate).wait_recv()
        for copy in token_moves(source, part, via):
            act(copy)

    def turning(lane, peer):
        return remote(
            turns.at[p], turns.at[p], t_send.at[lane], t_recv.at[p], (first_id + peer, core)
        )

    def home(unit, peer):
        part, low, count = units[unit]
        return remote(
            staged.at[part, peer, :, low : low + count],
            out.at[part, :, pl.ds(pl.multiple_of(p * GROUP + low, 128), count)],
            r_send.at[unit, peer],
            r_recv.at[unit, p],
            (first_id + peer, core),
        )

    def landed(unit, source):
        part, low, count = units[unit]
        return remote(
            staged.at[part, source, :, low : low + count],
            out.at[part, :, pl.ds(pl.multiple_of(source * GROUP + low, 128), count)],
            r_send.at[unit, source],
            r_recv.at[unit, source],
            (first_id + source, core),
        )

    def stay(unit):
        part, low, count = units[unit]
        return pltpu.make_async_copy(
            staged.at[part, p, :, low : low + count],
            out.at[part, :, pl.ds(pl.multiple_of(p * GROUP + low, 128), count)],
            keep_sem.at[unit],
        )

    start = lambda c: c.start()
    sent = lambda c: c.wait_send()

    own_along(0, start)
    scatters(0, start)
    load_tok = pltpu.make_async_copy(tok_in, tok, load_sem.at[0])
    load_tok.start()
    load_base = pltpu.make_async_copy(base_in, base, load_sem.at[1])
    load_base.start()
    for unit in range(len(units)):
        keep(unit).start()
    angle = lens[0].astype(jnp.float32) * row[...]
    turned = (jnp.cos(angle[0:1]), jnp.sin(angle[0:1]))
    sign = row[1:2]
    turns[p] = jnp.concatenate(
        [
            turned[0],
            -turned[1],
            turned[1] * sign,
            turned[0] * sign,
            jnp.zeros((4, GROUP), jnp.float32),
        ]
    )
    for lane, peer in enumerate((px, py, pd)):
        turning(lane, peer).start()

    rows = 64

    def measure(i, carry):
        at = pl.ds(i * rows, rows)
        v = tok[at, :].astype(jnp.float32)
        total = jnp.sum(v * v, axis=1, keepdims=True)
        squares[core, at, :] = jnp.broadcast_to(total, (rows, 128))
        return carry

    load_tok.wait()
    lax.fori_loop(0, span // rows, measure, 0)
    share = remote(squares.at[core], squares.at[core], q_send, q_recv.at[core], mate)
    share.start()
    remote(squares.at[1 - core], squares.at[1 - core], q_send, q_recv.at[1 - core], mate).wait_recv()
    gains = gain[...].astype(jnp.float32).reshape(1, width)

    def normalize(i, carry):
        at = pl.ds(i * rows, rows)
        spread = (squares[0, at, :] + squares[1, at, :])[:, :1] * (1.0 / features)
        v = tok[at, :].astype(jnp.float32) * lax.rsqrt(spread + epsilon) * gains
        v = v.astype(jnp.bfloat16)
        normed[p, 2 * core, at, :] = v[:, : width // 2]
        normed[p, 2 * core + 1, at, :] = v[:, width // 2 :]
        return carry

    for part in range(2):
        first = part * half // rows
        lax.fori_loop(first, first + half // rows, normalize, 0)
        tokens(p, part, "own", start, False)

    def terms(unit, peer, planes):
        part, low, count = units[unit]
        value = None
        for plane in planes:
            chunk = weights[part, plane, :, :, low : low + count]
            term = jnp.dot(
                normed[peer, plane],
                chunk.reshape(chunk.shape[0] * chunk.shape[1], count),
                preferred_element_type=jnp.float32,
            )
            value = term if value is None else value + term
        return value

    def by_distance():
        near = jnp.where(z < 2, 1 - z, 5 - z)
        return [z, near, jnp.where(z < 2, 2, 1), jnp.where(z < 2, 3, 0)]

    def peer_of(i):
        return jnp.where(i == 0, pd, jnp.where(i == 1, px, jnp.where(i == 2, py, p)))

    def compute_near(unit):
        def body(i, carry):
            near_terms[i] = terms(unit, peer_of(i), by_distance()[:3])
            return carry

        lax.fori_loop(0, 4, body, 0)

    def compute_far(unit):
        part, low, count = units[unit]

        def body(i, carry):
            peer = peer_of(i)
            value = near_terms[i] + terms(unit, peer, by_distance()[3:])
            staged[part, peer, :, low : low + count] = value.astype(jnp.bfloat16)

            @pl.when(i < 3)
            def _():
                home(unit, peer).start()

            return carry

        lax.fori_loop(0, 4, body, 0)
        stay(unit).start()

    def compute(unit, begin, end):
        part, low, count = units[unit]
        lane_in_head = lax.broadcasted_iota(jnp.int32, (span, GROUP), 1) % HD

        def body(i, carry):
            peer = peer_of(i)
            value = terms(unit, peer, range(4))
            if part < 2:
                r = turns[peer]
                cosine = r[0:1] * base[0] + r[1:2] * base[1]
                sine = r[2:3] * base[0] + r[3:4] * base[1]
                ahead = pltpu.roll(value, GROUP - HD // 2, 1)
                behind = pltpu.roll(value, HD // 2, 1)
                value = value * cosine + jnp.where(lane_in_head < HD // 2, ahead, behind) * sine
            staged[part, peer, :, low : low + count] = value.astype(jnp.bfloat16)

            @pl.when(i < 3)
            def _():
                home(unit, peer).start()

            return carry

        lax.fori_loop(begin, end, body, 0)
        if end == 4:
            stay(unit).start()

    def mates(sources):
        for source in sources:
            for part in range(2):
                token(source, 1 - core, part, 2, mate).wait_recv()

    arrivals(0, (0, 1), start, True)
    scatters(1, start)
    arrivals(0, (2,), start, True)
    own_along(1, start)
    arrivals(0, (3,), start, True)
    tokens(px, 0, "x", start, True)
    tokens(py, 0, "y", start, True)
    tokens(px, 1, "x", start, True)
    tokens(py, 1, "y", start, True)
    arrivals(1, (0, 1), start, True)
    scatters(2, start)
    arrivals(1, (2,), start, True)
    own_along(2, start)
    tokens(pd, 0, "d", start, True)
    tokens(pd, 1, "d", start, True)
    for peer in (px, py, pd):
        remote(turns.at[peer], turns.at[peer], t_send.at[0], t_recv.at[peer], to_x).wait_recv()
    mates((p, px, py, pd))
    load_base.wait()
    keep(0).wait()
    compute(0, 0, 2)
    arrivals(1, (3,), start, True)
    compute(0, 2, 4)
    arrivals(2, (0, 1), start, True)
    scatters(3, start)
    keep(1).wait()
    compute(1, 0, 2)
    arrivals(2, (2,), start, True)
    own_along(3, start)
    compute(1, 2, 4)
    arrivals(2, (3,), start, True)
    arrivals(3, (0, 1), start, True)
    keep(2).wait()
    compute(2, 0, 2)
    arrivals(3, (2,), start, True)
    compute(2, 2, 4)
    keep(3).wait()
    compute_near(3)
    arrivals(3, (3,), start, True)
    compute_far(3)

    share.wait_send()
    for lane, peer in enumerate((px, py, pd)):
        turning(lane, peer).wait_send()
    for part in range(2):
        for source, via in ((p, "own"), (px, "x"), (py, "y"), (pd, "d")):
            tokens(source, part, via, sent, False)
    for unit in range(len(units)):
        own_along(unit, sent)
        scatters(unit, sent)
        arrivals(unit, (0, 1, 2, 3), sent, False)
        for peer in (pd, px, py):
            home(unit, peer).wait_send()
        stay(unit).wait()
        for peer in (pd, px, py):
            landed(unit, peer).wait_recv()


def project(units, tokens, gain, shard, base, row, lens):
    span, width = tokens.shape
    count, rows, _ = shard.shape
    n = len(units)
    dma = pltpu.SemaphoreType.DMA
    vmem = pl.BlockSpec(memory_space=pltpu.VMEM)
    hbm = pl.BlockSpec(memory_space=pl.ANY)
    smem = pl.BlockSpec(memory_space=pltpu.SMEM)
    return pl.pallas_call(
        functools.partial(project_kernel, units),
        out_shape=jax.ShapeDtypeStruct((count, span, 4 * GROUP), jnp.bfloat16),
        in_specs=[hbm, vmem, hbm, hbm, vmem, smem],
        out_specs=hbm,
        scratch_shapes=[
            pltpu.VMEM((span, width), jnp.bfloat16),
            pltpu.VMEM((2, span, GROUP), jnp.float32),
            pltpu.VMEM((4, span, units[-1][2]), jnp.float32),
            pltpu.VMEM((4, 4, span, width // 2), jnp.bfloat16),
            pltpu.VMEM((count, 4, 4, rows, GROUP), jnp.bfloat16),
            pltpu.VMEM((count, 4, span, GROUP), jnp.bfloat16),
            pltpu.VMEM((4, 8, GROUP), jnp.float32),
            pltpu.VMEM((2, span, 128), jnp.float32),
            dma((n, 4, 4, 2)),
            dma((n, 4, 4)),
            dma((n,)),
            dma((n, 3)),
            dma((4, 2, 3)),
            dma((4, 2, 2)),
            dma((3,)),
            dma((4,)),
            dma,
            dma((2,)),
            dma((n, 4)),
            dma((n, 4)),
            dma((n,)),
            dma((2,)),
        ],
        compiler_params=pltpu.CompilerParams(
            collective_id=1, has_side_effects=True, vmem_limit_bytes=56 << 20
        ),
        cost_estimate=pl.CostEstimate(
            flops=2 * 4 * span * 2 * width * count * GROUP,
            bytes_accessed=64 << 20,
            transcendentals=0,
        ),
        name="project",
    )(tokens, gain, shard, base, row, lens)


def attend_group(span, cached, block, length, valid, qkv, cache, store, between):
    scale = math.log2(math.e) / math.sqrt(HD)
    cache_bias = jnp.where(
        lax.broadcasted_iota(jnp.int32, (1, cached), 1) < length, 0.0, masked_value
    )
    dims = (((1,), (1,)), ((), ()))
    for step in range(span // block):
        rows = slice(step * block, (step + 1) * block)
        seen = (step + 1) * block
        row_ids = lax.broadcasted_iota(jnp.int32, (block, seen), 0) + step * block
        col_ids = lax.broadcasted_iota(jnp.int32, (block, seen), 1)
        live = (col_ids <= row_ids) & (col_ids < valid)
        gathered = [None] * (GROUP // 128)

        def scores(head):
            low = head * HD // 128 * 128
            high = -(-(head + 1) * HD // 128) * 128
            window = slice(low, high)
            lane = lax.broadcasted_iota(jnp.int32, (block, high - low), 1) + low
            mine = (lane >= head * HD) & (lane < (head + 1) * HD)
            query = jnp.where(mine, qkv[0, rows, window].astype(jnp.float32), 0.0).astype(
                jnp.bfloat16
            )
            old = lax.dot_general(
                query, cache[0, 0, :, window], dims, preferred_element_type=jnp.float32
            )
            new = lax.dot_general(
                query, qkv[1, :seen, window], dims, preferred_element_type=jnp.float32
            )
            return low, high, window, mine, old, new

        ahead = scores(0)
        for head in range(GROUP // HD):
            between(step * (GROUP // HD) + head)
            low, high, window, mine, old, new = ahead
            if head + 1 < GROUP // HD:
                ahead = scores(head + 1)
            old = old * scale + cache_bias
            new = jnp.where(live, new * scale, masked_value)
            top = jnp.maximum(
                jnp.max(old, axis=1, keepdims=True), jnp.max(new, axis=1, keepdims=True)
            )
            old = jnp.exp2(old - top)
            new = jnp.exp2(new - top)
            total = jnp.sum(old, axis=1, keepdims=True) + jnp.sum(new, axis=1, keepdims=True)
            inverse = 1.0 / total
            result = jnp.dot(
                (old * inverse).astype(jnp.bfloat16),
                cache[0, 1, :, window],
                preferred_element_type=jnp.float32,
            ) + jnp.dot(
                (new * inverse).astype(jnp.bfloat16),
                qkv[2, :seen, window],
                preferred_element_type=jnp.float32,
            )
            result = jnp.where(mine, result, 0.0)
            for tile in range(low // 128, high // 128):
                piece = result[:, tile * 128 - low : (tile + 1) * 128 - low]
                gathered[tile] = piece if gathered[tile] is None else gathered[tile] + piece
        for tile, piece in enumerate(gathered):
            store(rows, slice(tile * 128, (tile + 1) * 128), piece.astype(jnp.bfloat16))


def attend_kernel(span, cached, block, limits, qkv, cache, att):
    def store(rows, columns, value):
        att[rows, columns] = value

    attend_group(
        span, cached, block, limits[0], limits[1], qkv, cache, store, lambda slot: None
    )


def attend(limits, qkv, cache):
    _, span, cols = qkv.shape
    groups = cols // GROUP
    cached = cache.shape[2]
    block = min(256, span)
    return pl.pallas_call(
        functools.partial(attend_kernel, span, cached, block),
        out_shape=jax.ShapeDtypeStruct((span, cols), jnp.bfloat16),
        grid=(groups,),
        in_specs=[
            pl.BlockSpec(memory_space=pltpu.SMEM),
            pl.BlockSpec((3, span, GROUP), lambda i: (0, 0, i)),
            pl.BlockSpec((1, 2, cached, GROUP), lambda i: (0, 0, 0, i)),
        ],
        out_specs=pl.BlockSpec((span, GROUP), lambda i: (0, i)),
        compiler_params=pltpu.CompilerParams(vmem_limit_bytes=48 << 20),
        name="attend",
    )(limits, qkv, cache)


def finish_kernel(
    span,
    cached,
    block,
    limits,
    qkv,
    cache,
    shard,
    mixed,
    att,
    wide,
    term,
    back,
    done,
    home,
    a_send,
    a_recv,
    z_send,
    z_recv,
    y_send,
    y_recv,
    w_own,
    m_send,
    m_recv,
    h_send,
    h_recv,
):
    step_id = pl.program_id(0)
    steps = att.shape[1]
    me = lax.axis_index("req")
    core = lax.axis_index("tp")
    z, y, x = lax.div(me, 4), lax.rem(lax.div(me, 2), 2), lax.rem(me, 2)
    to_x, to_y, mate = (me + 1 - 2 * x, core), (me + 2 - 4 * y, core), (me, 1 - core)
    half = span // 2
    slots = span // block * (GROUP // HD)

    def remote(source, target_ref, sent, received, target):
        return pltpu.make_async_remote_copy(
            src_ref=source,
            dst_ref=target_ref,
            send_sem=sent,
            recv_sem=received,
            device_id=target,
            device_id_type=pl.DeviceIdType.MESH,
        )

    def ship(side, group, part):
        ref = att.at[side, group, part * half : (part + 1) * half, :]
        return remote(ref, ref, a_send.at[group, part], a_recv.at[group, part], to_x)

    def along(plane, up, own):
        there = wide.at[plane, y]
        return remote(
            shard if own else there,
            there,
            z_send.at[plane, 0 if up else 1],
            z_recv.at[plane],
            (me + 4 if up else me - 4, core),
        )

    def across(plane, own):
        there = wide.at[plane, y]
        return remote(
            shard if own else there, there, y_send.at[plane], y_recv.at[plane], to_y
        )

    def crossed(plane):
        there = wide.at[plane, 1 - y]
        return remote(there, there, y_send.at[plane], y_recv.at[plane], to_y)

    def own_along(act):
        @pl.when(z < 3)
        def _():
            act(along(z, True, True))

        @pl.when(z > 0)
        def _():
            act(along(z, False, True))

        act(across(z, True))

    def arrivals(distance, act, arrived):
        for delta in (-distance, distance):

            def body(plane=z + delta, delta=delta):
                if arrived:
                    along(plane, True, False).wait_recv()
                if delta < 0:

                    @pl.when(z < 3)
                    def _():
                        act(along(plane, True, False))

                else:

                    @pl.when(z > 0)
                    def _():
                        act(along(plane, False, False))

                act(across(plane, False))

            pl.when(z + delta >= 0 if delta < 0 else z + delta <= 3)(body)

    keep = pltpu.make_async_copy(shard, wide.at[z, y], w_own)
    start = lambda c: c.start()
    sent = lambda c: c.wait_send()

    @pl.when(step_id == 0)
    def _():
        barrier = pltpu.get_barrier_semaphore()

        def greet(target):
            pl.semaphore_signal(
                barrier, inc=1, device_id=target, device_id_type=pl.DeviceIdType.MESH
            )

        greet(to_x)
        greet(to_y)
        greet(mate)

        @pl.when(z < 3)
        def _():
            greet((me + 4, core))

        @pl.when(z > 0)
        def _():
            greet((me - 4, core))

        inner = jnp.where(z > 0, 1, 0) + jnp.where(z < 3, 1, 0)
        pl.semaphore_wait(barrier, 3 + inner)
        own_along(start)
        keep.start()

    schedule = {(1, 3 * slots // 8): 1, (2, 5 * slots // 8): 2, (3, 6 * slots // 8): 3}

    def between(slot):
        if slot == slots // 2:
            ship(x, step_id, 0).start()
        if slot == 0:

            @pl.when(step_id > 0)
            def _():
                ship(x, step_id - 1, 1).start()

        for (step, at), distance in schedule.items():
            if at == slot:
                pl.when(step_id == step)(lambda d=distance: arrivals(d, start, True))

    def store(rows, columns, value):
        att[x, step_id, rows, columns] = value

    attend_group(
        span, cached, block, limits[0], limits[1], qkv, cache, store, between
    )

    @pl.when(step_id == steps - 1)
    def _():
        ship(x, steps - 1, 1).start()
        keep.wait()

        def product(side, plane):
            value = None
            for group in range(steps):
                part = wide[plane, :, :, group * GROUP : (group + 1) * GROUP]
                one = lax.dot_general(
                    att[side, group],
                    part.reshape(2 * part.shape[1], GROUP),
                    (((1,), (1,)), ((), ())),
                    preferred_element_type=jnp.float32,
                )
                value = one if value is None else value + one
            return value.astype(jnp.bfloat16)

        def over(side, plane):
            return remote(
                term.at[side, plane],
                back.at[side, lax.rem(plane, 2)],
                m_send.at[side, lax.rem(plane, 2)],
                m_recv.at[side, lax.rem(plane, 2)],
                mate,
            )

        def deliver(rel):
            return remote(
                done.at[rel], home.at[x, rel], h_send.at[rel], h_recv.at[rel], to_x
            )

        def total(side, plane, rel):
            over(side, plane).wait_recv()
            return (
                term[side, plane].astype(jnp.float32) + back[side, rel].astype(jnp.float32)
            ).astype(jnp.bfloat16)

        def nearest(k):
            near = jnp.where(z < 2, 1 - z, 5 - z)
            third = jnp.where(z < 2, 2, 1)
            fourth = jnp.where(z < 2, 3, 0)
            plane = jnp.where(
                k == 0, z, jnp.where(k == 1, near, jnp.where(k == 2, third, fourth))
            )
            return plane, lax.rem(plane, 2), lax.div(plane, 2) == core

        def make(side, plane, mine):
            term[side, plane] = product(side, plane)

            @pl.when(jnp.logical_not(mine))
            def _():
                over(side, plane).start()

        def send_home(plane, rel, mine):
            @pl.when(mine)
            def _():
                done[rel] = total(1 - x, plane, rel)
                deliver(rel).start()

        def own_rows(k, carry):
            plane, _, mine = nearest(k)
            crossed(plane).wait_recv()
            make(x, plane, mine)
            return carry

        def other_rows(k, carry):
            plane, rel, mine = nearest(k)
            make(1 - x, plane, mine)
            send_home(plane, rel, mine)
            return carry

        lax.fori_loop(0, 3, own_rows, 0)
        for group in range(steps):
            for part in range(2):
                ship(1 - x, group, part).wait_recv()
        lax.fori_loop(0, 3, other_rows, 0)
        plane, rel, mine = nearest(3)
        crossed(plane).wait_recv()
        make(1 - x, plane, mine)
        make(x, plane, mine)
        send_home(plane, rel, mine)
        kept = lax.broadcasted_iota(jnp.int32, (span, GROUP), 0) < limits[1]
        low_lanes = lax.broadcasted_iota(jnp.int32, (span, GROUP), 1) < GROUP // 2

        def put(i, carry):
            half_id = jnp.where(i == 0, 1 - rel, rel)
            home[x, half_id] = total(x, 2 * core + half_id, half_id)
            remote(
                done.at[half_id],
                home.at[1 - x, half_id],
                h_send.at[half_id],
                h_recv.at[half_id],
                to_x,
            ).wait_recv()
            even = home[0, half_id].astype(jnp.float32)
            odd = home[1, half_id].astype(jnp.float32)
            for side in range(2):
                if side == 0:
                    value = jnp.where(low_lanes, even, pltpu.roll(odd, GROUP // 2, 1))
                else:
                    value = jnp.where(low_lanes, pltpu.roll(even, GROUP // 2, 1), odd)
                at = pl.ds(pl.multiple_of((2 * half_id + side) * GROUP, 128), GROUP)
                mixed[:, at] = jnp.where(kept, value, 0.0).astype(jnp.bfloat16)
            return carry

        lax.fori_loop(0, 2, put, 0)
        for group in range(steps):
            for part in range(2):
                ship(x, group, part).wait_send()
        own_along(sent)
        for distance in (1, 2, 3):
            arrivals(distance, sent, False)
        for rel in range(2):
            for side in range(2):
                over(side, 2 * (1 - core) + rel).wait_send()
            deliver(rel).wait_send()


def finish(limits, qkv, cache, shard):
    _, span, cols = qkv.shape
    groups = cols // GROUP
    cached = cache.shape[2]
    block = min(256, span)
    dma = pltpu.SemaphoreType.DMA
    return pl.pallas_call(
        functools.partial(finish_kernel, span, cached, block),
        out_shape=jax.ShapeDtypeStruct((span, cols), jnp.bfloat16),
        grid=(groups,),
        in_specs=[
            pl.BlockSpec(memory_space=pltpu.SMEM),
            pl.BlockSpec((3, span, GROUP), lambda i: (0, 0, i)),
            pl.BlockSpec((1, 2, cached, GROUP), lambda i: (0, 0, 0, i)),
            pl.BlockSpec(memory_space=pl.ANY),
        ],
        out_specs=pl.BlockSpec((span, cols), lambda i: (0, 0)),
        scratch_shapes=[
            pltpu.VMEM((2, groups, span, GROUP), jnp.bfloat16),
            pltpu.VMEM((4, 2) + shard.shape, shard.dtype),
            pltpu.VMEM((2, 4, span, GROUP), jnp.bfloat16),
            pltpu.VMEM((2, 2, span, GROUP), jnp.bfloat16),
            pltpu.VMEM((2, span, GROUP), jnp.bfloat16),
            pltpu.VMEM((2, 2, span, GROUP), jnp.bfloat16),
            dma((groups, 2)),
            dma((groups, 2)),
            dma((4, 2)),
            dma((4,)),
            dma((4,)),
            dma((4,)),
            dma,
            dma((2, 2)),
            dma((2, 2)),
            dma((2,)),
            dma((2,)),
        ],
        compiler_params=pltpu.CompilerParams(
            collective_id=2, has_side_effects=True, vmem_limit_bytes=58 << 20
        ),
        name="finish",
    )(limits, qkv, cache, shard)


def project_grouped(tokens, norm_gain, qkv_weight, cache_lens):
    base_cos, base_sin, row, sign = base_tables(tokens.shape[0])
    rows = np.concatenate([row[None], sign[None], np.zeros((6, GROUP), np.float32)])
    units = ((0, 0, GROUP), (1, 0, GROUP), (2, 0, 256), (2, 256, 128))
    base = np.stack([base_cos, base_sin])
    return project(units, tokens, norm_gain, qkv_weight, base, rows, cache_lens)


def project_alone(tokens, norm_gain, qkv_weight, cache_lens):
    weights = lax.all_gather(qkv_weight, "req", axis=1, tiled=True)
    gathered = lax.all_gather(tokens, "tp", axis=1, tiled=True)
    gain_all = lax.all_gather(norm_gain, "tp", axis=0, tiled=True)
    inputs = gathered.astype(jnp.float32)
    spread = jnp.mean(inputs * inputs, axis=-1, keepdims=True)
    normed = (inputs * lax.rsqrt(spread + epsilon) * gain_all.astype(jnp.float32)).astype(
        jnp.bfloat16
    )
    span = normed.shape[0]
    cols = weights.shape[2]
    projected = jnp.einsum("td,jdc->jtc", normed, weights, preferred_element_type=jnp.float32)
    positions = cache_lens[0] + jnp.arange(span, dtype=jnp.int32)
    frequencies = jnp.power(theta_base, -jnp.arange(0, HD, 2, dtype=jnp.float32) / HD)
    angles = positions.astype(jnp.float32)[:, None] * frequencies[None, :]
    cosine, sine = jnp.cos(angles)[:, None, :], jnp.sin(angles)[:, None, :]
    heads = projected[:2].reshape(2, span, cols // HD, HD)
    a, b = heads[..., : HD // 2], heads[..., HD // 2 :]
    turned = jnp.concatenate([a * cosine - b * sine, b * cosine + a * sine], axis=-1)
    qkv = jnp.concatenate([turned.reshape(2, span, cols), projected[2:]], axis=0)
    return qkv.astype(jnp.bfloat16)


def per_device(mesh, tokens, norm_gain, qkv_weight, out_weight, cache, cache_lens, valid_tokens):
    span, width = tokens.shape
    rows, cols = qkv_weight.shape[1:]
    grouped = (
        mesh.shape["req"] == 16
        and mesh.shape["tp"] == 2
        and cols == 4 * GROUP
        and width == 8 * rows
        and rows % 16 == 0
        and width % 256 == 0
        and span % 128 == 0
        and 2 * rows == GROUP
        and out_weight.shape == (cols, rows)
    )
    limits = jnp.concatenate([cache_lens, valid_tokens])
    kept = (jnp.arange(span, dtype=jnp.int32) < valid_tokens[0])[:, None]
    if grouped:
        qkv = project_grouped(tokens, norm_gain, qkv_weight, cache_lens)
        mixed_out = finish(limits, qkv, cache, out_weight.T)
    else:
        qkv = project_alone(tokens, norm_gain, qkv_weight, cache_lens)
        out_all = lax.all_gather(out_weight.T, "req", axis=0, tiled=True)
        partial_value = lax.dot_general(
            attend(limits, qkv, cache),
            out_all,
            (((1,), (1,)), ((), ())),
            preferred_element_type=jnp.float32,
        )
        summed = lax.psum_scatter(
            partial_value.astype(jnp.bfloat16), "tp", scatter_dimension=1, tiled=True
        ).astype(jnp.float32)
        mixed_out = jnp.where(kept, summed, jnp.zeros_like(summed)).astype(jnp.bfloat16)
    new_entries = jnp.where(kept, qkv[1:], jnp.zeros_like(qkv[1:]))[None]
    return (mixed_out, new_entries)


def solution(mesh):
    placed = (
        P("req", "tp"),
        P("tp"),
        P(None, "req", "tp"),
        P("tp", "req"),
        P("req", None, None, "tp"),
        P("req"),
        P("req"),
    )
    return jax.shard_map(
        functools.partial(per_device, mesh),
        mesh=mesh,
        in_specs=placed,
        out_specs=(P("req", "tp"), P("req", None, None, "tp")),
        check_vma=False,
    )
```

```python
import functools
import math

import jax
import jax.numpy as jnp
import numpy as np
from jax import lax
from jax.experimental import pallas as pl
from jax.experimental.pallas import tpu as pltpu
from jax.sharding import PartitionSpec as P

HD = 96
GROUP = 4 * HD

epsilon = 1e-05
masked_value = -1e30
theta_base = 10000.0


def base_tables(span):
    frequencies = np.power(theta_base, -np.arange(0, HD, 2, dtype=np.float64) / HD)
    row = np.tile(frequencies.astype(np.float32), 2 * GROUP // HD)
    angles = np.arange(span, dtype=np.float64)[:, None] * row[None, :].astype(np.float64)
    sign = np.tile(np.where(np.arange(HD) < HD // 2, -1.0, 1.0), GROUP // HD).astype(np.float32)
    return (
        np.cos(angles).astype(np.float32),
        np.sin(angles).astype(np.float32),
        row,
        sign,
    )


def project_kernel(
    units,
    tok_in,
    gain,
    shard,
    base_in,
    row,
    lens,
    out,
    tok,
    base,
    near_terms,
    normed,
    weights,
    staged,
    turns,
    squares,
    z_send,
    w_recv,
    own_sem,
    s_send,
    n_send,
    n_recv,
    t_send,
    t_recv,
    q_send,
    q_recv,
    r_send,
    r_recv,
    keep_sem,
    load_sem,
):
    me = lax.axis_index("req")
    core = lax.axis_index("tp")
    z, y, x = lax.div(me, 4), lax.rem(lax.div(me, 2), 2), lax.rem(me, 2)
    p = lax.rem(me, 4)
    first_id = me - p
    px, py, pd = p + 1 - 2 * x, p + 2 - 4 * y, 3 - p
    span, width = tok.shape
    features = 2 * width
    half = span // 2
    mate = (me, 1 - core)

    barrier = pltpu.get_barrier_semaphore()

    def greet(target):
        pl.semaphore_signal(
            barrier, inc=1, device_id=target, device_id_type=pl.DeviceIdType.MESH
        )

    for peer in (px, py, pd):
        greet((first_id + peer, core))
    greet(mate)

    @pl.when(z < 3)
    def _():
        greet((me + 4, core))

    @pl.when(z > 0)
    def _():
        greet((me - 4, core))

    inner = jnp.where(z > 0, 1, 0) + jnp.where(z < 3, 1, 0)
    pl.semaphore_wait(barrier, 4 + inner)

    def remote(source, target_ref, sent, received, target):
        return pltpu.make_async_remote_copy(
            src_ref=source,
            dst_ref=target_ref,
            send_sem=sent,
            recv_sem=received,
            device_id=target,
            device_id_type=pl.DeviceIdType.MESH,
        )

    def columns(unit, peer):
        part, low, count = units[unit]
        return shard.at[part, :, pl.ds(pl.multiple_of(peer * GROUP + low, 128), count)]

    def block(unit, plane, source):
        part, low, count = units[unit]
        return weights.at[part, plane, source, :, low : low + count]

    def along(unit, plane, source, up, own):
        there = block(unit, plane, source)
        return remote(
            columns(unit, p) if own else there,
            there,
            z_send.at[unit, plane, source, 0 if up else 1],
            w_recv.at[unit, plane, source],
            (me + 4 if up else me - 4, core),
        )

    def scatter(unit, lane, peer):
        return remote(
            columns(unit, peer),
            block(unit, z, p),
            s_send.at[unit, lane],
            w_recv.at[unit, z, p],
            (first_id + peer, core),
        )

    def keep(unit):
        return pltpu.make_async_copy(columns(unit, p), block(unit, z, p), own_sem.at[unit])

    def own_along(unit, act):
        @pl.when(z < 3)
        def _():
            act(along(unit, z, p, True, True))

        @pl.when(z > 0)
        def _():
            act(along(unit, z, p, False, True))

    def scatters(unit, act):
        for lane, peer in enumerate((pd, px, py)):
            act(scatter(unit, lane, peer))

    def onward(unit, plane, source, up, down, act):
        if up:

            @pl.when(z < 3)
            def _():
                act(along(unit, plane, source, True, False))

        if down:

            @pl.when(z > 0)
            def _():
                act(along(unit, plane, source, False, False))

    def arrivals(unit, steps, act, arrived):
        for step in steps:
            if step == 0:
                for source in (px, py, pd):
                    if arrived:
                        along(unit, z, source, True, False).wait_recv()
                    onward(unit, z, source, True, True, act)
                continue
            for delta in (-step, step):

                def body(plane=z + delta, delta=delta):
                    for source in (p, px, py, pd):
                        if arrived:
                            along(unit, plane, source, True, False).wait_recv()
                        onward(unit, plane, source, delta < 0, delta > 0, act)

                pl.when(z + delta >= 0 if delta < 0 else z + delta <= 3)(body)

    def token(source, side, part, lane, target):
        ref = normed.at[source, pl.ds(2 * side, 2), part * half : (part + 1) * half, :]
        return remote(
            ref,
            ref,
            n_send.at[source, part, lane],
            n_recv.at[source, side, part],
            target,
        )

    to_x, to_y = (first_id + px, core), (first_id + py, core)

    def token_moves(source, part, via):
        moves = [(2, mate)]
        if via == "own" or (via == "y" and part == 1):
            moves.insert(0, (0, to_x))
        if via == "own" or (via == "x" and part == 0):
            moves.insert(0, (1, to_y))
        return [token(source, core, part, lane, target) for lane, target in moves]

    def tokens(source, part, via, act, arrived):
        if arrived:
            token(source, core, part, 2, mate).wait_recv()
        for copy in token_moves(source, part, via):
            act(copy)

    def turning(lane, peer):
        return remote(
            turns.at[p], turns.at[p], t_send.at[lane], t_recv.at[p], (first_id + peer, core)
        )

    def home(unit, peer):
        part, low, count = units[unit]
        return remote(
            staged.at[part, peer, :, low : low + count],
            out.at[part, :, pl.ds(pl.multiple_of(p * GROUP + low, 128), count)],
            r_send.at[unit, peer],
            r_recv.at[unit, p],
            (first_id + peer, core),
        )

    def landed(unit, source):
        part, low, count = units[unit]
        return remote(
            staged.at[part, source, :, low : low + count],
            out.at[part, :, pl.ds(pl.multiple_of(source * GROUP + low, 128), count)],
            r_send.at[unit, source],
            r_recv.at[unit, source],
            (first_id + source, core),
        )

    def stay(unit):
        part, low, count = units[unit]
        return pltpu.make_async_copy(
            staged.at[part, p, :, low : low + count],
            out.at[part, :, pl.ds(pl.multiple_of(p * GROUP + low, 128), count)],
            keep_sem.at[unit],
        )

    start = lambda c: c.start()
    sent = lambda c: c.wait_send()

    own_along(0, start)
    scatters(0, start)
    load_tok = pltpu.make_async_copy(tok_in, tok, load_sem.at[0])
    load_tok.start()
    load_base = pltpu.make_async_copy(base_in, base, load_sem.at[1])
    load_base.start()
    for unit in range(len(units)):
        keep(unit).start()
    angle = lens[0].astype(jnp.float32) * row[...]
    turned = (jnp.cos(angle[0:1]), jnp.sin(angle[0:1]))
    sign = row[1:2]
    turns[p] = jnp.concatenate(
        [
            turned[0],
            -turned[1],
            turned[1] * sign,
            turned[0] * sign,
            jnp.zeros((4, GROUP), jnp.float32),
        ]
    )
    for lane, peer in enumerate((px, py, pd)):
        turning(lane, peer).start()

    rows = 64

    def measure(i, carry):
        at = pl.ds(i * rows, rows)
        v = tok[at, :].astype(jnp.float32)
        total = jnp.sum(v * v, axis=1, keepdims=True)
        squares[core, at, :] = jnp.broadcast_to(total, (rows, 128))
        return carry

    load_tok.wait()
    lax.fori_loop(0, span // rows, measure, 0)
    share = remote(squares.at[core], squares.at[core], q_send, q_recv.at[core], mate)
    share.start()
    remote(squares.at[1 - core], squares.at[1 - core], q_send, q_recv.at[1 - core], mate).wait_recv()
    gains = gain[...].astype(jnp.float32).reshape(1, width)

    def normalize(i, carry):
        at = pl.ds(i * rows, rows)
        spread = (squares[0, at, :] + squares[1, at, :])[:, :1] * (1.0 / features)
        v = tok[at, :].astype(jnp.float32) * lax.rsqrt(spread + epsilon) * gains
        v = v.astype(jnp.bfloat16)
        normed[p, 2 * core, at, :] = v[:, : width // 2]
        normed[p, 2 * core + 1, at, :] = v[:, width // 2 :]
        return carry

    for part in range(2):
        first = part * half // rows
        lax.fori_loop(first, first + half // rows, normalize, 0)
        tokens(p, part, "own", start, False)

    def terms(unit, peer, planes):
        part, low, count = units[unit]
        value = None
        for plane in planes:
            chunk = weights[part, plane, :, :, low : low + count]
            term = jnp.dot(
                normed[peer, plane],
                chunk.reshape(chunk.shape[0] * chunk.shape[1], count),
                preferred_element_type=jnp.float32,
            )
            value = term if value is None else value + term
        return value

    def by_distance():
        near = jnp.where(z < 2, 1 - z, 5 - z)
        return [z, near, jnp.where(z < 2, 2, 1), jnp.where(z < 2, 3, 0)]

    def peer_of(i):
        return jnp.where(i == 0, pd, jnp.where(i == 1, px, jnp.where(i == 2, py, p)))

    def compute_near(unit):
        def body(i, carry):
            near_terms[i] = terms(unit, peer_of(i), by_distance()[:3])
            return carry

        lax.fori_loop(0, 4, body, 0)

    def compute_far(unit):
        part, low, count = units[unit]

        def body(i, carry):
            peer = peer_of(i)
            value = near_terms[i] + terms(unit, peer, by_distance()[3:])
            staged[part, peer, :, low : low + count] = value.astype(jnp.bfloat16)

            @pl.when(i < 3)
            def _():
                home(unit, peer).start()

            return carry

        lax.fori_loop(0, 4, body, 0)
        stay(unit).start()

    def compute(unit, begin, end):
        part, low, count = units[unit]
        lane_in_head = lax.broadcasted_iota(jnp.int32, (span, GROUP), 1) % HD

        def body(i, carry):
            peer = peer_of(i)
            value = terms(unit, peer, range(4))
            if part < 2:
                r = turns[peer]
                cosine = r[0:1] * base[0] + r[1:2] * base[1]
                sine = r[2:3] * base[0] + r[3:4] * base[1]
                ahead = pltpu.roll(value, GROUP - HD // 2, 1)
                behind = pltpu.roll(value, HD // 2, 1)
                value = value * cosine + jnp.where(lane_in_head < HD // 2, ahead, behind) * sine
            staged[part, peer, :, low : low + count] = value.astype(jnp.bfloat16)

            @pl.when(i < 3)
            def _():
                home(unit, peer).start()

            return carry

        lax.fori_loop(begin, end, body, 0)
        if end == 4:
            stay(unit).start()

    def mates(sources):
        for source in sources:
            for part in range(2):
                token(source, 1 - core, part, 2, mate).wait_recv()

    arrivals(0, (0, 1), start, True)
    scatters(1, start)
    arrivals(0, (2,), start, True)
    own_along(1, start)
    arrivals(0, (3,), start, True)
    tokens(px, 0, "x", start, True)
    tokens(py, 0, "y", start, True)
    tokens(px, 1, "x", start, True)
    tokens(py, 1, "y", start, True)
    arrivals(1, (0, 1), start, True)
    scatters(2, start)
    arrivals(1, (2,), start, True)
    own_along(2, start)
    tokens(pd, 0, "d", start, True)
    tokens(pd, 1, "d", start, True)
    for peer in (px, py, pd):
        remote(turns.at[peer], turns.at[peer], t_send.at[0], t_recv.at[peer], to_x).wait_recv()
    mates((p, px, py, pd))
    load_base.wait()
    keep(0).wait()
    compute(0, 0, 2)
    arrivals(1, (3,), start, True)
    compute(0, 2, 4)
    arrivals(2, (0, 1), start, True)
    scatters(3, start)
    keep(1).wait()
    compute(1, 0, 2)
    arrivals(2, (2,), start, True)
    own_along(3, start)
    compute(1, 2, 4)
    arrivals(2, (3,), start, True)
    arrivals(3, (0, 1), start, True)
    keep(2).wait()
    compute(2, 0, 2)
    arrivals(3, (2,), start, True)
    compute(2, 2, 4)
    keep(3).wait()
    compute_near(3)
    arrivals(3, (3,), start, True)
    compute_far(3)

    share.wait_send()
    for lane, peer in enumerate((px, py, pd)):
        turning(lane, peer).wait_send()
    for part in range(2):
        for source, via in ((p, "own"), (px, "x"), (py, "y"), (pd, "d")):
            tokens(source, part, via, sent, False)
    for unit in range(len(units)):
        own_along(unit, sent)
        scatters(unit, sent)
        arrivals(unit, (0, 1, 2, 3), sent, False)
        for peer in (pd, px, py):
            home(unit, peer).wait_send()
        stay(unit).wait()
        for peer in (pd, px, py):
            landed(unit, peer).wait_recv()


def project(units, tokens, gain, shard, base, row, lens):
    span, width = tokens.shape
    count, rows, _ = shard.shape
    n = len(units)
    dma = pltpu.SemaphoreType.DMA
    vmem = pl.BlockSpec(memory_space=pltpu.VMEM)
    hbm = pl.BlockSpec(memory_space=pl.ANY)
    smem = pl.BlockSpec(memory_space=pltpu.SMEM)
    return pl.pallas_call(
        functools.partial(project_kernel, units),
        out_shape=jax.ShapeDtypeStruct((count, span, 4 * GROUP), jnp.bfloat16),
        in_specs=[hbm, vmem, hbm, hbm, vmem, smem],
        out_specs=hbm,
        scratch_shapes=[
            pltpu.VMEM((span, width), jnp.bfloat16),
            pltpu.VMEM((2, span, GROUP), jnp.float32),
            pltpu.VMEM((4, span, units[-1][2]), jnp.float32),
            pltpu.VMEM((4, 4, span, width // 2), jnp.bfloat16),
            pltpu.VMEM((count, 4, 4, rows, GROUP), jnp.bfloat16),
            pltpu.VMEM((count, 4, span, GROUP), jnp.bfloat16),
            pltpu.VMEM((4, 8, GROUP), jnp.float32),
            pltpu.VMEM((2, span, 128), jnp.float32),
            dma((n, 4, 4, 2)),
            dma((n, 4, 4)),
            dma((n,)),
            dma((n, 3)),
            dma((4, 2, 3)),
            dma((4, 2, 2)),
            dma((3,)),
            dma((4,)),
            dma,
            dma((2,)),
            dma((n, 4)),
            dma((n, 4)),
            dma((n,)),
            dma((2,)),
        ],
        compiler_params=pltpu.CompilerParams(
            collective_id=1, has_side_effects=True, vmem_limit_bytes=56 << 20
        ),
        cost_estimate=pl.CostEstimate(
            flops=2 * 4 * span * 2 * width * count * GROUP,
            bytes_accessed=64 << 20,
            transcendentals=0,
        ),
        name="project",
    )(tokens, gain, shard, base, row, lens)


def attend_group(span, cached, block, length, valid, qkv, cache, store, between):
    scale = math.log2(math.e) / math.sqrt(HD)
    cache_bias = jnp.where(
        lax.broadcasted_iota(jnp.int32, (1, cached), 1) < length, 0.0, masked_value
    )
    dims = (((1,), (1,)), ((), ()))
    for step in range(span // block):
        rows = slice(step * block, (step + 1) * block)
        seen = (step + 1) * block
        row_ids = lax.broadcasted_iota(jnp.int32, (block, seen), 0) + step * block
        col_ids = lax.broadcasted_iota(jnp.int32, (block, seen), 1)
        live = (col_ids <= row_ids) & (col_ids < valid)
        gathered = [None] * (GROUP // 128)

        def scores(head):
            low = head * HD // 128 * 128
            high = -(-(head + 1) * HD // 128) * 128
            window = slice(low, high)
            lane = lax.broadcasted_iota(jnp.int32, (block, high - low), 1) + low
            mine = (lane >= head * HD) & (lane < (head + 1) * HD)
            query = jnp.where(mine, qkv[0, rows, window].astype(jnp.float32), 0.0).astype(
                jnp.bfloat16
            )
            old = lax.dot_general(
                query, cache[0, 0, :, window], dims, preferred_element_type=jnp.float32
            )
            new = lax.dot_general(
                query, qkv[1, :seen, window], dims, preferred_element_type=jnp.float32
            )
            return low, high, window, mine, old, new

        ahead = scores(0)
        for head in range(GROUP // HD):
            between(step * (GROUP // HD) + head)
            low, high, window, mine, old, new = ahead
            if head + 1 < GROUP // HD:
                ahead = scores(head + 1)
            old = old * scale + cache_bias
            new = jnp.where(live, new * scale, masked_value)
            top = jnp.maximum(
                jnp.max(old, axis=1, keepdims=True), jnp.max(new, axis=1, keepdims=True)
            )
            old = jnp.exp2(old - top)
            new = jnp.exp2(new - top)
            total = jnp.sum(old, axis=1, keepdims=True) + jnp.sum(new, axis=1, keepdims=True)
            inverse = 1.0 / total
            result = jnp.dot(
                (old * inverse).astype(jnp.bfloat16),
                cache[0, 1, :, window],
                preferred_element_type=jnp.float32,
            ) + jnp.dot(
                (new * inverse).astype(jnp.bfloat16),
                qkv[2, :seen, window],
                preferred_element_type=jnp.float32,
            )
            result = jnp.where(mine, result, 0.0)
            for tile in range(low // 128, high // 128):
                piece = result[:, tile * 128 - low : (tile + 1) * 128 - low]
                gathered[tile] = piece if gathered[tile] is None else gathered[tile] + piece
        for tile, piece in enumerate(gathered):
            store(rows, slice(tile * 128, (tile + 1) * 128), piece.astype(jnp.bfloat16))


def attend_kernel(span, cached, block, limits, qkv, cache, att):
    def store(rows, columns, value):
        att[rows, columns] = value

    attend_group(
        span, cached, block, limits[0], limits[1], qkv, cache, store, lambda slot: None
    )


def attend(limits, qkv, cache):
    _, span, cols = qkv.shape
    groups = cols // GROUP
    cached = cache.shape[2]
    block = min(256, span)
    return pl.pallas_call(
        functools.partial(attend_kernel, span, cached, block),
        out_shape=jax.ShapeDtypeStruct((span, cols), jnp.bfloat16),
        grid=(groups,),
        in_specs=[
            pl.BlockSpec(memory_space=pltpu.SMEM),
            pl.BlockSpec((3, span, GROUP), lambda i: (0, 0, i)),
            pl.BlockSpec((1, 2, cached, GROUP), lambda i: (0, 0, 0, i)),
        ],
        out_specs=pl.BlockSpec((span, GROUP), lambda i: (0, i)),
        compiler_params=pltpu.CompilerParams(vmem_limit_bytes=48 << 20),
        name="attend",
    )(limits, qkv, cache)


def finish_kernel(
    span,
    cached,
    block,
    limits,
    qkv,
    cache,
    shard,
    mixed,
    att,
    wide,
    term,
    back,
    done,
    home,
    a_send,
    a_recv,
    z_send,
    z_recv,
    y_send,
    y_recv,
    w_own,
    m_send,
    m_recv,
    h_send,
    h_recv,
):
    step_id = pl.program_id(0)
    steps = att.shape[1]
    me = lax.axis_index("req")
    core = lax.axis_index("tp")
    z, y, x = lax.div(me, 4), lax.rem(lax.div(me, 2), 2), lax.rem(me, 2)
    to_x, to_y, mate = (me + 1 - 2 * x, core), (me + 2 - 4 * y, core), (me, 1 - core)
    half = span // 2
    slots = span // block * (GROUP // HD)

    def remote(source, target_ref, sent, received, target):
        return pltpu.make_async_remote_copy(
            src_ref=source,
            dst_ref=target_ref,
            send_sem=sent,
            recv_sem=received,
            device_id=target,
            device_id_type=pl.DeviceIdType.MESH,
        )

    def ship(side, group, part):
        ref = att.at[side, group, part * half : (part + 1) * half, :]
        return remote(ref, ref, a_send.at[group, part], a_recv.at[group, part], to_x)

    def along(plane, up, own):
        there = wide.at[plane, y]
        return remote(
            shard if own else there,
            there,
            z_send.at[plane, 0 if up else 1],
            z_recv.at[plane],
            (me + 4 if up else me - 4, core),
        )

    def across(plane, own):
        there = wide.at[plane, y]
        return remote(
            shard if own else there, there, y_send.at[plane], y_recv.at[plane], to_y
        )

    def crossed(plane):
        there = wide.at[plane, 1 - y]
        return remote(there, there, y_send.at[plane], y_recv.at[plane], to_y)

    def own_along(act):
        @pl.when(z < 3)
        def _():
            act(along(z, True, True))

        @pl.when(z > 0)
        def _():
            act(along(z, False, True))

        act(across(z, True))

    def arrivals(distance, act, arrived):
        for delta in (-distance, distance):

            def body(plane=z + delta, delta=delta):
                if arrived:
                    along(plane, True, False).wait_recv()
                if delta < 0:

                    @pl.when(z < 3)
                    def _():
                        act(along(plane, True, False))

                else:

                    @pl.when(z > 0)
                    def _():
                        act(along(plane, False, False))

                act(across(plane, False))

            pl.when(z + delta >= 0 if delta < 0 else z + delta <= 3)(body)

    keep = pltpu.make_async_copy(shard, wide.at[z, y], w_own)
    start = lambda c: c.start()
    sent = lambda c: c.wait_send()

    @pl.when(step_id == 0)
    def _():
        barrier = pltpu.get_barrier_semaphore()

        def greet(target):
            pl.semaphore_signal(
                barrier, inc=1, device_id=target, device_id_type=pl.DeviceIdType.MESH
            )

        greet(to_x)
        greet(to_y)
        greet(mate)

        @pl.when(z < 3)
        def _():
            greet((me + 4, core))

        @pl.when(z > 0)
        def _():
            greet((me - 4, core))

        inner = jnp.where(z > 0, 1, 0) + jnp.where(z < 3, 1, 0)
        pl.semaphore_wait(barrier, 3 + inner)
        own_along(start)
        keep.start()

    schedule = {(1, 3 * slots // 8): 1, (2, 5 * slots // 8): 2}

    def between(slot):
        if slot == slots // 2:
            ship(x, step_id, 0).start()
        if slot == 0:

            @pl.when(step_id > 0)
            def _():
                ship(x, step_id - 1, 1).start()

        for (step, at), distance in schedule.items():
            if at == slot:
                pl.when(step_id == step)(lambda d=distance: arrivals(d, start, True))

    def store(rows, columns, value):
        att[x, step_id, rows, columns] = value

    attend_group(
        span, cached, block, limits[0], limits[1], qkv, cache, store, between
    )

    @pl.when(step_id == steps - 1)
    def _():
        ship(x, steps - 1, 1).start()
        arrivals(3, start, True)
        keep.wait()

        def product(side, plane):
            value = None
            for group in range(steps):
                part = wide[plane, :, :, group * GROUP : (group + 1) * GROUP]
                one = lax.dot_general(
                    att[side, group],
                    part.reshape(2 * part.shape[1], GROUP),
                    (((1,), (1,)), ((), ())),
                    preferred_element_type=jnp.float32,
                )
                value = one if value is None else value + one
            return value.astype(jnp.bfloat16)

        def over(side, plane):
            return remote(
                term.at[side, plane],
                back.at[side, lax.rem(plane, 2)],
                m_send.at[side, lax.rem(plane, 2)],
                m_recv.at[side, lax.rem(plane, 2)],
                mate,
            )

        def deliver(rel):
            return remote(
                done.at[rel], home.at[x, rel], h_send.at[rel], h_recv.at[rel], to_x
            )

        def total(side, plane, rel):
            over(side, plane).wait_recv()
            return (
                term[side, plane].astype(jnp.float32) + back[side, rel].astype(jnp.float32)
            ).astype(jnp.bfloat16)

        def nearest(k):
            near = jnp.where(z < 2, 1 - z, 5 - z)
            third = jnp.where(z < 2, 2, 1)
            fourth = jnp.where(z < 2, 3, 0)
            plane = jnp.where(
                k == 0, z, jnp.where(k == 1, near, jnp.where(k == 2, third, fourth))
            )
            return plane, lax.rem(plane, 2), lax.div(plane, 2) == core

        def make(side, plane, mine):
            term[side, plane] = product(side, plane)

            @pl.when(jnp.logical_not(mine))
            def _():
                over(side, plane).start()

        def send_home(plane, rel, mine):
            @pl.when(mine)
            def _():
                done[rel] = total(1 - x, plane, rel)
                deliver(rel).start()

        def own_rows(k, carry):
            plane, _, mine = nearest(k)
            crossed(plane).wait_recv()
            make(x, plane, mine)
            return carry

        def other_rows(k, carry):
            plane, rel, mine = nearest(k)
            make(1 - x, plane, mine)
            send_home(plane, rel, mine)
            return carry

        lax.fori_loop(0, 3, own_rows, 0)
        for group in range(steps):
            for part in range(2):
                ship(1 - x, group, part).wait_recv()
        lax.fori_loop(0, 3, other_rows, 0)
        plane, rel, mine = nearest(3)
        crossed(plane).wait_recv()
        make(1 - x, plane, mine)
        make(x, plane, mine)
        send_home(plane, rel, mine)
        kept = lax.broadcasted_iota(jnp.int32, (span, GROUP), 0) < limits[1]
        low_lanes = lax.broadcasted_iota(jnp.int32, (span, GROUP), 1) < GROUP // 2

        def put(i, carry):
            half_id = jnp.where(i == 0, 1 - rel, rel)
            home[x, half_id] = total(x, 2 * core + half_id, half_id)
            remote(
                done.at[half_id],
                home.at[1 - x, half_id],
                h_send.at[half_id],
                h_recv.at[half_id],
                to_x,
            ).wait_recv()
            even = home[0, half_id].astype(jnp.float32)
            odd = home[1, half_id].astype(jnp.float32)
            for side in range(2):
                if side == 0:
                    value = jnp.where(low_lanes, even, pltpu.roll(odd, GROUP // 2, 1))
                else:
                    value = jnp.where(low_lanes, pltpu.roll(even, GROUP // 2, 1), odd)
                at = pl.ds(pl.multiple_of((2 * half_id + side) * GROUP, 128), GROUP)
                mixed[:, at] = jnp.where(kept, value, 0.0).astype(jnp.bfloat16)
            return carry

        lax.fori_loop(0, 2, put, 0)
        for group in range(steps):
            for part in range(2):
                ship(x, group, part).wait_send()
        own_along(sent)
        for distance in (1, 2, 3):
            arrivals(distance, sent, False)
        for rel in range(2):
            for side in range(2):
                over(side, 2 * (1 - core) + rel).wait_send()
            deliver(rel).wait_send()


def finish(limits, qkv, cache, shard):
    _, span, cols = qkv.shape
    groups = cols // GROUP
    cached = cache.shape[2]
    block = min(256, span)
    dma = pltpu.SemaphoreType.DMA
    return pl.pallas_call(
        functools.partial(finish_kernel, span, cached, block),
        out_shape=jax.ShapeDtypeStruct((span, cols), jnp.bfloat16),
        grid=(groups,),
        in_specs=[
            pl.BlockSpec(memory_space=pltpu.SMEM),
            pl.BlockSpec((3, span, GROUP), lambda i: (0, 0, i)),
            pl.BlockSpec((1, 2, cached, GROUP), lambda i: (0, 0, 0, i)),
            pl.BlockSpec(memory_space=pl.ANY),
        ],
        out_specs=pl.BlockSpec((span, cols), lambda i: (0, 0)),
        scratch_shapes=[
            pltpu.VMEM((2, groups, span, GROUP), jnp.bfloat16),
            pltpu.VMEM((4, 2) + shard.shape, shard.dtype),
            pltpu.VMEM((2, 4, span, GROUP), jnp.bfloat16),
            pltpu.VMEM((2, 2, span, GROUP), jnp.bfloat16),
            pltpu.VMEM((2, span, GROUP), jnp.bfloat16),
            pltpu.VMEM((2, 2, span, GROUP), jnp.bfloat16),
            dma((groups, 2)),
            dma((groups, 2)),
            dma((4, 2)),
            dma((4,)),
            dma((4,)),
            dma((4,)),
            dma,
            dma((2, 2)),
            dma((2, 2)),
            dma((2,)),
            dma((2,)),
        ],
        compiler_params=pltpu.CompilerParams(
            collective_id=2, has_side_effects=True, vmem_limit_bytes=58 << 20
        ),
        name="finish",
    )(limits, qkv, cache, shard)


def project_grouped(tokens, norm_gain, qkv_weight, cache_lens):
    base_cos, base_sin, row, sign = base_tables(tokens.shape[0])
    rows = np.concatenate([row[None], sign[None], np.zeros((6, GROUP), np.float32)])
    units = ((0, 0, GROUP), (1, 0, GROUP), (2, 0, 256), (2, 256, 128))
    base = np.stack([base_cos, base_sin])
    return project(units, tokens, norm_gain, qkv_weight, base, rows, cache_lens)


def project_alone(tokens, norm_gain, qkv_weight, cache_lens):
    weights = lax.all_gather(qkv_weight, "req", axis=1, tiled=True)
    gathered = lax.all_gather(tokens, "tp", axis=1, tiled=True)
    gain_all = lax.all_gather(norm_gain, "tp", axis=0, tiled=True)
    inputs = gathered.astype(jnp.float32)
    spread = jnp.mean(inputs * inputs, axis=-1, keepdims=True)
    normed = (inputs * lax.rsqrt(spread + epsilon) * gain_all.astype(jnp.float32)).astype(
        jnp.bfloat16
    )
    span = normed.shape[0]
    cols = weights.shape[2]
    projected = jnp.einsum("td,jdc->jtc", normed, weights, preferred_element_type=jnp.float32)
    positions = cache_lens[0] + jnp.arange(span, dtype=jnp.int32)
    frequencies = jnp.power(theta_base, -jnp.arange(0, HD, 2, dtype=jnp.float32) / HD)
    angles = positions.astype(jnp.float32)[:, None] * frequencies[None, :]
    cosine, sine = jnp.cos(angles)[:, None, :], jnp.sin(angles)[:, None, :]
    heads = projected[:2].reshape(2, span, cols // HD, HD)
    a, b = heads[..., : HD // 2], heads[..., HD // 2 :]
    turned = jnp.concatenate([a * cosine - b * sine, b * cosine + a * sine], axis=-1)
    qkv = jnp.concatenate([turned.reshape(2, span, cols), projected[2:]], axis=0)
    return qkv.astype(jnp.bfloat16)


def per_device(mesh, tokens, norm_gain, qkv_weight, out_weight, cache, cache_lens, valid_tokens):
    span, width = tokens.shape
    rows, cols = qkv_weight.shape[1:]
    grouped = (
        mesh.shape["req"] == 16
        and mesh.shape["tp"] == 2
        and cols == 4 * GROUP
        and width == 8 * rows
        and rows % 16 == 0
        and width % 256 == 0
        and span % 128 == 0
        and 2 * rows == GROUP
        and out_weight.shape == (cols, rows)
    )
    limits = jnp.concatenate([cache_lens, valid_tokens])
    kept = (jnp.arange(span, dtype=jnp.int32) < valid_tokens[0])[:, None]
    if grouped:
        qkv = project_grouped(tokens, norm_gain, qkv_weight, cache_lens)
        mixed_out = finish(limits, qkv, cache, out_weight.T)
    else:
        qkv = project_alone(tokens, norm_gain, qkv_weight, cache_lens)
        out_all = lax.all_gather(out_weight.T, "req", axis=0, tiled=True)
        partial_value = lax.dot_general(
            attend(limits, qkv, cache),
            out_all,
            (((1,), (1,)), ((), ())),
            preferred_element_type=jnp.float32,
        )
        summed = lax.psum_scatter(
            partial_value.astype(jnp.bfloat16), "tp", scatter_dimension=1, tiled=True
        ).astype(jnp.float32)
        mixed_out = jnp.where(kept, summed, jnp.zeros_like(summed)).astype(jnp.bfloat16)
    new_entries = jnp.where(kept, qkv[1:], jnp.zeros_like(qkv[1:]))[None]
    return (mixed_out, new_entries)


def solution(mesh):
    placed = (
        P("req", "tp"),
        P("tp"),
        P(None, "req", "tp"),
        P("tp", "req"),
        P("req", None, None, "tp"),
        P("req"),
        P("req"),
    )
    return jax.shard_map(
        functools.partial(per_device, mesh),
        mesh=mesh,
        in_specs=placed,
        out_specs=(P("req", "tp"), P("req", None, None, "tp")),
        check_vma=False,
    )
```
